128 devices in a mesh: seq: 32 (over y, x, core), head: 4 (over z).
Axes of the slice: x: 4, y: 4, z: 4, core: 2. Of those that a mesh axis runs over, the one named last changes fastest.
Arguments:
- queries: bfloat16 [32768, 2048], P(('seq', 'head')), may hold values from -6 to 6
- keys_in: bfloat16 [32768, 2048], P(('seq', 'head')), may hold values from -6 to 6
- values_in: bfloat16 [32768, 2048], P(('seq', 'head')), may hold values from -6 to 6
- cotangent: bfloat16 [32768, 2048], P(('seq', 'head')), may hold values from -6 to 6
Outputs:
- attended: bfloat16 [32768, 2048], P(('seq', 'head'))
- grad_queries: bfloat16 [32768, 2048], P(('seq', 'head'))
- grad_keys: bfloat16 [32768, 2048], P(('seq', 'head'))
- grad_values: bfloat16 [32768, 2048], P(('seq', 'head'))
The draws below stay inside these ranges and needn't reach their ends.
All inputs are finite; a program needn't handle non-finite values.
Results may differ from the reference program's by a relative error of at most 0.029.
Values may be sent and summed in bfloat16 or wider, within the bound.
A program may use at most 128 MiB of HBM per device.

```python
import math
import jax
import jax.numpy as jnp
from jax import lax

HEADS = 16
HEAD_DIM = 128
WIDTH = 2048
BLOCK = 128
SUMMARY = 8
SEQ_LEN = 32768
NKEYS = 2048


def base_field(key):
    return jnp.clip(jax.random.normal(key, (SEQ_LEN, HEADS, HEAD_DIM), jnp.float32), -6.0, 6.0)


def draw_queries(key, part):
    field = base_field(jax.random.fold_in(key, 11))
    return field.reshape(SEQ_LEN, WIDTH).astype(jnp.bfloat16)


def draw_keys_in(key, part):
    field = base_field(jax.random.fold_in(key, 12))
    return field.reshape(SEQ_LEN, WIDTH).astype(jnp.bfloat16)


def block_levels(rng, dims, cuts, least, largest):
    level = 1.0
    for dim, parts in cuts:
        steps = jax.random.uniform(jax.random.fold_in(jax.random.fold_in(rng, 6), dim), (parts,), jnp.float32, least / len(cuts), largest / len(cuts))
        level = level * jnp.repeat(jnp.exp(steps), dims[dim] // parts).reshape((-1,) + (1,) * (len(dims) - 1 - dim))
    return level


def normal_values(stream_key, shape, deviation, reach, cuts=(), kind=jnp.bfloat16):
    result = jax.random.normal(stream_key, shape, jnp.float32) * deviation
    if len(cuts) > 0:
        result = block_levels(stream_key, shape, cuts, -0.22, 0.18) * result
    return jnp.clip(result, min=-reach, max=reach).astype(kind)


def setup_inputs(seed: int = 0) -> dict:
    splits = jax.random.split(jax.random.key(seed), 5)
    queries = draw_queries(jax.random.fold_in(splits[4], 71), 0)
    keys_in = draw_keys_in(jax.random.fold_in(splits[4], 71), 0)
    values_in = normal_values(splits[2], (SEQ_LEN, WIDTH), 1.0, 6.0, ((0, 128),))
    cotangent = normal_values(splits[3], (SEQ_LEN, WIDTH), 1.0, 6.0, ((0, 128),))
    return dict(queries=queries, keys_in=keys_in, values_in=values_in, cotangent=cotangent)


neg_fill = -1e+30

def rounded(matrix):
    return lax.optimization_barrier(matrix.astype(jnp.bfloat16)).astype(jnp.float32)

def reference(queries, keys_in, values_in, cotangent):
    scaling = 1.0 / math.sqrt(HEAD_DIM)
    nblocks = SEQ_LEN // BLOCK
    block_shape = (nblocks, BLOCK, HEADS, HEAD_DIM)
    query_blocks = queries.reshape(block_shape)
    key_blocks = keys_in.reshape(block_shape)
    value_blocks = values_in.reshape(block_shape)
    grad_blocks = cotangent.reshape(block_shape)
    key_rows = key_blocks[:, BLOCK - SUMMARY:].reshape(NKEYS, HEADS, HEAD_DIM).astype(jnp.float32)
    value_rows = value_blocks[:, BLOCK - SUMMARY:].reshape(NKEYS, HEADS, HEAD_DIM).astype(jnp.float32)
    key_block = jnp.arange(NKEYS, dtype=jnp.int32) // SUMMARY
    causal = jnp.arange(BLOCK, dtype=jnp.int32)[:, None] >= jnp.arange(BLOCK, dtype=jnp.int32)[None, :]

    def block_turn(carried, block_data):
        key_sum, value_sum = carried
        query_b, key_b, value_b, grad_b, block_index = block_data
        query_f = query_b.astype(jnp.float32)
        key_f = key_b.astype(jnp.float32)
        value_f = value_b.astype(jnp.float32)
        grad_f = grad_b.astype(jnp.float32)
        seen = (key_block < block_index)[None, None, :]
        local_scores = jnp.einsum('ihe,jhe->hij', query_f, key_f) * scaling
        summary_scores = jnp.einsum('ihe,jhe->hij', query_f, key_rows) * scaling
        highest = jnp.maximum(lax.optimization_barrier(jnp.max(jnp.where(causal, local_scores, neg_fill), axis=-1)), lax.optimization_barrier(jnp.max(jnp.where(seen, summary_scores, neg_fill), axis=-1)))
        norm_sum = lax.optimization_barrier(jnp.sum(jnp.where(causal, jnp.exp(local_scores - highest[..., None]), 0.0), axis=-1))
        norm_sum = norm_sum + lax.optimization_barrier(jnp.sum(jnp.where(seen, jnp.exp(summary_scores - highest[..., None]), 0.0), axis=-1))
        log_norm = highest + jnp.log(norm_sum)
        local_probs = jnp.where(causal, jnp.exp(local_scores - log_norm[..., None]), 0.0)
        summary_probs = jnp.where(seen, jnp.exp(summary_scores - log_norm[..., None]), 0.0)
        local_pb = rounded(local_probs)
        summary_pb = rounded(summary_probs)
        output = jnp.einsum('hij,jhe->ihe', local_pb, value_f) + jnp.einsum('hij,jhe->ihe', summary_pb, value_rows)
        output = rounded(output)
        delta = lax.optimization_barrier(jnp.sum(grad_f * output, axis=-1)).T
        local_ds = rounded(local_probs * (jnp.einsum('ihe,jhe->hij', grad_f, value_f) - delta[..., None]))
        summary_ds = rounded(summary_probs * (jnp.einsum('ihe,jhe->hij', grad_f, value_rows) - delta[..., None]))
        grad_query = (jnp.einsum('hij,jhe->ihe', local_ds, key_f) + jnp.einsum('hij,jhe->ihe', summary_ds, key_rows)) * scaling
        grad_key = jnp.einsum('hij,ihe->jhe', local_ds, query_f) * scaling
        grad_value = jnp.einsum('hij,ihe->jhe', local_pb, grad_f)
        key_sum = key_sum + jnp.einsum('hij,ihe->jhe', summary_ds, query_f) * scaling
        value_sum = value_sum + jnp.einsum('hij,ihe->jhe', summary_pb, grad_f)
        return ((key_sum, value_sum), (output, grad_query, grad_key, grad_value))
    start_sums = (jnp.zeros((NKEYS, HEADS, HEAD_DIM), jnp.float32), jnp.zeros((NKEYS, HEADS, HEAD_DIM), jnp.float32))
    block_ids = jnp.arange(nblocks, dtype=jnp.int32)
    (key_sum, value_sum), results = lax.scan(block_turn, start_sums, (query_blocks, key_blocks, value_blocks, grad_blocks, block_ids))
    output, grad_query, grad_key, grad_value = results
    key_extra = key_sum.reshape(nblocks, SUMMARY, HEADS, HEAD_DIM)
    value_extra = value_sum.reshape(nblocks, SUMMARY, HEADS, HEAD_DIM)
    grad_key = jnp.concatenate([grad_key[:, :BLOCK - SUMMARY], grad_key[:, BLOCK - SUMMARY:] + key_extra], axis=1)
    grad_value = jnp.concatenate([grad_value[:, :BLOCK - SUMMARY], grad_value[:, BLOCK - SUMMARY:] + value_extra], axis=1)
    attended = output.reshape(SEQ_LEN, WIDTH).astype(jnp.bfloat16)
    grad_queries = grad_query.reshape(SEQ_LEN, WIDTH).astype(jnp.bfloat16)
    grad_keys = grad_key.reshape(SEQ_LEN, WIDTH).astype(jnp.bfloat16)
    grad_values = grad_value.reshape(SEQ_LEN, WIDTH).astype(jnp.bfloat16)
    return (attended, grad_queries, grad_keys, grad_values)
```

```python
import math

import jax
import jax.numpy as jnp
from jax import lax
from jax.experimental import pallas as pl
from jax.experimental.pallas import tpu as pltpu
from jax.sharding import PartitionSpec as P

HEADS = 16
HEAD_DIM = 128
BLOCK = 128
SUMMARY = 8
WIDTH = 2048
ROWS = 256
PAIR = 256
NY, NX, NC, NZ = 4, 4, 2, 4
TILE = 512

MESH = pl.DeviceIdType.MESH
NEG = -1e30
LOG2E = 1.4426950408889634
SCALE = 1.0 / math.sqrt(HEAD_DIM)
C2 = SCALE * LOG2E
BF = jnp.bfloat16
F32 = jnp.float32

NT = (((1,), (1,)), ((), ()))
TN = (((0,), (0,)), ((), ()))
NN = (((1,), (0,)), ((), ()))


def dot(a, b, dims):
    return lax.dot_general(a, b, dims, preferred_element_type=F32)


def cols_of(pair):
    return pl.ds(pl.multiple_of(pair * PAIR, PAIR), PAIR)


def exchange_kernel(
    q_hbm, k_hbm, v_hbm, g_hbm,
    o_out, dq_out, st_out, dkv_out,
    q_v, k_v, v_v, g_v,
    kv_pack, kv_col, q_all, g_all, kv_all,
    k_h, v_h, kt_h, vt_h,
    q_t, g_t, score, acc_t, grad_kv,
    rs_send, rs_recv, o_buf, dq_buf, st_send, st_all, st_back, dkv_sum,
    load_sem, own_sem,
    kv_ss, kv_rs, q_ss, q_rs, g_ss, g_rs, st_ss, st_rs,
    ag_ss, ag_rs, o_ss, o_rs, dq_ss, dq_rs, sb_ss, sb_rs,
    rs_ss, rs_rs, dkv_ss, dkv_rs,
):
    s = lax.axis_index("seq")
    z0 = lax.axis_index("head")
    y0 = lax.div(s, 8)
    x0 = lax.rem(lax.div(s, 2), 4)
    c0 = lax.rem(s, 2)
    j0 = y0 * 2 + c0
    p0 = x0 * 4 + z0

    def member_id(pair):
        return (lax.div(pair, 2) * 8 + x0 * 2 + lax.rem(pair, 2), z0)

    def plane_id(place):
        return (y0 * 8 + lax.div(place, 4) * 2 + c0, lax.rem(place, 4))

    def group_peer(step):
        yt = lax.rem(y0 + step // 2, 4)
        ct = lax.rem(c0 + step % 2, 2)
        return yt * 2 + ct

    group_steps = (1, 2, 3, 6, 7, 4, 5)

    loads = [
        pltpu.make_async_copy(src, dst, load_sem.at[i])
        for i, (src, dst) in enumerate(((k_hbm, k_v), (v_hbm, v_v), (q_hbm, q_v), (g_hbm, g_v)))
    ]
    for load in loads:
        load.start()
    own_q = pltpu.make_async_copy(q_hbm.at[:, cols_of(j0)], q_all.at[j0], own_sem.at[0])
    own_g = pltpu.make_async_copy(g_hbm.at[:, cols_of(j0)], g_all.at[j0], own_sem.at[1])
    own_q.start()
    own_g.start()

    barrier = pltpu.get_barrier_semaphore()
    for step in range(1, 8):
        pl.semaphore_signal(
            barrier, inc=1, device_id=member_id(group_peer(step)), device_id_type=MESH
        )

    def greet(i, carry):
        pl.semaphore_signal(
            barrier, inc=1, device_id=plane_id(lax.rem(p0 + i, 16)), device_id_type=MESH
        )
        return carry

    lax.fori_loop(1, 16, greet, 0)

    loads[0].wait()
    loads[1].wait()
    for i, src in enumerate((k_v, v_v)):
        for j in range(8):
            top = src[112:128, j * PAIR : (j + 1) * PAIR].astype(F32)[8:, :]
            low = src[240:256, j * PAIR : (j + 1) * PAIR].astype(F32)[8:, :]
            kv_pack[j, i] = jnp.concatenate([top, low], axis=0).astype(BF)
    own_kv = pltpu.make_async_copy(kv_pack.at[j0], kv_col.at[j0], own_sem.at[2])
    own_kv.start()
    pl.semaphore_wait(barrier, 22)

    def to_member(src, dst, ssem, rsem, pair, slot):
        return pltpu.make_async_remote_copy(
            src_ref=src,
            dst_ref=dst,
            send_sem=ssem.at[pair],
            recv_sem=rsem.at[slot],
            device_id=member_id(pair),
            device_id_type=MESH,
        )

    def kv_copy(pair, slot):
        return to_member(kv_pack.at[pair], kv_col.at[slot], kv_ss, kv_rs, pair, slot)

    def q_copy(pair, slot):
        return to_member(q_hbm.at[:, cols_of(pair)], q_all.at[slot], q_ss, q_rs, pair, slot)

    def g_copy(pair, slot):
        return to_member(g_hbm.at[:, cols_of(pair)], g_all.at[slot], g_ss, g_rs, pair, slot)

    def st_copy(pair, slot):
        return to_member(st_send.at[pair], st_all.at[slot], st_ss, st_rs, pair, slot)

    def o_copy(pair, slot):
        return to_member(o_buf.at[pair], o_out.at[:, cols_of(slot)], o_ss, o_rs, pair, slot)

    def dq_copy(pair, slot):
        return to_member(dq_buf.at[pair], dq_out.at[:, cols_of(slot)], dq_ss, dq_rs, pair, slot)

    def sb_copy(pair, slot):
        return to_member(st_back.at[pair], st_out.at[slot], sb_ss, sb_rs, pair, slot)

    def dkv_copy(pair, slot):
        return to_member(dkv_sum.at[pair], dkv_out.at[slot], dkv_ss, dkv_rs, pair, slot)

    def ag_copy(place, slot):
        return pltpu.make_async_remote_copy(
            src_ref=kv_col,
            dst_ref=kv_all.at[slot],
            send_sem=ag_ss.at[place],
            recv_sem=ag_rs.at[slot],
            device_id=plane_id(place),
            device_id_type=MESH,
        )

    def rs_copy(y, place, slot):
        return pltpu.make_async_remote_copy(
            src_ref=rs_send.at[y, place],
            dst_ref=rs_recv.at[y, slot],
            send_sem=rs_ss.at[y, place],
            recv_sem=rs_rs.at[y, slot],
            device_id=plane_id(place),
            device_id_type=MESH,
        )

    for step in group_steps:
        kv_copy(group_peer(step), j0).start()
    for step in group_steps:
        q_copy(group_peer(step), j0).start()
        g_copy(group_peer(step), j0).start()

    own_kv.wait()
    for step in group_steps:
        kv_copy(group_peer(step), group_peer(step)).wait_recv()

    def ag_start(i, carry):
        ag_copy(lax.rem(p0 + i, 16), p0).start()
        return carry

    lax.fori_loop(1, 16, ag_start, 0)
    own_ag = pltpu.make_async_copy(kv_col, kv_all.at[p0], own_sem.at[3])
    own_ag.start()

    loads[2].wait()
    loads[3].wait()
    key_pos = lax.broadcasted_iota(jnp.int32, (BLOCK, BLOCK), 0)
    query_pos = lax.broadcasted_iota(jnp.int32, (BLOCK, BLOCK), 1)
    causal = key_pos <= query_pos

    def local_turn(j, carry):
        for hh in range(2):
            cols = pl.ds(pl.multiple_of(j * PAIR + hh * HEAD_DIM, HEAD_DIM), HEAD_DIM)
            for r in range(2):
                rows = slice(r * BLOCK, (r + 1) * BLOCK)
                raw = dot(k_v[rows, cols], q_v[rows, cols], NT)
                raw = jnp.where(causal, raw, NEG)
                high = jnp.max(raw, axis=0, keepdims=True)
                weights = jnp.exp2((raw - high) * C2)
                dprob = dot(v_v[rows, cols], g_v[rows, cols], NT)
                st_send[j, 3 * hh : 3 * hh + 1, rows] = high
                st_send[j, 3 * hh + 1 : 3 * hh + 2, rows] = jnp.sum(weights, axis=0, keepdims=True)
                st_send[j, 3 * hh + 2 : 3 * hh + 3, rows] = jnp.sum(
                    weights * dprob, axis=0, keepdims=True
                )
        return carry

    st_send[...] = jnp.zeros_like(st_send)
    lax.fori_loop(0, 8, local_turn, 0)
    own_st = pltpu.make_async_copy(st_send.at[j0], st_all.at[j0], own_sem.at[4])
    own_st.start()
    for step in group_steps:
        st_copy(group_peer(step), j0).start()

    grad_kv[...] = jnp.zeros_like(grad_kv)
    st_back[...] = jnp.zeros_like(st_back)

    own_ag.wait()

    def ag_wait(i, carry):
        ag_copy(lax.rem(p0 + i, 16), lax.rem(p0 + i, 16)).wait_recv()
        return carry

    lax.fori_loop(1, 16, ag_wait, 0)

    def arrange(y, carry):
        for x in range(4):
            for c in range(2):
                for z in range(4):
                    row = pl.multiple_of(y * TILE + x * 128 + c * 64 + z * 16, 16)
                    for hh in range(2):
                        cols = slice(hh * HEAD_DIM, (hh + 1) * HEAD_DIM)
                        k_h[hh, pl.ds(row, 16), :] = kv_all[x * 4 + z, y * 2 + c, 0, :, cols]
                        v_h[hh, pl.ds(row, 16), :] = kv_all[x * 4 + z, y * 2 + c, 1, :, cols]
        tile = pl.ds(pl.multiple_of(y * TILE, TILE), TILE)
        for hh in range(2):
            kt_h[hh, y] = k_h[hh, tile, :].T
            vt_h[hh, y] = v_h[hh, tile, :].T
        return carry

    lax.fori_loop(0, 4, arrange, 0)

    own_q.wait()
    own_g.wait()
    own_st.wait()
    for step in group_steps:
        pair = group_peer(step)
        q_copy(pair, pair).wait_recv()
        g_copy(pair, pair).wait_recv()
        st_copy(pair, pair).wait_recv()

    lane = lax.broadcasted_iota(jnp.int32, (1, 2 * ROWS), 1)
    lane_limit = x0 * 128 + z0 * 16 + lax.div(lane, 256) * 64 + lax.rem(lax.div(lane, 128), 2) * 8
    key_row = lax.broadcasted_iota(jnp.int32, (TILE, 2 * ROWS), 0)

    for y in (3, 2, 1, 0):
        limit = lane_limit + y * TILE

        def head_turn(hh, carry, y=y, limit=limit):
            cols = pl.ds(pl.multiple_of(hh * HEAD_DIM, HEAD_DIM), HEAD_DIM)
            q_rows = q_all[2 * y : 2 * y + 2, :, cols].reshape(2 * ROWS, HEAD_DIM)
            g_rows = g_all[2 * y : 2 * y + 2, :, cols].reshape(2 * ROWS, HEAD_DIM)
            q_t[...] = q_rows.T
            g_t[...] = g_rows.T

            def stat(kind):
                row = pl.ds(hh * 3 + kind, 1)
                return jnp.concatenate(
                    [st_all[2 * y, row, :], st_all[2 * y + 1, row, :]], axis=1
                )

            local_high = stat(0)
            local_sum = stat(1)
            local_delta = stat(2)

            def score_turn(kt, high):
                raw = dot(k_h[hh, pl.ds(pl.multiple_of(kt * TILE, TILE), TILE), :], q_t[...], NN)
                raw = jnp.where(key_row + kt * TILE < limit, raw, NEG)
                score[kt] = raw
                return jnp.maximum(high, jnp.max(raw, axis=0, keepdims=True))

            high = lax.fori_loop(0, y + 1, score_turn, local_high)
            acc_t[...] = jnp.zeros_like(acc_t)

            def value_turn(kt, total):
                weights = jnp.exp2((score[kt] - high) * C2)
                score[kt] = weights
                acc_t[...] += dot(vt_h[hh, kt], weights.astype(BF), NN)
                return total + jnp.sum(weights, axis=0, keepdims=True)

            shrink = jnp.exp2((local_high - high) * C2)
            total = lax.fori_loop(0, y + 1, value_turn, local_sum * shrink)
            inverse = 1.0 / total
            out_t = acc_t[...]
            delta = (
                local_delta * shrink
                + jnp.sum(out_t * g_t[...].astype(F32), axis=0, keepdims=True)
            ) * inverse
            lse = high * C2 + jnp.log(total) * LOG2E
            out = (out_t * inverse).T.astype(BF)
            for c in range(2):
                half = slice(c * ROWS, (c + 1) * ROWS)
                o_buf[2 * y + c, :, cols] = out[half]
                st_back[2 * y + c, pl.ds(hh, 1), :] = lse[:, half]
                st_back[2 * y + c, pl.ds(hh + 2, 1), :] = delta[:, half]
            acc_t[...] = jnp.zeros_like(acc_t)

            def grad_turn(kt, carry):
                tile = pl.ds(pl.multiple_of(kt * TILE, TILE), TILE)
                probs = score[kt] * inverse
                dprob = dot(v_h[hh, tile, :], g_t[...], NN)
                dscore = (probs * (dprob - delta)).astype(BF)
                acc_t[...] += dot(kt_h[hh, kt], dscore, NN)
                grad_kv[0, hh, tile, :] += dot(dscore, q_rows, NN)
                grad_kv[1, hh, tile, :] += dot(probs.astype(BF), g_rows, NN)
                return carry

            lax.fori_loop(0, y + 1, grad_turn, 0)
            grad_q = (acc_t[...] * SCALE).T.astype(BF)
            for c in range(2):
                dq_buf[2 * y + c, :, cols] = grad_q[c * ROWS : (c + 1) * ROWS]
            return carry

        lax.fori_loop(0, 2, head_turn, 0)

        for c in range(2):
            pair = 2 * y + c

            @pl.when(pair != j0)
            def _(pair=pair):
                o_copy(pair, j0).start()
                dq_copy(pair, j0).start()
                sb_copy(pair, j0).start()

        def pack_turn(x, carry, y=y):
            for zz in range(4):
                for c in range(2):
                    row = pl.multiple_of(y * TILE + x * 128 + c * 64 + zz * 16, 16)
                    for hh in range(2):
                        cols = slice(hh * HEAD_DIM, (hh + 1) * HEAD_DIM)
                        rs_send[y, x * 4 + zz, c, 0, :, cols] = (
                            grad_kv[0, hh, pl.ds(row, 16), :] * SCALE
                        ).astype(BF)
                        rs_send[y, x * 4 + zz, c, 1, :, cols] = grad_kv[
                            1, hh, pl.ds(row, 16), :
                        ].astype(BF)
            return carry

        lax.fori_loop(0, 4, pack_turn, 0)

        def rs_start(i, carry, y=y):
            rs_copy(y, lax.rem(p0 + i, 16), p0).start()
            return carry

        lax.fori_loop(1, 16, rs_start, 0)

    own_o = pltpu.make_async_copy(o_buf.at[j0], o_out.at[:, cols_of(j0)], own_sem.at[0])
    own_dq = pltpu.make_async_copy(dq_buf.at[j0], dq_out.at[:, cols_of(j0)], own_sem.at[1])
    own_sb = pltpu.make_async_copy(st_back.at[j0], st_out.at[j0], own_sem.at[2])
    own_o.start()
    own_dq.start()
    own_sb.start()

    for y in (3, 2, 1, 0):

        def rs_wait(i, carry, y=y):
            place = lax.rem(p0 + i, 16)
            rs_copy(y, place, place).wait_recv()
            return carry

        lax.fori_loop(1, 16, rs_wait, 0)
        for c in range(2):

            def add_turn(i, total, y=y, c=c):
                return total + rs_recv[y, lax.rem(p0 + i, 16), c].astype(F32)

            dkv_sum[2 * y + c] = lax.fori_loop(1, 16, add_turn, rs_send[y, p0, c].astype(F32))
            pair = 2 * y + c

            @pl.when(pair != j0)
            def _(pair=pair):
                dkv_copy(pair, j0).start()

    own_dkv = pltpu.make_async_copy(dkv_sum.at[j0], dkv_out.at[j0], own_sem.at[3])
    own_dkv.start()

    own_o.wait()
    own_dq.wait()
    own_sb.wait()
    own_dkv.wait()
    for step in group_steps:
        pair = group_peer(step)
        for copy in (o_copy, dq_copy, sb_copy, dkv_copy):
            copy(pair, pair).wait_recv()
        for copy in (kv_copy, q_copy, g_copy, st_copy, o_copy, dq_copy, sb_copy, dkv_copy):
            copy(pair, j0).wait_send()

    def drain(i, carry):
        place = lax.rem(p0 + i, 16)
        ag_copy(place, p0).wait_send()
        for y in range(4):
            rs_copy(y, place, p0).wait_send()
        return carry

    lax.fori_loop(1, 16, drain, 0)


def exchange(queries, keys_in, values_in, cotangent):
    any_spec = pl.BlockSpec(memory_space=pl.ANY)
    dma = pltpu.SemaphoreType.DMA
    return pl.pallas_call(
        exchange_kernel,
        out_shape=(
            jax.ShapeDtypeStruct((ROWS, WIDTH), BF),
            jax.ShapeDtypeStruct((ROWS, WIDTH), BF),
            jax.ShapeDtypeStruct((8, 8, ROWS), F32),
            jax.ShapeDtypeStruct((8, 2, 16, PAIR), F32),
        ),
        in_specs=[any_spec] * 4,
        out_specs=(any_spec,) * 4,
        scratch_shapes=[
            pltpu.VMEM((ROWS, WIDTH), BF),
            pltpu.VMEM((ROWS, WIDTH), BF),
            pltpu.VMEM((ROWS, WIDTH), BF),
            pltpu.VMEM((ROWS, WIDTH), BF),
            pltpu.VMEM((8, 2, 16, PAIR), BF),
            pltpu.VMEM((8, 2, 16, PAIR), BF),
            pltpu.VMEM((8, ROWS, PAIR), BF),
            pltpu.VMEM((8, ROWS, PAIR), BF),
            pltpu.VMEM((16, 8, 2, 16, PAIR), BF),
            pltpu.VMEM((2, 4 * TILE, HEAD_DIM), BF),
            pltpu.VMEM((2, 4 * TILE, HEAD_DIM), BF),
            pltpu.VMEM((2, 4, HEAD_DIM, TILE), BF),
            pltpu.VMEM((2, 4, HEAD_DIM, TILE), BF),
            pltpu.VMEM((HEAD_DIM, 2 * ROWS), BF),
            pltpu.VMEM((HEAD_DIM, 2 * ROWS), BF),
            pltpu.VMEM((4, TILE, 2 * ROWS), F32),
            pltpu.VMEM((HEAD_DIM, 2 * ROWS), F32),
            pltpu.VMEM((2, 2, 4 * TILE, HEAD_DIM), F32),
            pltpu.VMEM((4, 16, 2, 2, 16, PAIR), BF),
            pltpu.VMEM((4, 16, 2, 2, 16, PAIR), BF),
            pltpu.VMEM((8, ROWS, PAIR), BF),
            pltpu.VMEM((8, ROWS, PAIR), BF),
            pltpu.VMEM((8, 8, ROWS), F32),
            pltpu.VMEM((8, 8, ROWS), F32),
            pltpu.VMEM((8, 8, ROWS), F32),
            pltpu.VMEM((8, 2, 16, PAIR), F32),
            dma((4,)),
            dma((5,)),
        ]
        + [dma((8,))] * 8
        + [dma((16,))] * 2
        + [dma((8,))] * 6
        + [dma((4, 16))] * 2
        + [dma((8,))] * 2,
        compiler_params=pltpu.CompilerParams(
            collective_id=0, has_side_effects=True, vmem_limit_bytes=56 * 1024 * 1024
        ),
        name="exchange",
    )(queries, keys_in, values_in, cotangent)


def local_kernel(
    q_ref, k_ref, v_ref, g_ref, o_ref, dq_ref, st_ref, dkv_ref, out_ref, gq_ref, gk_ref, gv_ref
):
    key_pos = lax.broadcasted_iota(jnp.int32, (BLOCK, BLOCK), 0)
    query_pos = lax.broadcasted_iota(jnp.int32, (BLOCK, BLOCK), 1)
    causal = key_pos <= query_pos
    for hh in range(2):
        cols = slice(hh * HEAD_DIM, (hh + 1) * HEAD_DIM)
        for r in range(2):
            rows = slice(r * BLOCK, (r + 1) * BLOCK)
            q, k, v, g = q_ref[rows, cols], k_ref[rows, cols], v_ref[rows, cols], g_ref[rows, cols]
            lse = st_ref[0, hh : hh + 1, rows]
            delta = st_ref[0, hh + 2 : hh + 3, rows]
            raw = dot(k, q, NT)
            probs = jnp.where(causal, jnp.exp2(jnp.where(causal, raw * C2 - lse, NEG)), 0.0)
            probs_b = probs.astype(BF)
            dprob = dot(v, g, NT)
            dscore = (probs * (dprob - delta)).astype(BF)
            out = dot(probs_b, v, TN)
            out_ref[rows, cols] = (out + o_ref[rows, cols].astype(F32)).astype(BF)
            grad_q = dot(dscore, k, TN) * SCALE
            gq_ref[rows, cols] = (grad_q + dq_ref[rows, cols].astype(F32)).astype(BF)
            keep = slice(0, BLOCK - SUMMARY)
            last = slice(BLOCK - SUMMARY, BLOCK)
            part = slice(r * SUMMARY, (r + 1) * SUMMARY)
            grad_k = dot(dscore, q, NN) * SCALE
            grad_k = jnp.concatenate([grad_k[keep], grad_k[last] + dkv_ref[0, 0, part, cols]], axis=0)
            gk_ref[rows, cols] = grad_k.astype(BF)
            grad_v = dot(probs_b, g, NN)
            grad_v = jnp.concatenate([grad_v[keep], grad_v[last] + dkv_ref[0, 1, part, cols]], axis=0)
            gv_ref[rows, cols] = grad_v.astype(BF)


def finish(queries, keys_in, values_in, cotangent, o_sum, dq_sum, stats, dkv_sum):
    wide = pl.BlockSpec((ROWS, PAIR), lambda j: (0, j))
    return pl.pallas_call(
        local_kernel,
        grid=(8,),
        out_shape=[jax.ShapeDtypeStruct((ROWS, WIDTH), BF)] * 4,
        in_specs=[wide] * 6
        + [
            pl.BlockSpec((1, 8, ROWS), lambda j: (j, 0, 0)),
            pl.BlockSpec((1, 2, 16, PAIR), lambda j: (j, 0, 0, 0)),
        ],
        out_specs=[wide] * 4,
        name="finish",
    )(queries, keys_in, values_in, cotangent, o_sum, dq_sum, stats, dkv_sum)


def on_device(queries, keys_in, values_in, cotangent):
    args = (queries, keys_in, values_in, cotangent)
    return tuple(finish(*args, *exchange(*args)))


def solution(mesh):
    spec = P(("seq", "head"), None)
    return jax.shard_map(
        on_device,
        mesh=mesh,
        in_specs=(spec,) * 4,
        out_specs=(spec,) * 4,
        check_vma=False,
    )
```

```python
import math

import jax
import jax.numpy as jnp
from jax import lax
from jax.experimental import pallas as pl
from jax.experimental.pallas import tpu as pltpu
from jax.sharding import PartitionSpec as P

HEADS = 16
HEAD_DIM = 128
BLOCK = 128
SUMMARY = 8
WIDTH = 2048
ROWS = 256
PAIR = 256
NY, NX, NC, NZ = 4, 4, 2, 4
TILE = 512

MESH = pl.DeviceIdType.MESH
NEG = -1e30
LOG2E = 1.4426950408889634
SCALE = 1.0 / math.sqrt(HEAD_DIM)
C2 = SCALE * LOG2E
BF = jnp.bfloat16
F32 = jnp.float32

NT = (((1,), (1,)), ((), ()))
TN = (((0,), (0,)), ((), ()))
NN = (((1,), (0,)), ((), ()))


def dot(a, b, dims):
    return lax.dot_general(a, b, dims, preferred_element_type=F32)


def cols_of(pair):
    return pl.ds(pl.multiple_of(pair * PAIR, PAIR), PAIR)


def exchange_kernel(
    q_hbm, k_hbm, v_hbm, g_hbm,
    o_out, dq_out, st_out, dkv_out,
    q_v, k_v, v_v, g_v,
    kv_pack, q_all, g_all, kv_all, kt_h, vt_h,
    q_t, g_t, score, acc_t, grad_kv,
    part_one, recv_one, part_two, recv_two,
    o_buf, dq_buf, st_send, st_all, st_back, dkv_sum,
    load_sem, own_sem,
    kv_ss, kv_rs, q_ss, q_rs, g_ss, g_rs, st_ss, st_rs,
    near_ss, near_rs, far_ss, far_rs,
    o_ss, o_rs, dq_ss, dq_rs, sb_ss, sb_rs,
    one_ss, one_rs, two_ss, two_rs, dkv_ss, dkv_rs,
):
    s = lax.axis_index("seq")
    z0 = lax.axis_index("head")
    y0 = lax.div(s, 8)
    x0 = lax.rem(lax.div(s, 2), 4)
    c0 = lax.rem(s, 2)
    j0 = y0 * 2 + c0

    def member_id(pair):
        return (lax.div(pair, 2) * 8 + x0 * 2 + lax.rem(pair, 2), z0)

    def x_id(xt):
        return (y0 * 8 + xt * 2 + c0, z0)

    def z_id(zt):
        return (s, zt)

    def group_peer(step):
        yt = lax.rem(y0 + step // 2, 4)
        ct = lax.rem(c0 + step % 2, 2)
        return yt * 2 + ct

    group_steps = (1, 2, 3, 6, 7, 4, 5)
    ring_steps = (1, 3, 2)

    def head_cols(pair, hh):
        return pl.ds(pl.multiple_of(pair * PAIR + hh * HEAD_DIM, HEAD_DIM), HEAD_DIM)

    loads = [
        pltpu.make_async_copy(src, dst, load_sem.at[i])
        for i, (src, dst) in enumerate(((k_hbm, k_v), (v_hbm, v_v), (q_hbm, q_v), (g_hbm, g_v)))
    ]
    for load in loads:
        load.start()
    own_in = []
    for hh in range(2):
        own_in.append((
            pltpu.make_async_copy(
                q_hbm.at[:, head_cols(j0, hh)], q_all.at[hh, j0], own_sem.at[2 * hh]
            ),
            pltpu.make_async_copy(
                g_hbm.at[:, head_cols(j0, hh)], g_all.at[hh, j0], own_sem.at[2 * hh + 1]
            ),
        ))
        own_in[hh][0].start()
        own_in[hh][1].start()

    barrier = pltpu.get_barrier_semaphore()

    def greet(device):
        pl.semaphore_signal(barrier, inc=1, device_id=device, device_id_type=MESH)

    for step in range(1, 8):
        greet(member_id(group_peer(step)))
    for step in ring_steps:
        greet(x_id(lax.rem(x0 + step, 4)))
        greet(z_id(lax.rem(z0 + step, 4)))

    loads[0].wait()
    loads[1].wait()
    for i, src in enumerate((k_v, v_v)):
        for j in range(8):
            for hh in range(2):
                cols = slice(j * PAIR + hh * HEAD_DIM, j * PAIR + (hh + 1) * HEAD_DIM)
                top = src[112:128, cols].astype(F32)[8:, :]
                low = src[240:256, cols].astype(F32)[8:, :]
                kv_pack[j, hh, i] = jnp.concatenate([top, low], axis=0).astype(BF)
    own_kv = pltpu.make_async_copy(
        kv_pack.at[j0], kv_all.at[:, :, y0, x0, c0, z0], own_sem.at[4]
    )
    own_kv.start()
    pl.semaphore_wait(barrier, 13)

    def remote(src, dst, ssem, rsem, device):
        return pltpu.make_async_remote_copy(
            src_ref=src,
            dst_ref=dst,
            send_sem=ssem,
            recv_sem=rsem,
            device_id=device,
            device_id_type=MESH,
        )

    def kv_copy(pair, slot):
        dst = kv_all.at[:, :, lax.div(slot, 2), x0, lax.rem(slot, 2), z0]
        return remote(kv_pack.at[pair], dst, kv_ss.at[pair], kv_rs.at[slot], member_id(pair))

    def q_copy(hh, pair, slot):
        return remote(
            q_hbm.at[:, head_cols(pair, hh)], q_all.at[hh, slot],
            q_ss.at[hh, pair], q_rs.at[hh, slot], member_id(pair),
        )

    def g_copy(hh, pair, slot):
        return remote(
            g_hbm.at[:, head_cols(pair, hh)], g_all.at[hh, slot],
            g_ss.at[hh, pair], g_rs.at[hh, slot], member_id(pair),
        )

    def st_copy(pair, slot):
        return remote(
            st_send.at[pair], st_all.at[slot], st_ss.at[pair], st_rs.at[slot], member_id(pair)
        )

    def o_copy(hh, pair, slot):
        return remote(
            o_buf.at[hh, pair], o_out.at[:, head_cols(slot, hh)],
            o_ss.at[hh, pair], o_rs.at[hh, slot], member_id(pair),
        )

    def dq_copy(hh, pair, slot):
        return remote(
            dq_buf.at[hh, pair], dq_out.at[:, head_cols(slot, hh)],
            dq_ss.at[hh, pair], dq_rs.at[hh, slot], member_id(pair),
        )

    def sb_copy(pair, slot):
        return remote(
            st_back.at[pair], st_out.at[slot], sb_ss.at[pair], sb_rs.at[slot], member_id(pair)
        )

    def dkv_copy(hh, pair, slot):
        return remote(
            dkv_sum.at[hh, pair], dkv_out.at[slot, hh],
            dkv_ss.at[hh, pair], dkv_rs.at[hh, slot], member_id(pair),
        )

    def near_copy(hh, kind, peer, slot):
        if kind == 0:
            view, device = kv_all.at[hh, 0, :, slot, :, z0], x_id(peer)
        else:
            view, device = kv_all.at[hh, 1, :, x0, :, slot], z_id(peer)
        return remote(
            view, view, near_ss.at[hh, kind, peer], near_rs.at[hh, kind, slot], device
        )

    def far_copy(hh, kind, item, peer, slot):
        if kind == 0:
            view, device = kv_all.at[hh, 0, :, item, :, slot], z_id(peer)
        else:
            view, device = kv_all.at[hh, 1, :, slot, :, item], x_id(peer)
        return remote(
            view, view, far_ss.at[hh, kind, item, peer], far_rs.at[hh, kind, item, slot], device
        )

    def one_copy(hh, kind, peer, slot):
        if kind == 0:
            src, device = part_one.at[hh, 0, :, peer], x_id(peer)
            dst = recv_one.at[hh, 0, slot]
        else:
            src, device = part_one.at[hh, 1, :, :, :, peer], z_id(peer)
            dst = recv_one.at[hh, 1, slot]
        dst = dst.reshape(*src.shape)
        return remote(src, dst, one_ss.at[hh, kind, peer], one_rs.at[hh, kind, slot], device)

    def two_copy(hh, kind, peer, slot):
        device = z_id(peer) if kind == 0 else x_id(peer)
        return remote(
            part_two.at[hh, kind, peer], recv_two.at[hh, kind, slot],
            two_ss.at[hh, kind, peer], two_rs.at[hh, kind, slot], device,
        )

    near_place = (x0, z0)
    far_place = (z0, x0)

    def near_peer(kind, step):
        return lax.rem(near_place[kind] + step, 4)

    def far_peer(kind, step):
        return lax.rem(far_place[kind] + step, 4)

    for step in group_steps:
        kv_copy(group_peer(step), j0).start()
    for step in group_steps:
        q_copy(0, group_peer(step), j0).start()
        g_copy(0, group_peer(step), j0).start()

    own_kv.wait()
    for step in group_steps:
        kv_copy(group_peer(step), group_peer(step)).wait_recv()

    def gather_start(hh):
        for kind in range(2):
            for step in ring_steps:
                near_copy(hh, kind, near_peer(kind, step), near_place[kind]).start()
        for kind in range(2):
            for step in ring_steps:
                far_copy(
                    hh, kind, near_place[kind], far_peer(kind, step), far_place[kind]
                ).start()

    def gather_forward(hh):
        for step in ring_steps:
            for kind in range(2):
                item = near_peer(kind, step)
                near_copy(hh, kind, item, item).wait_recv()
                for hop in ring_steps:
                    far_copy(hh, kind, item, far_peer(kind, hop), far_place[kind]).start()

    def gather_wait(hh):
        for kind in range(2):
            for step in (0,) + ring_steps:
                item = near_peer(kind, step)
                for hop in ring_steps:
                    peer = far_peer(kind, hop)
                    far_copy(hh, kind, item, peer, peer).wait_recv()

    gather_start(0)

    loads[2].wait()
    loads[3].wait()
    key_pos = lax.broadcasted_iota(jnp.int32, (BLOCK, BLOCK), 0)
    query_pos = lax.broadcasted_iota(jnp.int32, (BLOCK, BLOCK), 1)
    causal = key_pos <= query_pos

    def local_turn(j, carry):
        for hh in range(2):
            cols = head_cols(j, hh)
            for r in range(2):
                rows = slice(r * BLOCK, (r + 1) * BLOCK)
                raw = dot(k_v[rows, cols], q_v[rows, cols], NT)
                raw = jnp.where(causal, raw, NEG)
                high = jnp.max(raw, axis=0, keepdims=True)
                weights = jnp.exp2((raw - high) * C2)
                dprob = dot(v_v[rows, cols], g_v[rows, cols], NT)
                st_send[j, 3 * hh : 3 * hh + 1, rows] = high
                st_send[j, 3 * hh + 1 : 3 * hh + 2, rows] = jnp.sum(weights, axis=0, keepdims=True)
                st_send[j, 3 * hh + 2 : 3 * hh + 3, rows] = jnp.sum(
                    weights * dprob, axis=0, keepdims=True
                )
        return carry

    st_send[...] = jnp.zeros_like(st_send)
    lax.fori_loop(0, 4, local_turn, 0)
    gather_forward(0)
    gather_start(1)
    lax.fori_loop(4, 8, local_turn, 0)
    own_st = pltpu.make_async_copy(st_send.at[j0], st_all.at[j0], own_sem.at[5])
    own_st.start()
    for step in group_steps:
        st_copy(group_peer(step), j0).start()
    for step in group_steps:
        q_copy(1, group_peer(step), j0).start()
        g_copy(1, group_peer(step), j0).start()

    grad_kv[...] = jnp.zeros_like(grad_kv)
    st_back[...] = jnp.zeros_like(st_back)
    own_st.wait()

    lane = lax.broadcasted_iota(jnp.int32, (1, 2 * ROWS), 1)
    lane_limit = x0 * 128 + z0 * 16 + lax.div(lane, 256) * 64 + lax.rem(lax.div(lane, 128), 2) * 8
    key_row = lax.broadcasted_iota(jnp.int32, (TILE, 2 * ROWS), 0)

    def tile_of(hh, kind, kt):
        return kv_all[hh, kind, kt].reshape(TILE, HEAD_DIM)

    def attend(hh, y):
        q_rows = q_all[hh, pl.ds(2 * y, 2)].reshape(2 * ROWS, HEAD_DIM)
        g_rows = g_all[hh, pl.ds(2 * y, 2)].reshape(2 * ROWS, HEAD_DIM)
        q_t[...] = q_rows.T
        g_t[...] = g_rows.T
        limit = lane_limit + y * TILE

        def stat(kind):
            row = slice(hh * 3 + kind, hh * 3 + kind + 1)
            return jnp.concatenate([st_all[2 * y, row, :], st_all[2 * y + 1, row, :]], axis=1)

        local_high = stat(0)
        local_sum = stat(1)
        local_delta = stat(2)

        def score_turn(kt, high):
            raw = dot(tile_of(hh, 0, kt), q_t[...], NN)
            raw = jnp.where(key_row + kt * TILE < limit, raw, NEG)
            score[kt] = raw
            return jnp.maximum(high, jnp.max(raw, axis=0, keepdims=True))

        high = lax.fori_loop(0, y + 1, score_turn, local_high)
        acc_t[...] = jnp.zeros_like(acc_t)

        def value_turn(kt, total):
            weights = jnp.exp2((score[kt] - high) * C2)
            score[kt] = weights
            acc_t[...] += dot(vt_h[kt], weights.astype(BF), NN)
            return total + jnp.sum(weights, axis=0, keepdims=True)

        shrink = jnp.exp2((local_high - high) * C2)
        total = lax.fori_loop(0, y + 1, value_turn, local_sum * shrink)
        inverse = 1.0 / total
        out_t = acc_t[...]
        delta = (
            local_delta * shrink
            + jnp.sum(out_t * g_t[...].astype(F32), axis=0, keepdims=True)
        ) * inverse
        lse = high * C2 + jnp.log(total) * LOG2E
        out = (out_t * inverse).T.astype(BF)
        for c in range(2):
            half = slice(c * ROWS, (c + 1) * ROWS)
            o_buf[hh, 2 * y + c] = out[half]
            st_back[2 * y + c, hh : hh + 1, :] = lse[:, half]
            st_back[2 * y + c, hh + 2 : hh + 3, :] = delta[:, half]
        acc_t[...] = jnp.zeros_like(acc_t)

        def grad_turn(kt, carry):
            tile = pl.ds(pl.multiple_of(kt * TILE, TILE), TILE)
            probs = score[kt] * inverse
            dprob = dot(tile_of(hh, 1, kt), g_t[...], NN)
            dscore = (probs * (dprob - delta)).astype(BF)
            acc_t[...] += dot(kt_h[kt], dscore, NN)
            grad_kv[hh, 0, tile, :] += dot(dscore, q_rows, NN)
            grad_kv[hh, 1, tile, :] += dot(probs.astype(BF), g_rows, NN)
            return carry

        lax.fori_loop(0, y + 1, grad_turn, 0)
        grad_q = (acc_t[...] * SCALE).T.astype(BF)
        for c in range(2):
            dq_buf[hh, 2 * y + c] = grad_q[c * ROWS : (c + 1) * ROWS]

    def reduce_start(hh):
        def cast_turn(y, carry):
            tile = pl.ds(pl.multiple_of(y * TILE, TILE), TILE)
            shape = (4, 2, 4, 16, HEAD_DIM)
            part_one[hh, 0, y] = (grad_kv[hh, 0, tile, :] * SCALE).astype(BF).reshape(shape)
            part_one[hh, 1, y] = grad_kv[hh, 1, tile, :].astype(BF).reshape(shape)
            return carry

        lax.fori_loop(0, 4, cast_turn, 0)
        for step in ring_steps:
            for kind in range(2):
                one_copy(hh, kind, near_peer(kind, step), near_place[kind]).start()

    def reduce_middle(hh):
        for kind in range(2):
            for step in ring_steps:
                peer = near_peer(kind, step)
                one_copy(hh, kind, peer, peer).wait_recv()
        for kind in range(2):

            def add_turn(y, carry, kind=kind):
                if kind == 0:
                    total = part_one[hh, 0, y, x0].astype(F32)
                else:
                    total = part_one[hh, 1, y, :, :, z0].astype(F32)
                for step in ring_steps:
                    total += recv_one[hh, kind, near_peer(kind, step), y].reshape(
                        total.shape
                    ).astype(F32)
                total = total.astype(BF)
                for item in range(4):
                    part_two[hh, kind, item, y] = total[:, item] if kind == 0 else total[item]
                return carry

            lax.fori_loop(0, 4, add_turn, 0)
            for step in ring_steps:
                two_copy(hh, kind, far_peer(kind, step), far_place[kind]).start()

    def reduce_end(hh):
        for kind in range(2):
            for step in ring_steps:
                peer = far_peer(kind, step)
                two_copy(hh, kind, peer, peer).wait_recv()
            total = part_two[hh, kind, far_place[kind]].astype(F32)
            for step in ring_steps:
                total += recv_two[hh, kind, far_peer(kind, step)].astype(F32)
            for y in range(4):
                for c in range(2):
                    dkv_sum[hh, 2 * y + c, kind] = total[y, c]
        for step in group_steps:
            dkv_copy(hh, group_peer(step), j0).start()
        pltpu.make_async_copy(dkv_sum.at[hh, j0], dkv_out.at[j0, hh], own_sem.at[6 + hh]).start()

    for hh in range(2):
        if hh == 0:
            gather_forward(1)
        gather_wait(hh)
        for y in range(4):
            kt_h[y] = tile_of(hh, 0, y).T
            vt_h[y] = tile_of(hh, 1, y).T
        own_in[hh][0].wait()
        own_in[hh][1].wait()

        def member_turn(i, carry, hh=hh):
            if hh == 1:

                @pl.when(i == 2)
                def _():
                    reduce_middle(0)

            turn = i if hh == 0 else 3 - i
            dy = turn + lax.div(turn, 2) * (5 - 2 * turn)
            y = lax.rem(y0 + dy, 4)
            for c in range(2):
                pair = 2 * y + c

                @pl.when(pair != j0)
                def _(pair=pair):
                    q_copy(hh, pair, pair).wait_recv()
                    g_copy(hh, pair, pair).wait_recv()
                    if hh == 0:
                        st_copy(pair, pair).wait_recv()

            attend(hh, y)
            for c in range(2):
                pair = 2 * y + c

                @pl.when(pair != j0)
                def _(pair=pair):
                    o_copy(hh, pair, j0).start()
                    dq_copy(hh, pair, j0).start()
                    if hh == 1:
                        sb_copy(pair, j0).start()

            return carry

        lax.fori_loop(0, 4, member_turn, 0)
        reduce_start(hh)

    own_out = [
        pltpu.make_async_copy(st_back.at[j0], st_out.at[j0], own_sem.at[4])
    ]
    for hh in range(2):
        own_out.append(pltpu.make_async_copy(
            o_buf.at[hh, j0], o_out.at[:, head_cols(j0, hh)], own_sem.at[2 * hh]
        ))
        own_out.append(pltpu.make_async_copy(
            dq_buf.at[hh, j0], dq_out.at[:, head_cols(j0, hh)], own_sem.at[2 * hh + 1]
        ))
    for copy in own_out:
        copy.start()
    reduce_end(0)
    reduce_middle(1)
    reduce_end(1)

    for copy in own_out:
        copy.wait()
    for hh in range(2):
        pltpu.make_async_copy(dkv_sum.at[hh, j0], dkv_out.at[j0, hh], own_sem.at[6 + hh]).wait()
    for step in group_steps:
        pair = group_peer(step)
        sb_copy(pair, pair).wait_recv()
        for hh in range(2):
            o_copy(hh, pair, pair).wait_recv()
            dq_copy(hh, pair, pair).wait_recv()
            dkv_copy(hh, pair, pair).wait_recv()
        kv_copy(pair, j0).wait_send()
        st_copy(pair, j0).wait_send()
        sb_copy(pair, j0).wait_send()
        for hh in range(2):
            for copy in (q_copy, g_copy, o_copy, dq_copy, dkv_copy):
                copy(hh, pair, j0).wait_send()
    for hh in range(2):
        for kind in range(2):
            for step in ring_steps:
                peer = near_peer(kind, step)
                near_copy(hh, kind, peer, near_place[kind]).wait_send()
                one_copy(hh, kind, peer, near_place[kind]).wait_send()
                peer = far_peer(kind, step)
                two_copy(hh, kind, peer, far_place[kind]).wait_send()
                for hop in (0,) + ring_steps:
                    item = near_peer(kind, hop)
                    far_copy(hh, kind, item, peer, far_place[kind]).wait_send()


def exchange(queries, keys_in, values_in, cotangent):
    any_spec = pl.BlockSpec(memory_space=pl.ANY)
    dma = pltpu.SemaphoreType.DMA
    return pl.pallas_call(
        exchange_kernel,
        out_shape=(
            jax.ShapeDtypeStruct((ROWS, WIDTH), BF),
            jax.ShapeDtypeStruct((ROWS, WIDTH), BF),
            jax.ShapeDtypeStruct((8, 8, ROWS), F32),
            jax.ShapeDtypeStruct((8, 2, 2, 16, HEAD_DIM), F32),
        ),
        in_specs=[any_spec] * 4,
        out_specs=(any_spec,) * 4,
        scratch_shapes=[
            pltpu.VMEM((ROWS, WIDTH), BF),
            pltpu.VMEM((ROWS, WIDTH), BF),
            pltpu.VMEM((ROWS, WIDTH), BF),
            pltpu.VMEM((ROWS, WIDTH), BF),
            pltpu.VMEM((8, 2, 2, 16, HEAD_DIM), BF),
            pltpu.VMEM((2, 8, ROWS, HEAD_DIM), BF),
            pltpu.VMEM((2, 8, ROWS, HEAD_DIM), BF),
            pltpu.VMEM((2, 2, 4, 4, 2, 4, 16, HEAD_DIM), BF),
            pltpu.VMEM((4, HEAD_DIM, TILE), BF),
            pltpu.VMEM((4, HEAD_DIM, TILE), BF),
            pltpu.VMEM((HEAD_DIM, 2 * ROWS), BF),
            pltpu.VMEM((HEAD_DIM, 2 * ROWS), BF),
            pltpu.VMEM((4, TILE, 2 * ROWS), F32),
            pltpu.VMEM((HEAD_DIM, 2 * ROWS), F32),
            pltpu.VMEM((2, 2, 4 * TILE, HEAD_DIM), F32),
            pltpu.VMEM((2, 2, 4, 4, 2, 4, 16, HEAD_DIM), BF),
            pltpu.VMEM((2, 2, 4, 4, 8, 16, HEAD_DIM), BF),
            pltpu.VMEM((2, 2, 4, 4, 2, 16, HEAD_DIM), BF),
            pltpu.VMEM((2, 2, 4, 4, 2, 16, HEAD_DIM), BF),
            pltpu.VMEM((2, 8, ROWS, HEAD_DIM), BF),
            pltpu.VMEM((2, 8, ROWS, HEAD_DIM), BF),
            pltpu.VMEM((8, 8, ROWS), F32),
            pltpu.VMEM((8, 8, ROWS), F32),
            pltpu.VMEM((8, 8, ROWS), F32),
            pltpu.VMEM((2, 8, 2, 16, HEAD_DIM), F32),
            dma((4,)),
            dma((8,)),
        ]
        + [dma((8,))] * 2
        + [dma((2, 8))] * 4
        + [dma((8,))] * 2
        + [dma((2, 2, 4))] * 2
        + [dma((2, 2, 4, 4))] * 2
        + [dma((2, 8))] * 4
        + [dma((8,))] * 2
        + [dma((2, 2, 4))] * 4
        + [dma((2, 8))] * 2,
        compiler_params=pltpu.CompilerParams(
            collective_id=0, has_side_effects=True, vmem_limit_bytes=56 * 1024 * 1024
        ),
        name="exchange",
    )(queries, keys_in, values_in, cotangent)


def local_kernel(
    q_ref, k_ref, v_ref, g_ref, o_ref, dq_ref, st_ref, dkv_ref, out_ref, gq_ref, gk_ref, gv_ref
):
    key_pos = lax.broadcasted_iota(jnp.int32, (BLOCK, BLOCK), 0)
    query_pos = lax.broadcasted_iota(jnp.int32, (BLOCK, BLOCK), 1)
    causal = key_pos <= query_pos
    for hh in range(2):
        cols = slice(hh * HEAD_DIM, (hh + 1) * HEAD_DIM)
        for r in range(2):
            rows = slice(r * BLOCK, (r + 1) * BLOCK)
            q, k, v, g = q_ref[rows, cols], k_ref[rows, cols], v_ref[rows, cols], g_ref[rows, cols]
            lse = st_ref[0, hh : hh + 1, rows]
            delta = st_ref[0, hh + 2 : hh + 3, rows]
            raw = dot(k, q, NT)
            probs = jnp.where(causal, jnp.exp2(jnp.where(causal, raw * C2 - lse, NEG)), 0.0)
            probs_b = probs.astype(BF)
            dprob = dot(v, g, NT)
            dscore = (probs * (dprob - delta)).astype(BF)
            out = dot(probs_b, v, TN)
            out_ref[rows, cols] = (out + o_ref[rows, cols].astype(F32)).astype(BF)
            grad_q = dot(dscore, k, TN) * SCALE
            gq_ref[rows, cols] = (grad_q + dq_ref[rows, cols].astype(F32)).astype(BF)
            keep = slice(0, BLOCK - SUMMARY)
            last = slice(BLOCK - SUMMARY, BLOCK)
            part = slice(r * SUMMARY, (r + 1) * SUMMARY)
            grad_k = dot(dscore, q, NN) * SCALE
            grad_k = jnp.concatenate([grad_k[keep], grad_k[last] + dkv_ref[0, hh, 0, part, :]], axis=0)
            gk_ref[rows, cols] = grad_k.astype(BF)
            grad_v = dot(probs_b, g, NN)
            grad_v = jnp.concatenate([grad_v[keep], grad_v[last] + dkv_ref[0, hh, 1, part, :]], axis=0)
            gv_ref[rows, cols] = grad_v.astype(BF)


def finish(queries, keys_in, values_in, cotangent, o_sum, dq_sum, stats, dkv_sum):
    wide = pl.BlockSpec((ROWS, PAIR), lambda j: (0, j))
    return pl.pallas_call(
        local_kernel,
        grid=(8,),
        out_shape=[jax.ShapeDtypeStruct((ROWS, WIDTH), BF)] * 4,
        in_specs=[wide] * 6
        + [
            pl.BlockSpec((1, 8, ROWS), lambda j: (j, 0, 0)),
            pl.BlockSpec((1, 2, 2, 16, HEAD_DIM), lambda j: (j, 0, 0, 0, 0)),
        ],
        out_specs=[wide] * 4,
        name="finish",
    )(queries, keys_in, values_in, cotangent, o_sum, dq_sum, stats, dkv_sum)


def on_device(queries, keys_in, values_in, cotangent):
    args = (queries, keys_in, values_in, cotangent)
    return tuple(finish(*args, *exchange(*args)))


def solution(mesh):
    spec = P(("seq", "head"), None)
    return jax.shard_map(
        on_device,
        mesh=mesh,
        in_specs=(spec,) * 4,
        out_specs=(spec,) * 4,
        check_vma=False,
    )
```

```python
import math

import jax
import jax.numpy as jnp
from jax import lax
from jax.experimental import pallas as pl
from jax.experimental.pallas import tpu as pltpu
from jax.sharding import PartitionSpec as P

HEADS = 16
HEAD_DIM = 128
BLOCK = 128
SUMMARY = 8
WIDTH = 2048
ROWS = 256
PAIR = 256
NY, NX, NC, NZ = 4, 4, 2, 4
TILE = 512

MESH = pl.DeviceIdType.MESH
NEG = -1e30
LOG2E = 1.4426950408889634
SCALE = 1.0 / math.sqrt(HEAD_DIM)
C2 = SCALE * LOG2E
BF = jnp.bfloat16
F32 = jnp.float32

NT = (((1,), (1,)), ((), ()))
TN = (((0,), (0,)), ((), ()))
NN = (((1,), (0,)), ((), ()))


def dot(a, b, dims):
    return lax.dot_general(a, b, dims, preferred_element_type=F32)


def cols_of(pair):
    return pl.ds(pl.multiple_of(pair * PAIR, PAIR), PAIR)


def exchange_kernel(
    q_hbm, k_hbm, v_hbm, g_hbm,
    out_hbm, gq_hbm, gk_hbm, gv_hbm,
    q_v, k_v, v_v, g_v,
    kv_pack, q_all, g_all, kv_all, kt_h, vt_h,
    q_t, g_t, score, acc_t, grad_kv,
    part_one, recv_one, part_two, recv_two,
    o_buf, dq_buf, st_send, st_all, st_back, dkv_sum,
    o_in, dq_in, st_in, dkv_in,
    own_e, own_dp, own_o, own_dq, last_rows, out_v, gq_v, gk_v, gv_v,
    load_sem, own_sem, out_sem,
    kv_ss, kv_rs, q_ss, q_rs, g_ss, g_rs, st_ss, st_rs,
    near_ss, near_rs, far_ss, far_rs,
    o_ss, o_rs, dq_ss, dq_rs, sb_ss, sb_rs,
    one_ss, one_rs, two_ss, two_rs, dkv_ss, dkv_rs,
):
    s = lax.axis_index("seq")
    z0 = lax.axis_index("head")
    y0 = lax.div(s, 8)
    x0 = lax.rem(lax.div(s, 2), 4)
    c0 = lax.rem(s, 2)
    j0 = y0 * 2 + c0

    def member_id(pair):
        return (lax.div(pair, 2) * 8 + x0 * 2 + lax.rem(pair, 2), z0)

    def x_id(xt):
        return (y0 * 8 + xt * 2 + c0, z0)

    def z_id(zt):
        return (s, zt)

    def group_peer(step):
        yt = lax.rem(y0 + step // 2, 4)
        ct = lax.rem(c0 + step % 2, 2)
        return yt * 2 + ct

    group_steps = (1, 2, 3, 6, 7, 4, 5)
    ring_steps = (1, 3, 2)

    def head_cols(pair, hh):
        return pl.ds(pl.multiple_of(pair * PAIR + hh * HEAD_DIM, HEAD_DIM), HEAD_DIM)

    loads = [
        pltpu.make_async_copy(src, dst, load_sem.at[i])
        for i, (src, dst) in enumerate(((k_hbm, k_v), (v_hbm, v_v), (q_hbm, q_v), (g_hbm, g_v)))
    ]
    for load in loads:
        load.start()
    own_in = []
    for hh in range(2):
        own_in.append((
            pltpu.make_async_copy(
                q_hbm.at[:, head_cols(j0, hh)], q_all.at[hh, j0], own_sem.at[2 * hh]
            ),
            pltpu.make_async_copy(
                g_hbm.at[:, head_cols(j0, hh)], g_all.at[hh, j0], own_sem.at[2 * hh + 1]
            ),
        ))
        own_in[hh][0].start()
        own_in[hh][1].start()

    barrier = pltpu.get_barrier_semaphore()

    def greet(device):
        pl.semaphore_signal(barrier, inc=1, device_id=device, device_id_type=MESH)

    for step in range(1, 8):
        greet(member_id(group_peer(step)))
    for step in ring_steps:
        greet(x_id(lax.rem(x0 + step, 4)))
        greet(z_id(lax.rem(z0 + step, 4)))

    loads[0].wait()
    loads[1].wait()
    for i, src in enumerate((k_v, v_v)):
        for j in range(8):
            for hh in range(2):
                cols = slice(j * PAIR + hh * HEAD_DIM, j * PAIR + (hh + 1) * HEAD_DIM)
                top = src[112:128, cols].astype(F32)[8:, :]
                low = src[240:256, cols].astype(F32)[8:, :]
                kv_pack[j, hh, i] = jnp.concatenate([top, low], axis=0).astype(BF)
    own_kv = pltpu.make_async_copy(
        kv_pack.at[j0], kv_all.at[:, :, y0, x0, c0, z0], own_sem.at[4]
    )
    own_kv.start()
    pl.semaphore_wait(barrier, 13)

    def remote(src, dst, ssem, rsem, device):
        return pltpu.make_async_remote_copy(
            src_ref=src,
            dst_ref=dst,
            send_sem=ssem,
            recv_sem=rsem,
            device_id=device,
            device_id_type=MESH,
        )

    def kv_copy(pair, slot):
        dst = kv_all.at[:, :, lax.div(slot, 2), x0, lax.rem(slot, 2), z0]
        return remote(kv_pack.at[pair], dst, kv_ss.at[pair], kv_rs.at[slot], member_id(pair))

    def q_copy(hh, pair, slot):
        return remote(
            q_hbm.at[:, head_cols(pair, hh)], q_all.at[hh, slot],
            q_ss.at[hh, pair], q_rs.at[hh, slot], member_id(pair),
        )

    def g_copy(hh, pair, slot):
        return remote(
            g_hbm.at[:, head_cols(pair, hh)], g_all.at[hh, slot],
            g_ss.at[hh, pair], g_rs.at[hh, slot], member_id(pair),
        )

    def st_copy(pair, slot):
        return remote(
            st_send.at[pair], st_all.at[slot], st_ss.at[pair], st_rs.at[slot], member_id(pair)
        )

    def o_copy(hh, pair, slot):
        return remote(
            o_buf.at[hh, pair], o_in.at[hh, slot],
            o_ss.at[hh, pair], o_rs.at[hh, slot], member_id(pair),
        )

    def dq_copy(hh, pair, slot):
        return remote(
            dq_buf.at[hh, pair], dq_in.at[hh, slot],
            dq_ss.at[hh, pair], dq_rs.at[hh, slot], member_id(pair),
        )

    def sb_copy(pair, slot):
        return remote(
            st_back.at[pair], st_in.at[slot], sb_ss.at[pair], sb_rs.at[slot], member_id(pair)
        )

    def dkv_copy(hh, pair, slot):
        return remote(
            dkv_sum.at[hh, pair], dkv_in.at[hh, slot],
            dkv_ss.at[hh, pair], dkv_rs.at[hh, slot], member_id(pair),
        )

    def near_copy(hh, kind, peer, slot):
        if kind == 0:
            view, device = kv_all.at[hh, 0, :, slot, :, z0], x_id(peer)
        else:
            view, device = kv_all.at[hh, 1, :, x0, :, slot], z_id(peer)
        return remote(
            view, view, near_ss.at[hh, kind, peer], near_rs.at[hh, kind, slot], device
        )

    def far_copy(hh, kind, item, peer, slot):
        if kind == 0:
            view, device = kv_all.at[hh, 0, :, item, :, slot], z_id(peer)
        else:
            view, device = kv_all.at[hh, 1, :, slot, :, item], x_id(peer)
        return remote(
            view, view, far_ss.at[hh, kind, item, peer], far_rs.at[hh, kind, item, slot], device
        )

    def one_copy(hh, kind, peer, slot):
        if kind == 0:
            src, device = part_one.at[hh, 0, :, peer], x_id(peer)
            dst = recv_one.at[hh, 0, slot]
        else:
            src, device = part_one.at[hh, 1, :, :, :, peer], z_id(peer)
            dst = recv_one.at[hh, 1, slot]
        dst = dst.reshape(*src.shape)
        return remote(src, dst, one_ss.at[hh, kind, peer], one_rs.at[hh, kind, slot], device)

    def two_copy(hh, kind, peer, slot):
        device = z_id(peer) if kind == 0 else x_id(peer)
        return remote(
            part_two.at[hh, kind, peer], recv_two.at[hh, kind, slot],
            two_ss.at[hh, kind, peer], two_rs.at[hh, kind, slot], device,
        )

    near_place = (x0, z0)
    far_place = (z0, x0)

    def near_peer(kind, step):
        return lax.rem(near_place[kind] + step, 4)

    def far_peer(kind, step):
        return lax.rem(far_place[kind] + step, 4)

    for step in group_steps:
        kv_copy(group_peer(step), j0).start()
    for step in group_steps:
        q_copy(0, group_peer(step), j0).start()
        g_copy(0, group_peer(step), j0).start()

    own_kv.wait()
    for step in group_steps:
        kv_copy(group_peer(step), group_peer(step)).wait_recv()

    def gather_start(hh):
        for kind in range(2):
            for step in ring_steps:
                near_copy(hh, kind, near_peer(kind, step), near_place[kind]).start()
        for kind in range(2):
            for step in ring_steps:
                far_copy(
                    hh, kind, near_place[kind], far_peer(kind, step), far_place[kind]
                ).start()

    def gather_forward(hh):
        for step in ring_steps:
            for kind in range(2):
                item = near_peer(kind, step)
                near_copy(hh, kind, item, item).wait_recv()
                for hop in ring_steps:
                    far_copy(hh, kind, item, far_peer(kind, hop), far_place[kind]).start()

    def gather_wait(hh):
        for kind in range(2):
            for step in (0,) + ring_steps:
                item = near_peer(kind, step)
                for hop in ring_steps:
                    peer = far_peer(kind, hop)
                    far_copy(hh, kind, item, peer, peer).wait_recv()

    gather_start(0)

    loads[2].wait()
    loads[3].wait()
    key_pos = lax.broadcasted_iota(jnp.int32, (BLOCK, BLOCK), 0)
    query_pos = lax.broadcasted_iota(jnp.int32, (BLOCK, BLOCK), 1)
    causal = key_pos <= query_pos

    def local_turn(j, carry):
        for hh in range(2):
            cols = head_cols(j, hh)
            for r in range(2):
                rows = slice(r * BLOCK, (r + 1) * BLOCK)
                raw = dot(k_v[rows, cols], q_v[rows, cols], NT)
                raw = jnp.where(causal, raw, NEG)
                high = jnp.max(raw, axis=0, keepdims=True)
                weights = jnp.exp2((raw - high) * C2)
                dprob = dot(v_v[rows, cols], g_v[rows, cols], NT)
                own_e[j, 2 * hh + r] = weights
                own_dp[j, 2 * hh + r] = dprob
                st_send[j, 3 * hh : 3 * hh + 1, rows] = high
                st_send[j, 3 * hh + 1 : 3 * hh + 2, rows] = jnp.sum(weights, axis=0, keepdims=True)
                st_send[j, 3 * hh + 2 : 3 * hh + 3, rows] = jnp.sum(
                    weights * dprob, axis=0, keepdims=True
                )
        return carry

    st_send[...] = jnp.zeros_like(st_send)
    lax.fori_loop(0, 4, local_turn, 0)
    gather_forward(0)
    gather_start(1)
    lax.fori_loop(4, 8, local_turn, 0)
    own_st = pltpu.make_async_copy(st_send.at[j0], st_all.at[j0], own_sem.at[5])
    own_st.start()
    for step in group_steps:
        st_copy(group_peer(step), j0).start()
    for step in group_steps:
        q_copy(1, group_peer(step), j0).start()
        g_copy(1, group_peer(step), j0).start()

    grad_kv[...] = jnp.zeros_like(grad_kv)
    st_back[...] = jnp.zeros_like(st_back)
    own_st.wait()

    lane = lax.broadcasted_iota(jnp.int32, (1, 2 * ROWS), 1)
    lane_limit = x0 * 128 + z0 * 16 + lax.div(lane, 256) * 64 + lax.rem(lax.div(lane, 128), 2) * 8
    key_row = lax.broadcasted_iota(jnp.int32, (TILE, 2 * ROWS), 0)

    def tile_of(hh, kind, kt):
        return kv_all[hh, kind, kt].reshape(TILE, HEAD_DIM)

    def attend(hh, y):
        q_rows = q_all[hh, pl.ds(2 * y, 2)].reshape(2 * ROWS, HEAD_DIM)
        g_rows = g_all[hh, pl.ds(2 * y, 2)].reshape(2 * ROWS, HEAD_DIM)
        q_t[...] = q_rows.T
        g_t[...] = g_rows.T
        limit = lane_limit + y * TILE

        def stat(kind):
            row = slice(hh * 3 + kind, hh * 3 + kind + 1)
            return jnp.concatenate([st_all[2 * y, row, :], st_all[2 * y + 1, row, :]], axis=1)

        local_high = stat(0)
        local_sum = stat(1)
        local_delta = stat(2)

        def score_turn(kt, high):
            raw = dot(tile_of(hh, 0, kt), q_t[...], NN)
            raw = jnp.where(key_row + kt * TILE < limit, raw, NEG)
            score[kt] = raw
            return jnp.maximum(high, jnp.max(raw, axis=0, keepdims=True))

        high = lax.fori_loop(0, y + 1, score_turn, local_high)
        acc_t[...] = jnp.zeros_like(acc_t)

        def value_turn(kt, total):
            weights = jnp.exp2((score[kt] - high) * C2)
            score[kt] = weights
            acc_t[...] += dot(vt_h[kt], weights.astype(BF), NN)
            return total + jnp.sum(weights, axis=0, keepdims=True)

        shrink = jnp.exp2((local_high - high) * C2)
        total = lax.fori_loop(0, y + 1, value_turn, local_sum * shrink)
        inverse = 1.0 / total
        out_t = acc_t[...]
        delta = (
            local_delta * shrink
            + jnp.sum(out_t * g_t[...].astype(F32), axis=0, keepdims=True)
        ) * inverse
        lse = high * C2 + jnp.log(total) * LOG2E
        out = (out_t * inverse).T.astype(BF)
        for c in range(2):
            half = slice(c * ROWS, (c + 1) * ROWS)
            o_buf[hh, 2 * y + c] = out[half]
            st_back[2 * y + c, hh : hh + 1, :] = lse[:, half]
            st_back[2 * y + c, hh + 2 : hh + 3, :] = delta[:, half]
        acc_t[...] = jnp.zeros_like(acc_t)

        def grad_turn(kt, carry):
            tile = pl.ds(pl.multiple_of(kt * TILE, TILE), TILE)
            probs = score[kt] * inverse
            dprob = dot(tile_of(hh, 1, kt), g_t[...], NN)
            dscore = (probs * (dprob - delta)).astype(BF)
            acc_t[...] += dot(kt_h[kt], dscore, NN)
            grad_kv[hh, 0, tile, :] += dot(dscore, q_rows, NN)
            grad_kv[hh, 1, tile, :] += dot(probs.astype(BF), g_rows, NN)
            return carry

        lax.fori_loop(0, y + 1, grad_turn, 0)
        grad_q = (acc_t[...] * SCALE).T.astype(BF)
        for c in range(2):
            dq_buf[hh, 2 * y + c] = grad_q[c * ROWS : (c + 1) * ROWS]

    def reduce_start(hh):
        def cast_turn(y, carry):
            tile = pl.ds(pl.multiple_of(y * TILE, TILE), TILE)
            shape = (4, 2, 4, 16, HEAD_DIM)
            part_one[hh, 0, y] = (grad_kv[hh, 0, tile, :] * SCALE).astype(BF).reshape(shape)
            part_one[hh, 1, y] = grad_kv[hh, 1, tile, :].astype(BF).reshape(shape)
            return carry

        lax.fori_loop(0, 4, cast_turn, 0)
        for step in ring_steps:
            for kind in range(2):
                one_copy(hh, kind, near_peer(kind, step), near_place[kind]).start()

    def reduce_middle(hh):
        for kind in range(2):
            for step in ring_steps:
                peer = near_peer(kind, step)
                one_copy(hh, kind, peer, peer).wait_recv()
        for kind in range(2):

            def add_turn(y, carry, kind=kind):
                if kind == 0:
                    total = part_one[hh, 0, y, x0].astype(F32)
                else:
                    total = part_one[hh, 1, y, :, :, z0].astype(F32)
                for step in ring_steps:
                    total += recv_one[hh, kind, near_peer(kind, step), y].reshape(
                        total.shape
                    ).astype(F32)
                total = total.astype(BF)
                for item in range(4):
                    part_two[hh, kind, item, y] = total[:, item] if kind == 0 else total[item]
                return carry

            lax.fori_loop(0, 4, add_turn, 0)
            for step in ring_steps:
                two_copy(hh, kind, far_peer(kind, step), far_place[kind]).start()

    def reduce_end(hh):
        for kind in range(2):
            for step in ring_steps:
                peer = far_peer(kind, step)
                two_copy(hh, kind, peer, peer).wait_recv()
            total = part_two[hh, kind, far_place[kind]].astype(F32)
            for step in ring_steps:
                total += recv_two[hh, kind, far_peer(kind, step)].astype(F32)
            for y in range(4):
                for c in range(2):
                    dkv_sum[hh, 2 * y + c, kind] = total[y, c]
        for step in group_steps:
            dkv_copy(hh, group_peer(step), j0).start()

    for hh in range(2):
        if hh == 0:
            gather_forward(1)
        gather_wait(hh)
        for y in range(4):
            kt_h[y] = tile_of(hh, 0, y).T
            vt_h[y] = tile_of(hh, 1, y).T
        own_in[hh][0].wait()
        own_in[hh][1].wait()

        def member_turn(i, carry, hh=hh):
            if hh == 1:

                @pl.when(i == 2)
                def _():
                    reduce_middle(0)

            turn = i if hh == 0 else 3 - i
            dy = turn + lax.div(turn, 2) * (5 - 2 * turn)
            y = lax.rem(y0 + dy, 4)
            for c in range(2):
                pair = 2 * y + c

                @pl.when(pair != j0)
                def _(pair=pair):
                    q_copy(hh, pair, pair).wait_recv()
                    g_copy(hh, pair, pair).wait_recv()
                    if hh == 0:
                        st_copy(pair, pair).wait_recv()

            attend(hh, y)
            for c in range(2):
                pair = 2 * y + c

                @pl.when(pair != j0)
                def _(pair=pair):
                    if hh == 1:
                        sb_copy(pair, j0).start()
                    o_copy(hh, pair, j0).start()
                    dq_copy(hh, pair, j0).start()

            return carry

        lax.fori_loop(0, 4, member_turn, 0)
        reduce_start(hh)

    def pair_at(t):
        turn = 3 - lax.div(t, 2)
        dy = turn + lax.div(turn, 2) * (5 - 2 * turn)
        return lax.rem(y0 + dy, 4) * 2 + lax.rem(c0 + 1 + lax.rem(t, 2), 2)

    def own_turn(t, carry):
        pair = pair_at(t)

        @pl.when(pair != j0)
        def _():
            sb_copy(pair, pair).wait_recv()

        @pl.when(pair == j0)
        def _():
            st_in[pair] = st_back[pair]

        for hh in range(2):
            cols = head_cols(pair, hh)
            for r in range(2):
                rows = slice(r * BLOCK, (r + 1) * BLOCK)
                lse = st_in[pair, hh : hh + 1, rows]
                delta = st_in[pair, hh + 2 : hh + 3, rows]
                high = st_send[pair, 3 * hh : 3 * hh + 1, rows]
                probs = own_e[pair, 2 * hh + r] * jnp.exp2(high * C2 - lse)
                probs_b = probs.astype(BF)
                dscore = (probs * (own_dp[pair, 2 * hh + r] - delta)).astype(BF)
                own_o[rows, cols] = dot(probs_b, v_v[rows, cols], TN)
                own_dq[rows, cols] = dot(dscore, k_v[rows, cols], TN) * SCALE
                grad_k = dot(dscore, q_v[rows, cols], NN) * SCALE
                gk_v[rows, cols] = grad_k.astype(BF)
                last_rows[0, r, :, cols] = grad_k[BLOCK - 16 :]
                grad_v = dot(probs_b, g_v[rows, cols], NN)
                gv_v[rows, cols] = grad_v.astype(BF)
                last_rows[1, r, :, cols] = grad_v[BLOCK - 16 :]
        return carry

    def out_copies(pair):
        cols = cols_of(pair)
        return (
            pltpu.make_async_copy(out_v.at[:, cols], out_hbm.at[:, cols], out_sem.at[0, pair]),
            pltpu.make_async_copy(gq_v.at[:, cols], gq_hbm.at[:, cols], out_sem.at[1, pair]),
        )

    def sum_turn(t, carry):
        pair = pair_at(t)

        @pl.when(pair != j0)
        def _():
            for hh in range(2):
                o_copy(hh, pair, pair).wait_recv()
                dq_copy(hh, pair, pair).wait_recv()

        @pl.when(pair == j0)
        def _():
            for hh in range(2):
                o_in[hh, pair] = o_buf[hh, pair]
                dq_in[hh, pair] = dq_buf[hh, pair]

        for hh in range(2):
            cols = head_cols(pair, hh)
            out_v[:, cols] = (own_o[:, cols] + o_in[hh, pair].astype(F32)).astype(BF)
            gq_v[:, cols] = (own_dq[:, cols] + dq_in[hh, pair].astype(F32)).astype(BF)
        for copy in out_copies(pair):
            copy.start()
        return carry

    reduce_end(0)
    lax.fori_loop(0, 4, own_turn, 0)
    reduce_middle(1)
    lax.fori_loop(4, 8, own_turn, 0)
    lax.fori_loop(0, 2, sum_turn, 0)
    reduce_end(1)
    lax.fori_loop(2, 8, sum_turn, 0)

    def last_turn(t, carry):
        pair = pair_at(t)

        @pl.when(pair != j0)
        def _():
            dkv_copy(0, pair, pair).wait_recv()
            dkv_copy(1, pair, pair).wait_recv()

        @pl.when(pair == j0)
        def _():
            for hh in range(2):
                dkv_in[hh, pair] = dkv_sum[hh, pair]

        for hh in range(2):
            cols = head_cols(pair, hh)
            for kind, dst in enumerate((gk_v, gv_v)):
                for r in range(2):
                    part = dkv_in[hh, pair, kind, r * SUMMARY : (r + 1) * SUMMARY, :]
                    part = jnp.concatenate([jnp.zeros_like(part), part], axis=0)
                    rows = slice((r + 1) * BLOCK - 16, (r + 1) * BLOCK)
                    dst[rows, cols] = (last_rows[kind, r, :, cols] + part).astype(BF)
        return carry

    lax.fori_loop(0, 8, last_turn, 0)
    last_out = (
        pltpu.make_async_copy(gk_v, gk_hbm, load_sem.at[0]),
        pltpu.make_async_copy(gv_v, gv_hbm, load_sem.at[1]),
    )
    for copy in last_out:
        copy.start()

    for step in group_steps:
        pair = group_peer(step)
        kv_copy(pair, j0).wait_send()
        st_copy(pair, j0).wait_send()
        sb_copy(pair, j0).wait_send()
        for hh in range(2):
            for copy in (q_copy, g_copy, o_copy, dq_copy, dkv_copy):
                copy(hh, pair, j0).wait_send()
    for hh in range(2):
        for kind in range(2):
            for step in ring_steps:
                peer = near_peer(kind, step)
                near_copy(hh, kind, peer, near_place[kind]).wait_send()
                one_copy(hh, kind, peer, near_place[kind]).wait_send()
                peer = far_peer(kind, step)
                two_copy(hh, kind, peer, far_place[kind]).wait_send()
                for hop in (0,) + ring_steps:
                    item = near_peer(kind, hop)
                    far_copy(hh, kind, item, peer, far_place[kind]).wait_send()
    for copy in last_out:
        copy.wait()

    def out_wait(pair, carry):
        for copy in out_copies(pair):
            copy.wait()
        return carry

    lax.fori_loop(0, 8, out_wait, 0)


def exchange(queries, keys_in, values_in, cotangent):
    any_spec = pl.BlockSpec(memory_space=pl.ANY)
    dma = pltpu.SemaphoreType.DMA
    return pl.pallas_call(
        exchange_kernel,
        out_shape=(jax.ShapeDtypeStruct((ROWS, WIDTH), BF),) * 4,
        in_specs=[any_spec] * 4,
        out_specs=(any_spec,) * 4,
        scratch_shapes=[
            pltpu.VMEM((ROWS, WIDTH), BF),
            pltpu.VMEM((ROWS, WIDTH), BF),
            pltpu.VMEM((ROWS, WIDTH), BF),
            pltpu.VMEM((ROWS, WIDTH), BF),
            pltpu.VMEM((8, 2, 2, 16, HEAD_DIM), BF),
            pltpu.VMEM((2, 8, ROWS, HEAD_DIM), BF),
            pltpu.VMEM((2, 8, ROWS, HEAD_DIM), BF),
            pltpu.VMEM((2, 2, 4, 4, 2, 4, 16, HEAD_DIM), BF),
            pltpu.VMEM((4, HEAD_DIM, TILE), BF),
            pltpu.VMEM((4, HEAD_DIM, TILE), BF),
            pltpu.VMEM((HEAD_DIM, 2 * ROWS), BF),
            pltpu.VMEM((HEAD_DIM, 2 * ROWS), BF),
            pltpu.VMEM((4, TILE, 2 * ROWS), F32),
            pltpu.VMEM((HEAD_DIM, 2 * ROWS), F32),
            pltpu.VMEM((2, 2, 4 * TILE, HEAD_DIM), F32),
            pltpu.VMEM((2, 2, 4, 4, 2, 4, 16, HEAD_DIM), BF),
            pltpu.VMEM((2, 2, 4, 4, 8, 16, HEAD_DIM), BF),
            pltpu.VMEM((2, 2, 4, 4, 2, 16, HEAD_DIM), BF),
            pltpu.VMEM((2, 2, 4, 4, 2, 16, HEAD_DIM), BF),
            pltpu.VMEM((2, 8, ROWS, HEAD_DIM), BF),
            pltpu.VMEM((2, 8, ROWS, HEAD_DIM), BF),
            pltpu.VMEM((8, 8, ROWS), F32),
            pltpu.VMEM((8, 8, ROWS), F32),
            pltpu.VMEM((8, 8, ROWS), F32),
            pltpu.VMEM((2, 8, 2, 16, HEAD_DIM), F32),
            pltpu.VMEM((2, 8, ROWS, HEAD_DIM), BF),
            pltpu.VMEM((2, 8, ROWS, HEAD_DIM), BF),
            pltpu.VMEM((8, 8, ROWS), F32),
            pltpu.VMEM((2, 8, 2, 16, HEAD_DIM), F32),
            pltpu.VMEM((8, 4, BLOCK, BLOCK), F32),
            pltpu.VMEM((8, 4, BLOCK, BLOCK), F32),
            pltpu.VMEM((ROWS, WIDTH), F32),
            pltpu.VMEM((ROWS, WIDTH), F32),
            pltpu.VMEM((2, 2, 16, WIDTH), F32),
            pltpu.VMEM((ROWS, WIDTH), BF),
            pltpu.VMEM((ROWS, WIDTH), BF),
            pltpu.VMEM((ROWS, WIDTH), BF),
            pltpu.VMEM((ROWS, WIDTH), BF),
            dma((4,)),
            dma((8,)),
            dma((2, 8)),
        ]
        + [dma((8,))] * 2
        + [dma((2, 8))] * 4
        + [dma((8,))] * 2
        + [dma((2, 2, 4))] * 2
        + [dma((2, 2, 4, 4))] * 2
        + [dma((2, 8))] * 4
        + [dma((8,))] * 2
        + [dma((2, 2, 4))] * 4
        + [dma((2, 8))] * 2,
        compiler_params=pltpu.CompilerParams(
            collective_id=0, has_side_effects=True, vmem_limit_bytes=56 * 1024 * 1024
        ),
        name="exchange",
    )(queries, keys_in, values_in, cotangent)


def on_device(queries, keys_in, values_in, cotangent):
    return tuple(exchange(queries, keys_in, values_in, cotangent))


def solution(mesh):
    spec = P(("seq", "head"), None)
    return jax.shard_map(
        on_device,
        mesh=mesh,
        in_specs=(spec,) * 4,
        out_specs=(spec,) * 4,
        check_vma=False,
    )
```

```python
import math

import jax
import jax.numpy as jnp
from jax import lax
from jax.experimental import pallas as pl
from jax.experimental.pallas import tpu as pltpu
from jax.sharding import PartitionSpec as P

HEADS = 16
HEAD_DIM = 128
BLOCK = 128
SUMMARY = 8
WIDTH = 2048
ROWS = 256
PAIR = 256
NY, NX, NC, NZ = 4, 4, 2, 4
TILE = 512

MESH = pl.DeviceIdType.MESH
NEG = -1e30
LOG2E = 1.4426950408889634
SCALE = 1.0 / math.sqrt(HEAD_DIM)
C2 = SCALE * LOG2E
BF = jnp.bfloat16
F32 = jnp.float32

NT = (((1,), (1,)), ((), ()))
TN = (((0,), (0,)), ((), ()))
NN = (((1,), (0,)), ((), ()))


def dot(a, b, dims):
    return lax.dot_general(a, b, dims, preferred_element_type=F32)


def cols_of(pair):
    return pl.ds(pl.multiple_of(pair * PAIR, PAIR), PAIR)


def exchange_kernel(
    q_hbm, k_hbm, v_hbm, g_hbm,
    out_hbm, gq_hbm, gk_hbm, gv_hbm,
    q_v, k_v, v_v, g_v,
    kv_pack, q_all, g_all, kv_all, kt_h, vt_h,
    q_t, g_t, score, grad_kv,
    part_one, recv_one, part_two, recv_two,
    o_buf, dq_buf, st_send, st_all, st_back, dkv_sum,
    o_in, dq_in, st_in, dkv_in,
    own_e, own_dp, own_o, own_dq, last_rows, out_v, gq_v, gk_v, gv_v,
    load_sem, own_sem, out_sem,
    kv_ss, kv_rs, q_ss, q_rs, g_ss, g_rs, st_ss, st_rs,
    near_ss, near_rs, far_ss, far_rs,
    o_ss, o_rs, dq_ss, dq_rs, sb_ss, sb_rs,
    one_ss, one_rs, two_ss, two_rs, dkv_ss, dkv_rs,
):
    s = lax.axis_index("seq")
    z0 = lax.axis_index("head")
    y0 = lax.div(s, 8)
    x0 = lax.rem(lax.div(s, 2), 4)
    c0 = lax.rem(s, 2)
    j0 = y0 * 2 + c0

    def member_id(pair):
        return (lax.div(pair, 2) * 8 + x0 * 2 + lax.rem(pair, 2), z0)

    def x_id(xt):
        return (y0 * 8 + xt * 2 + c0, z0)

    def z_id(zt):
        return (s, zt)

    def group_peer(step):
        yt = lax.rem(y0 + step // 2, 4)
        ct = lax.rem(c0 + step % 2, 2)
        return yt * 2 + ct

    group_steps = (1, 2, 3, 6, 7, 4, 5)
    ring_steps = (1, 3, 2)

    def head_cols(pair, hh):
        return pl.ds(pl.multiple_of(pair * PAIR + hh * HEAD_DIM, HEAD_DIM), HEAD_DIM)

    loads = [
        pltpu.make_async_copy(src, dst, load_sem.at[i])
        for i, (src, dst) in enumerate(((k_hbm, k_v), (v_hbm, v_v), (q_hbm, q_v), (g_hbm, g_v)))
    ]
    for load in loads:
        load.start()
    own_in = []
    for hh in range(2):
        own_in.append((
            pltpu.make_async_copy(
                q_hbm.at[:, head_cols(j0, hh)], q_all.at[hh, j0], own_sem.at[2 * hh]
            ),
            pltpu.make_async_copy(
                g_hbm.at[:, head_cols(j0, hh)], g_all.at[hh, j0], own_sem.at[2 * hh + 1]
            ),
        ))
        own_in[hh][0].start()
        own_in[hh][1].start()

    barrier = pltpu.get_barrier_semaphore()

    def greet(device):
        pl.semaphore_signal(barrier, inc=1, device_id=device, device_id_type=MESH)

    for step in range(1, 8):
        greet(member_id(group_peer(step)))
    for step in ring_steps:
        greet(x_id(lax.rem(x0 + step, 4)))
        greet(z_id(lax.rem(z0 + step, 4)))

    loads[0].wait()
    loads[1].wait()
    for i, src in enumerate((k_v, v_v)):
        for j in range(8):
            for hh in range(2):
                cols = slice(j * PAIR + hh * HEAD_DIM, j * PAIR + (hh + 1) * HEAD_DIM)
                top = src[112:128, cols].astype(F32)[8:, :]
                low = src[240:256, cols].astype(F32)[8:, :]
                kv_pack[j, hh, i] = jnp.concatenate([top, low], axis=0).astype(BF)
    own_kv = pltpu.make_async_copy(
        kv_pack.at[j0], kv_all.at[:, :, y0, x0, c0, z0], own_sem.at[4]
    )
    own_kv.start()
    pl.semaphore_wait(barrier, 13)

    def remote(src, dst, ssem, rsem, device):
        return pltpu.make_async_remote_copy(
            src_ref=src,
            dst_ref=dst,
            send_sem=ssem,
            recv_sem=rsem,
            device_id=device,
            device_id_type=MESH,
        )

    def kv_copy(pair, slot):
        dst = kv_all.at[:, :, lax.div(slot, 2), x0, lax.rem(slot, 2), z0]
        return remote(kv_pack.at[pair], dst, kv_ss.at[pair], kv_rs.at[slot], member_id(pair))

    def q_copy(hh, pair, slot):
        return remote(
            q_hbm.at[:, head_cols(pair, hh)], q_all.at[hh, slot],
            q_ss.at[hh, pair], q_rs.at[hh, slot], member_id(pair),
        )

    def g_copy(hh, pair, slot):
        return remote(
            g_hbm.at[:, head_cols(pair, hh)], g_all.at[hh, slot],
            g_ss.at[hh, pair], g_rs.at[hh, slot], member_id(pair),
        )

    def st_copy(pair, slot):
        return remote(
            st_send.at[pair], st_all.at[slot], st_ss.at[pair], st_rs.at[slot], member_id(pair)
        )

    def o_copy(hh, pair, slot):
        return remote(
            o_buf.at[hh, pair], o_in.at[hh, slot],
            o_ss.at[hh, pair], o_rs.at[hh, slot], member_id(pair),
        )

    def dq_copy(hh, pair, slot):
        return remote(
            dq_buf.at[hh, pair], dq_in.at[hh, slot],
            dq_ss.at[hh, pair], dq_rs.at[hh, slot], member_id(pair),
        )

    def sb_copy(pair, slot):
        return remote(
            st_back.at[pair], st_in.at[slot], sb_ss.at[pair], sb_rs.at[slot], member_id(pair)
        )

    def dkv_copy(hh, pair, slot):
        return remote(
            dkv_sum.at[hh, pair], dkv_in.at[hh, slot],
            dkv_ss.at[hh, pair], dkv_rs.at[hh, slot], member_id(pair),
        )

    def near_copy(hh, kind, peer, slot):
        if kind == 0:
            view, device = kv_all.at[hh, 0, :, slot, :, z0], x_id(peer)
        else:
            view, device = kv_all.at[hh, 1, :, x0, :, slot], z_id(peer)
        return remote(
            view, view, near_ss.at[hh, kind, peer], near_rs.at[hh, kind, slot], device
        )

    def far_copy(hh, kind, item, peer, slot):
        if kind == 0:
            view, device = kv_all.at[hh, 0, :, item, :, slot], z_id(peer)
        else:
            view, device = kv_all.at[hh, 1, :, slot, :, item], x_id(peer)
        return remote(
            view, view, far_ss.at[hh, kind, item, peer], far_rs.at[hh, kind, item, slot], device
        )

    def one_copy(hh, kind, peer, slot):
        if kind == 0:
            src, device = part_one.at[hh, 0, :, peer], x_id(peer)
            dst = recv_one.at[hh, 0, slot]
        else:
            src, device = part_one.at[hh, 1, :, :, :, peer], z_id(peer)
            dst = recv_one.at[hh, 1, slot]
        dst = dst.reshape(*src.shape)
        return remote(src, dst, one_ss.at[hh, kind, peer], one_rs.at[hh, kind, slot], device)

    def two_copy(hh, kind, peer, slot):
        device = z_id(peer) if kind == 0 else x_id(peer)
        return remote(
            part_two.at[hh, kind, peer], recv_two.at[hh, kind, slot],
            two_ss.at[hh, kind, peer], two_rs.at[hh, kind, slot], device,
        )

    near_place = (x0, z0)
    far_place = (z0, x0)

    def near_peer(kind, step):
        return lax.rem(near_place[kind] + step, 4)

    def far_peer(kind, step):
        return lax.rem(far_place[kind] + step, 4)

    for step in group_steps:
        kv_copy(group_peer(step), j0).start()
    for step in group_steps:
        q_copy(0, group_peer(step), j0).start()
        g_copy(0, group_peer(step), j0).start()

    own_kv.wait()
    for step in group_steps:
        kv_copy(group_peer(step), group_peer(step)).wait_recv()

    def gather_start(hh):
        for kind in range(2):
            for step in ring_steps:
                near_copy(hh, kind, near_peer(kind, step), near_place[kind]).start()
        for kind in range(2):
            for step in ring_steps:
                far_copy(
                    hh, kind, near_place[kind], far_peer(kind, step), far_place[kind]
                ).start()

    def gather_forward(hh):
        for step in ring_steps:
            for kind in range(2):
                item = near_peer(kind, step)
                near_copy(hh, kind, item, item).wait_recv()
                for hop in ring_steps:
                    far_copy(hh, kind, item, far_peer(kind, hop), far_place[kind]).start()

    def gather_wait(hh):
        for kind in range(2):
            for step in (0,) + ring_steps:
                item = near_peer(kind, step)
                for hop in ring_steps:
                    peer = far_peer(kind, hop)
                    far_copy(hh, kind, item, peer, peer).wait_recv()

    gather_start(0)

    loads[2].wait()
    loads[3].wait()
    key_pos = lax.broadcasted_iota(jnp.int32, (BLOCK, BLOCK), 0)
    query_pos = lax.broadcasted_iota(jnp.int32, (BLOCK, BLOCK), 1)
    causal = key_pos <= query_pos

    def local_turn(j, carry):
        for hh in range(2):
            cols = head_cols(j, hh)
            for r in range(2):
                rows = slice(r * BLOCK, (r + 1) * BLOCK)
                raw = dot(k_v[rows, cols], q_v[rows, cols], NT)
                raw = jnp.where(causal, raw, NEG)
                high = jnp.max(raw, axis=0, keepdims=True)
                weights = jnp.exp2((raw - high) * C2)
                dprob = dot(v_v[rows, cols], g_v[rows, cols], NT)
                own_e[j, 2 * hh + r] = weights
                own_dp[j, 2 * hh + r] = dprob
                st_send[j, 3 * hh : 3 * hh + 1, rows] = high
                st_send[j, 3 * hh + 1 : 3 * hh + 2, rows] = jnp.sum(weights, axis=0, keepdims=True)
                st_send[j, 3 * hh + 2 : 3 * hh + 3, rows] = jnp.sum(
                    weights * dprob, axis=0, keepdims=True
                )
        return carry

    st_send[...] = jnp.zeros_like(st_send)
    lax.fori_loop(0, 4, local_turn, 0)
    gather_forward(0)
    gather_start(1)
    lax.fori_loop(4, 8, local_turn, 0)
    own_st = pltpu.make_async_copy(st_send.at[j0], st_all.at[j0], own_sem.at[5])
    own_st.start()
    for step in group_steps:
        st_copy(group_peer(step), j0).start()
    for step in group_steps:
        q_copy(1, group_peer(step), j0).start()
        g_copy(1, group_peer(step), j0).start()

    grad_kv[...] = jnp.zeros_like(grad_kv)
    st_back[...] = jnp.zeros_like(st_back)
    own_st.wait()

    lane = lax.broadcasted_iota(jnp.int32, (1, 2 * ROWS), 1)
    lane_limit = x0 * 128 + z0 * 16 + lax.div(lane, 256) * 64 + lax.rem(lax.div(lane, 128), 2) * 8
    key_row = lax.broadcasted_iota(jnp.int32, (TILE, 2 * ROWS), 0)

    def tile_of(hh, kind, kt):
        return kv_all[hh, kind, kt].reshape(TILE, HEAD_DIM)

    def attend(hh, y):
        q_rows = q_all[hh, 2 * y : 2 * y + 2].reshape(2 * ROWS, HEAD_DIM)
        g_rows = g_all[hh, 2 * y : 2 * y + 2].reshape(2 * ROWS, HEAD_DIM)
        q_t[...] = q_rows.T
        g_t[...] = g_rows.T

        def stat(kind):
            row = slice(hh * 3 + kind, hh * 3 + kind + 1)
            return jnp.concatenate([st_all[2 * y, row, :], st_all[2 * y + 1, row, :]], axis=1)

        local_high = stat(0)
        high = local_high
        for kt in range(y + 1):
            raw = dot(tile_of(hh, 0, kt), q_t[...], NN)
            if kt == y:
                raw = jnp.where(key_row < lane_limit, raw, NEG)
            score[kt] = raw
            high = jnp.maximum(high, jnp.max(raw, axis=0, keepdims=True))

        shrink = jnp.exp2((local_high - high) * C2)
        total = stat(1) * shrink
        out_t = jnp.zeros((HEAD_DIM, 2 * ROWS), F32)
        for kt in range(y + 1):
            weights = jnp.exp2((score[kt] - high) * C2)
            score[kt] = weights
            out_t = out_t + dot(vt_h[kt], weights.astype(BF), NN)
            total = total + jnp.sum(weights, axis=0, keepdims=True)

        inverse = 1.0 / total
        delta = (
            stat(2) * shrink + jnp.sum(out_t * g_t[...].astype(F32), axis=0, keepdims=True)
        ) * inverse
        lse = high * C2 + jnp.log(total) * LOG2E
        out = (out_t * inverse).T.astype(BF)
        for c in range(2):
            half = slice(c * ROWS, (c + 1) * ROWS)
            o_buf[hh, 2 * y + c] = out[half]
            st_back[2 * y + c, hh : hh + 1, :] = lse[:, half]
            st_back[2 * y + c, hh + 2 : hh + 3, :] = delta[:, half]

        grad_t = jnp.zeros((HEAD_DIM, 2 * ROWS), F32)
        for kt in range(y + 1):
            tile = slice(kt * TILE, (kt + 1) * TILE)
            probs = score[kt] * inverse
            dprob = dot(tile_of(hh, 1, kt), g_t[...], NN)
            dscore = (probs * (dprob - delta)).astype(BF)
            grad_t = grad_t + dot(kt_h[kt], dscore, NN)
            grad_kv[hh, 0, tile, :] += dot(dscore, q_rows, NN)
            grad_kv[hh, 1, tile, :] += dot(probs.astype(BF), g_rows, NN)
        grad_q = (grad_t * SCALE).T.astype(BF)
        for c in range(2):
            dq_buf[hh, 2 * y + c] = grad_q[c * ROWS : (c + 1) * ROWS]

    def reduce_start(hh):
        def cast_turn(y, carry):
            tile = pl.ds(pl.multiple_of(y * TILE, TILE), TILE)
            shape = (4, 2, 4, 16, HEAD_DIM)
            part_one[hh, 0, y] = (grad_kv[hh, 0, tile, :] * SCALE).astype(BF).reshape(shape)
            part_one[hh, 1, y] = grad_kv[hh, 1, tile, :].astype(BF).reshape(shape)
            return carry

        lax.fori_loop(0, 4, cast_turn, 0)
        for step in ring_steps:
            for kind in range(2):
                one_copy(hh, kind, near_peer(kind, step), near_place[kind]).start()

    def reduce_middle(hh):
        for kind in range(2):
            for step in ring_steps:
                peer = near_peer(kind, step)
                one_copy(hh, kind, peer, peer).wait_recv()
        for kind in range(2):

            def add_turn(y, carry, kind=kind):
                if kind == 0:
                    total = part_one[hh, 0, y, x0].astype(F32)
                else:
                    total = part_one[hh, 1, y, :, :, z0].astype(F32)
                for step in ring_steps:
                    total += recv_one[hh, kind, near_peer(kind, step), y].reshape(
                        total.shape
                    ).astype(F32)
                total = total.astype(BF)
                for item in range(4):
                    part_two[hh, kind, item, y] = total[:, item] if kind == 0 else total[item]
                return carry

            lax.fori_loop(0, 4, add_turn, 0)
            for step in ring_steps:
                two_copy(hh, kind, far_peer(kind, step), far_place[kind]).start()

    def reduce_end(hh):
        for kind in range(2):
            for step in ring_steps:
                peer = far_peer(kind, step)
                two_copy(hh, kind, peer, peer).wait_recv()
            total = part_two[hh, kind, far_place[kind]].astype(F32)
            for step in ring_steps:
                total += recv_two[hh, kind, far_peer(kind, step)].astype(F32)
            for y in range(4):
                for c in range(2):
                    dkv_sum[hh, 2 * y + c, kind] = total[y, c]
        for step in group_steps:
            dkv_copy(hh, group_peer(step), j0).start()

    for hh in range(2):
        if hh == 0:
            gather_forward(1)
        gather_wait(hh)
        for y in range(4):
            kt_h[y] = tile_of(hh, 0, y).T
            vt_h[y] = tile_of(hh, 1, y).T
        own_in[hh][0].wait()
        own_in[hh][1].wait()

        def member_turn(i, carry, hh=hh):
            if hh == 1:

                @pl.when(i == 2)
                def _():
                    reduce_middle(0)

            turn = i if hh == 0 else 3 - i
            dy = turn + lax.div(turn, 2) * (5 - 2 * turn)
            y = lax.rem(y0 + dy, 4)
            for c in range(2):
                pair = 2 * y + c

                @pl.when(pair != j0)
                def _(pair=pair):
                    q_copy(hh, pair, pair).wait_recv()
                    g_copy(hh, pair, pair).wait_recv()
                    if hh == 0:
                        st_copy(pair, pair).wait_recv()

            for row in range(4):

                @pl.when(y == row)
                def _(row=row):
                    attend(hh, row)

            for c in range(2):
                pair = 2 * y + c

                @pl.when(pair != j0)
                def _(pair=pair):
                    if hh == 1:
                        sb_copy(pair, j0).start()
                    o_copy(hh, pair, j0).start()
                    dq_copy(hh, pair, j0).start()

            return carry

        lax.fori_loop(0, 4, member_turn, 0)
        reduce_start(hh)

    def pair_at(t):
        turn = 3 - lax.div(t, 2)
        dy = turn + lax.div(turn, 2) * (5 - 2 * turn)
        return lax.rem(y0 + dy, 4) * 2 + lax.rem(c0 + 1 + lax.rem(t, 2), 2)

    def own_turn(t, carry):
        pair = pair_at(t)

        @pl.when(pair != j0)
        def _():
            sb_copy(pair, pair).wait_recv()

        @pl.when(pair == j0)
        def _():
            st_in[pair] = st_back[pair]

        for hh in range(2):
            cols = head_cols(pair, hh)
            for r in range(2):
                rows = slice(r * BLOCK, (r + 1) * BLOCK)
                lse = st_in[pair, hh : hh + 1, rows]
                delta = st_in[pair, hh + 2 : hh + 3, rows]
                high = st_send[pair, 3 * hh : 3 * hh + 1, rows]
                probs = own_e[pair, 2 * hh + r] * jnp.exp2(high * C2 - lse)
                probs_b = probs.astype(BF)
                dscore = (probs * (own_dp[pair, 2 * hh + r] - delta)).astype(BF)
                own_o[rows, cols] = dot(probs_b, v_v[rows, cols], TN)
                own_dq[rows, cols] = dot(dscore, k_v[rows, cols], TN) * SCALE
                grad_k = dot(dscore, q_v[rows, cols], NN) * SCALE
                gk_v[rows, cols] = grad_k.astype(BF)
                last_rows[0, r, :, cols] = grad_k[BLOCK - 16 :]
                grad_v = dot(probs_b, g_v[rows, cols], NN)
                gv_v[rows, cols] = grad_v.astype(BF)
                last_rows[1, r, :, cols] = grad_v[BLOCK - 16 :]
        return carry

    def out_copies(pair):
        cols = cols_of(pair)
        return (
            pltpu.make_async_copy(out_v.at[:, cols], out_hbm.at[:, cols], out_sem.at[0, pair]),
            pltpu.make_async_copy(gq_v.at[:, cols], gq_hbm.at[:, cols], out_sem.at[1, pair]),
        )

    def sum_turn(t, carry):
        pair = pair_at(t)

        @pl.when(pair != j0)
        def _():
            for hh in range(2):
                o_copy(hh, pair, pair).wait_recv()
                dq_copy(hh, pair, pair).wait_recv()

        @pl.when(pair == j0)
        def _():
            for hh in range(2):
                o_in[hh, pair] = o_buf[hh, pair]
                dq_in[hh, pair] = dq_buf[hh, pair]

        for hh in range(2):
            cols = head_cols(pair, hh)
            out_v[:, cols] = (own_o[:, cols] + o_in[hh, pair].astype(F32)).astype(BF)
            gq_v[:, cols] = (own_dq[:, cols] + dq_in[hh, pair].astype(F32)).astype(BF)
        for copy in out_copies(pair):
            copy.start()
        return carry

    reduce_end(0)
    lax.fori_loop(0, 4, own_turn, 0)
    reduce_middle(1)
    lax.fori_loop(4, 8, own_turn, 0)
    lax.fori_loop(0, 2, sum_turn, 0)
    reduce_end(1)
    lax.fori_loop(2, 8, sum_turn, 0)

    def last_turn(t, carry):
        pair = pair_at(t)

        @pl.when(pair != j0)
        def _():
            dkv_copy(0, pair, pair).wait_recv()
            dkv_copy(1, pair, pair).wait_recv()

        @pl.when(pair == j0)
        def _():
            for hh in range(2):
                dkv_in[hh, pair] = dkv_sum[hh, pair]

        for hh in range(2):
            cols = head_cols(pair, hh)
            for kind, dst in enumerate((gk_v, gv_v)):
                for r in range(2):
                    part = dkv_in[hh, pair, kind, r * SUMMARY : (r + 1) * SUMMARY, :]
                    part = jnp.concatenate([jnp.zeros_like(part), part], axis=0)
                    rows = slice((r + 1) * BLOCK - 16, (r + 1) * BLOCK)
                    dst[rows, cols] = (last_rows[kind, r, :, cols] + part).astype(BF)
        return carry

    lax.fori_loop(0, 8, last_turn, 0)
    last_out = (
        pltpu.make_async_copy(gk_v, gk_hbm, load_sem.at[0]),
        pltpu.make_async_copy(gv_v, gv_hbm, load_sem.at[1]),
    )
    for copy in last_out:
        copy.start()

    for step in group_steps:
        pair = group_peer(step)
        kv_copy(pair, j0).wait_send()
        st_copy(pair, j0).wait_send()
        sb_copy(pair, j0).wait_send()
        for hh in range(2):
            for copy in (q_copy, g_copy, o_copy, dq_copy, dkv_copy):
                copy(hh, pair, j0).wait_send()
    for hh in range(2):
        for kind in range(2):
            for step in ring_steps:
                peer = near_peer(kind, step)
                near_copy(hh, kind, peer, near_place[kind]).wait_send()
                one_copy(hh, kind, peer, near_place[kind]).wait_send()
                peer = far_peer(kind, step)
                two_copy(hh, kind, peer, far_place[kind]).wait_send()
                for hop in (0,) + ring_steps:
                    item = near_peer(kind, hop)
                    far_copy(hh, kind, item, peer, far_place[kind]).wait_send()
    for copy in last_out:
        copy.wait()

    def out_wait(pair, carry):
        for copy in out_copies(pair):
            copy.wait()
        return carry

    lax.fori_loop(0, 8, out_wait, 0)


def exchange(queries, keys_in, values_in, cotangent):
    any_spec = pl.BlockSpec(memory_space=pl.ANY)
    dma = pltpu.SemaphoreType.DMA
    return pl.pallas_call(
        exchange_kernel,
        out_shape=(jax.ShapeDtypeStruct((ROWS, WIDTH), BF),) * 4,
        in_specs=[any_spec] * 4,
        out_specs=(any_spec,) * 4,
        scratch_shapes=[
            pltpu.VMEM((ROWS, WIDTH), BF),
            pltpu.VMEM((ROWS, WIDTH), BF),
            pltpu.VMEM((ROWS, WIDTH), BF),
            pltpu.VMEM((ROWS, WIDTH), BF),
            pltpu.VMEM((8, 2, 2, 16, HEAD_DIM), BF),
            pltpu.VMEM((2, 8, ROWS, HEAD_DIM), BF),
            pltpu.VMEM((2, 8, ROWS, HEAD_DIM), BF),
            pltpu.VMEM((2, 2, 4, 4, 2, 4, 16, HEAD_DIM), BF),
            pltpu.VMEM((4, HEAD_DIM, TILE), BF),
            pltpu.VMEM((4, HEAD_DIM, TILE), BF),
            pltpu.VMEM((HEAD_DIM, 2 * ROWS), BF),
            pltpu.VMEM((HEAD_DIM, 2 * ROWS), BF),
            pltpu.VMEM((4, TILE, 2 * ROWS), F32),
            pltpu.VMEM((2, 2, 4 * TILE, HEAD_DIM), F32),
            pltpu.VMEM((2, 2, 4, 4, 2, 4, 16, HEAD_DIM), BF),
            pltpu.VMEM((2, 2, 4, 4, 8, 16, HEAD_DIM), BF),
            pltpu.VMEM((2, 2, 4, 4, 2, 16, HEAD_DIM), BF),
            pltpu.VMEM((2, 2, 4, 4, 2, 16, HEAD_DIM), BF),
            pltpu.VMEM((2, 8, ROWS, HEAD_DIM), BF),
            pltpu.VMEM((2, 8, ROWS, HEAD_DIM), BF),
            pltpu.VMEM((8, 8, ROWS), F32),
            pltpu.VMEM((8, 8, ROWS), F32),
            pltpu.VMEM((8, 8, ROWS), F32),
            pltpu.VMEM((2, 8, 2, 16, HEAD_DIM), F32),
            pltpu.VMEM((2, 8, ROWS, HEAD_DIM), BF),
            pltpu.VMEM((2, 8, ROWS, HEAD_DIM), BF),
            pltpu.VMEM((8, 8, ROWS), F32),
            pltpu.VMEM((2, 8, 2, 16, HEAD_DIM), F32),
            pltpu.VMEM((8, 4, BLOCK, BLOCK), F32),
            pltpu.VMEM((8, 4, BLOCK, BLOCK), F32),
            pltpu.VMEM((ROWS, WIDTH), F32),
            pltpu.VMEM((ROWS, WIDTH), F32),
            pltpu.VMEM((2, 2, 16, WIDTH), F32),
            pltpu.VMEM((ROWS, WIDTH), BF),
            pltpu.VMEM((ROWS, WIDTH), BF),
            pltpu.VMEM((ROWS, WIDTH), BF),
            pltpu.VMEM((ROWS, WIDTH), BF),
            dma((4,)),
            dma((8,)),
            dma((2, 8)),
        ]
        + [dma((8,))] * 2
        + [dma((2, 8))] * 4
        + [dma((8,))] * 2
        + [dma((2, 2, 4))] * 2
        + [dma((2, 2, 4, 4))] * 2
        + [dma((2, 8))] * 4
        + [dma((8,))] * 2
        + [dma((2, 2, 4))] * 4
        + [dma((2, 8))] * 2,
        compiler_params=pltpu.CompilerParams(
            collective_id=0, has_side_effects=True, vmem_limit_bytes=48 * 1024 * 1024
        ),
        name="exchange",
    )(queries, keys_in, values_in, cotangent)


def on_device(queries, keys_in, values_in, cotangent):
    return tuple(exchange(queries, keys_in, values_in, cotangent))


def solution(mesh):
    spec = P(("seq", "head"), None)
    return jax.shard_map(
        on_device,
        mesh=mesh,
        in_specs=(spec,) * 4,
        out_specs=(spec,) * 4,
        check_vma=False,
    )
```

```python
import functools
import math

import jax
import jax.numpy as jnp
from jax import lax
from jax.experimental import pallas as pl
from jax.experimental.pallas import tpu as pltpu
from jax.sharding import PartitionSpec as P

HEADS = 16
HEAD_DIM = 128
BLOCK = 128
SUMMARY = 8
WIDTH = 2048
ROWS = 256
PAIR = 256
NY, NX, NC, NZ = 4, 4, 2, 4
TILE = 512

MESH = pl.DeviceIdType.MESH
NEG = -1e30
LOG2E = 1.4426950408889634
SCALE = 1.0 / math.sqrt(HEAD_DIM)
C2 = SCALE * LOG2E
BF = jnp.bfloat16
F32 = jnp.float32

NT = (((1,), (1,)), ((), ()))
TN = (((0,), (0,)), ((), ()))
NN = (((1,), (0,)), ((), ()))


def dot(a, b, dims):
    return lax.dot_general(a, b, dims, preferred_element_type=F32)


def cols_of(pair):
    return pl.ds(pl.multiple_of(pair * PAIR, PAIR), PAIR)


def exchange_kernel(
    q_hbm, k_hbm, v_hbm, g_hbm,
    out_v, gq_v, gk_v, gv_v,
    q_v, k_v, v_v, g_v,
    kv_edge, kv_pack, q_all, g_all, kv_all, kt_h, vt_h,
    q_t, g_t, score, row_stat, grad_q_t, grad_kv,
    part_one, recv_one, part_two, recv_two,
    o_buf, dq_buf, st_send, st_all, st_back, dkv_sum,
    o_in, dq_in, st_in, dkv_in,
    own_e, own_dp, own_o, own_dq, last_rows,
    load_sem, edge_sem, own_sem,
    kv_ss, kv_rs, q_ss, q_rs, g_ss, g_rs, st_ss, st_rs,
    near_ss, near_rs, far_ss, far_rs,
    o_ss, o_rs, dq_ss, dq_rs, sb_ss, sb_rs,
    one_ss, one_rs, two_ss, two_rs, dkv_ss, dkv_rs,
):
    s = lax.axis_index("seq")
    z0 = lax.axis_index("head")
    y0 = lax.div(s, 8)
    x0 = lax.rem(lax.div(s, 2), 4)
    c0 = lax.rem(s, 2)
    j0 = y0 * 2 + c0

    def member_id(pair):
        return (lax.div(pair, 2) * 8 + x0 * 2 + lax.rem(pair, 2), z0)

    def x_id(xt):
        return (y0 * 8 + xt * 2 + c0, z0)

    def z_id(zt):
        return (s, zt)

    def group_peer(step):
        yt = lax.rem(y0 + step // 2, 4)
        ct = lax.rem(c0 + step % 2, 2)
        return yt * 2 + ct

    group_steps = (1, 2, 3, 6, 7, 4, 5)
    ring_steps = (1, 3, 2)
    gather_parts = (((0, 4),), ((0, 4),))
    reduce_parts = (((0, 4),), ((0, 1), (1, 1), (2, 1), (3, 1)))

    def head_cols(pair, hh):
        return pl.ds(pl.multiple_of(pair * PAIR + hh * HEAD_DIM, HEAD_DIM), HEAD_DIM)

    loads = [
        pltpu.make_async_copy(src, dst, load_sem.at[i])
        for i, (src, dst) in enumerate(((k_hbm, k_v), (v_hbm, v_v), (q_hbm, q_v), (g_hbm, g_v)))
    ]
    edges = [
        pltpu.make_async_copy(
            src.at[pl.ds(r * BLOCK + BLOCK - 16, 16)], kv_edge.at[i, r], edge_sem.at[i, r]
        )
        for i, src in enumerate((k_hbm, v_hbm))
        for r in range(2)
    ]
    for edge in edges:
        edge.start()
    own_in = []
    for hh in range(2):
        own_in.append((
            pltpu.make_async_copy(
                q_hbm.at[:, head_cols(j0, hh)], q_all.at[hh, j0], own_sem.at[2 * hh]
            ),
            pltpu.make_async_copy(
                g_hbm.at[:, head_cols(j0, hh)], g_all.at[hh, j0], own_sem.at[2 * hh + 1]
            ),
        ))

    barrier = pltpu.get_barrier_semaphore()

    def greet(device):
        pl.semaphore_signal(barrier, inc=1, device_id=device, device_id_type=MESH)

    for step in range(1, 8):
        greet(member_id(group_peer(step)))
    for step in ring_steps:
        greet(x_id(lax.rem(x0 + step, 4)))
        greet(z_id(lax.rem(z0 + step, 4)))

    for edge in edges:
        edge.wait()
    for i in range(2):
        for j in range(8):
            for hh in range(2):
                cols = slice(j * PAIR + hh * HEAD_DIM, j * PAIR + (hh + 1) * HEAD_DIM)
                top = kv_edge[i, 0, :, cols].astype(F32)[8:, :]
                low = kv_edge[i, 1, :, cols].astype(F32)[8:, :]
                kv_pack[j, hh, i] = jnp.concatenate([top, low], axis=0).astype(BF)
    own_kv = pltpu.make_async_copy(
        kv_pack.at[j0], kv_all.at[:, :, y0, x0, c0, z0], own_sem.at[4]
    )
    own_kv.start()
    pl.semaphore_wait(barrier, 13)

    def remote(src, dst, ssem, rsem, device):
        return pltpu.make_async_remote_copy(
            src_ref=src,
            dst_ref=dst,
            send_sem=ssem,
            recv_sem=rsem,
            device_id=device,
            device_id_type=MESH,
        )

    def kv_copy(pair, slot):
        dst = kv_all.at[:, :, lax.div(slot, 2), x0, lax.rem(slot, 2), z0]
        return remote(kv_pack.at[pair], dst, kv_ss.at[pair], kv_rs.at[slot], member_id(pair))

    def q_copy(hh, pair, slot):
        return remote(
            q_hbm.at[:, head_cols(pair, hh)], q_all.at[hh, slot],
            q_ss.at[hh, pair], q_rs.at[hh, slot], member_id(pair),
        )

    def g_copy(hh, pair, slot):
        return remote(
            g_hbm.at[:, head_cols(pair, hh)], g_all.at[hh, slot],
            g_ss.at[hh, pair], g_rs.at[hh, slot], member_id(pair),
        )

    def st_copy(pair, slot):
        return remote(
            st_send.at[pair], st_all.at[slot], st_ss.at[pair], st_rs.at[slot], member_id(pair)
        )

    def o_copy(hh, pair, slot):
        return remote(
            o_buf.at[hh, pair], o_in.at[hh, slot],
            o_ss.at[hh, pair], o_rs.at[hh, slot], member_id(pair),
        )

    def dq_copy(hh, pair, slot):
        return remote(
            dq_buf.at[hh, pair], dq_in.at[hh, slot],
            dq_ss.at[hh, pair], dq_rs.at[hh, slot], member_id(pair),
        )

    def sb_copy(pair, slot):
        return remote(
            st_back.at[pair], st_in.at[slot], sb_ss.at[pair], sb_rs.at[slot], member_id(pair)
        )

    def dkv_copy(hh, pair, slot):
        return remote(
            dkv_sum.at[hh, pair], dkv_in.at[hh, slot],
            dkv_ss.at[hh, pair], dkv_rs.at[hh, slot], member_id(pair),
        )

    def near_copy(hh, part, kind, peer, slot):
        ys = pl.ds(*gather_parts[hh][part])
        if kind == 0:
            view, device = kv_all.at[hh, 0, ys, slot, :, z0], x_id(peer)
        else:
            view, device = kv_all.at[hh, 1, ys, x0, :, slot], z_id(peer)
        return remote(
            view, view,
            near_ss.at[hh, part, kind, peer], near_rs.at[hh, part, kind, slot], device,
        )

    def far_copy(hh, part, kind, item, peer, slot):
        ys = pl.ds(*gather_parts[hh][part])
        if kind == 0:
            view, device = kv_all.at[hh, 0, ys, item, :, slot], z_id(peer)
        else:
            view, device = kv_all.at[hh, 1, ys, slot, :, item], x_id(peer)
        return remote(
            view, view,
            far_ss.at[hh, part, kind, item, peer], far_rs.at[hh, part, kind, item, slot], device,
        )

    def one_copy(hh, part, kind, peer, slot):
        ys = pl.ds(*reduce_parts[hh][part])
        if kind == 0:
            src, device = part_one.at[hh, 0, ys, peer], x_id(peer)
        else:
            src, device = part_one.at[hh, 1, ys, :, :, peer], z_id(peer)
        dst = recv_one.at[hh, kind, slot, ys].reshape(*src.shape)
        return remote(
            src, dst, one_ss.at[hh, part, kind, peer], one_rs.at[hh, part, kind, slot], device
        )

    def two_copy(hh, part, kind, peer, slot):
        ys = pl.ds(*reduce_parts[hh][part])
        device = z_id(peer) if kind == 0 else x_id(peer)
        return remote(
            part_two.at[hh, kind, peer, ys], recv_two.at[hh, kind, slot, ys],
            two_ss.at[hh, part, kind, peer], two_rs.at[hh, part, kind, slot], device,
        )

    near_place = (x0, z0)
    far_place = (z0, x0)

    def near_peer(kind, step):
        return lax.rem(near_place[kind] + step, 4)

    def far_peer(kind, step):
        return lax.rem(far_place[kind] + step, 4)

    for step in group_steps:
        kv_copy(group_peer(step), j0).start()
    for step in group_steps:
        q_copy(0, group_peer(step), j0).start()
        g_copy(0, group_peer(step), j0).start()

    for load in loads:
        load.start()
    for hh in range(2):
        own_in[hh][0].start()
        own_in[hh][1].start()
    own_kv.wait()
    for step in group_steps:
        kv_copy(group_peer(step), group_peer(step)).wait_recv()

    def gather_start(hh, part):
        for kind in range(2):
            for step in ring_steps:
                near_copy(hh, part, kind, near_peer(kind, step), near_place[kind]).start()
        for kind in range(2):
            for step in ring_steps:
                far_copy(
                    hh, part, kind, near_place[kind], far_peer(kind, step), far_place[kind]
                ).start()

    def gather_forward(hh, part):
        for step in ring_steps:
            for kind in range(2):
                item = near_peer(kind, step)
                near_copy(hh, part, kind, item, item).wait_recv()
                for hop in ring_steps:
                    far_copy(hh, part, kind, item, far_peer(kind, hop), far_place[kind]).start()

    def gather_wait(hh, part):
        for kind in range(2):
            for step in (0,) + ring_steps:
                item = near_peer(kind, step)
                for hop in ring_steps:
                    peer = far_peer(kind, hop)
                    far_copy(hh, part, kind, item, peer, peer).wait_recv()
        lo, count = gather_parts[hh][part]
        for y in range(lo, lo + count):
            kt_h[y] = tile_of(hh, 0, y).T
            vt_h[y] = tile_of(hh, 1, y).T

    gather_start(0, 0)

    for load in loads:
        load.wait()
    key_pos = lax.broadcasted_iota(jnp.int32, (BLOCK, BLOCK), 0)
    query_pos = lax.broadcasted_iota(jnp.int32, (BLOCK, BLOCK), 1)
    causal = key_pos <= query_pos

    def local_turn(j, carry):
        for hh in range(2):
            cols = head_cols(j, hh)
            for r in range(2):
                rows = slice(r * BLOCK, (r + 1) * BLOCK)
                raw = dot(k_v[rows, cols], q_v[rows, cols], NT)
                raw = jnp.where(causal, raw, NEG)
                high = jnp.max(raw, axis=0, keepdims=True)
                weights = jnp.exp2((raw - high) * C2)
                dprob = dot(v_v[rows, cols], g_v[rows, cols], NT)
                own_e[j, 2 * hh + r] = weights
                own_dp[j, 2 * hh + r] = dprob
                st_send[j, 3 * hh : 3 * hh + 1, rows] = high
                st_send[j, 3 * hh + 1 : 3 * hh + 2, rows] = jnp.sum(weights, axis=0, keepdims=True)
                st_send[j, 3 * hh + 2 : 3 * hh + 3, rows] = jnp.sum(
                    weights * dprob, axis=0, keepdims=True
                )
        return carry

    st_send[...] = jnp.zeros_like(st_send)
    lax.fori_loop(0, 8, local_turn, 0)
    own_st = pltpu.make_async_copy(st_send.at[j0], st_all.at[j0], own_sem.at[5])
    own_st.start()
    for step in group_steps:
        st_copy(group_peer(step), j0).start()
    for step in group_steps:
        q_copy(1, group_peer(step), j0).start()
        g_copy(1, group_peer(step), j0).start()

    grad_kv[...] = jnp.zeros_like(grad_kv)
    st_back[...] = jnp.zeros_like(st_back)
    gather_forward(0, 0)
    gather_start(1, 0)
    own_st.wait()

    lane = lax.broadcasted_iota(jnp.int32, (1, 2 * ROWS), 1)
    lane_limit = x0 * 128 + z0 * 16 + lax.div(lane, 256) * 64 + lax.rem(lax.div(lane, 128), 2) * 8
    key_row = lax.broadcasted_iota(jnp.int32, (TILE, 2 * ROWS), 0)

    def tile_of(hh, kind, kt):
        return kv_all[hh, kind, kt].reshape(TILE, HEAD_DIM)

    def place_of(y, kt):
        return y * (y + 1) // 2 + kt

    def group_rows(ref, hh, y):
        return ref[hh, 2 * y : 2 * y + 2].reshape(2 * ROWS, HEAD_DIM)

    def forward(hh, y):
        q_t[...] = group_rows(q_all, hh, y).T
        g_t[y] = group_rows(g_all, hh, y).T

        def stat(kind):
            row = slice(hh * 3 + kind, hh * 3 + kind + 1)
            return jnp.concatenate([st_all[2 * y, row, :], st_all[2 * y + 1, row, :]], axis=1)

        local_high = stat(0)
        high = local_high
        for kt in range(y + 1):
            raw = dot(tile_of(hh, 0, kt), q_t[...], NN)
            if kt == y:
                raw = jnp.where(key_row < lane_limit, raw, NEG)
            score[place_of(y, kt)] = raw
            high = jnp.maximum(high, jnp.max(raw, axis=0, keepdims=True))

        shrink = jnp.exp2((local_high - high) * C2)
        total = stat(1) * shrink
        out_t = jnp.zeros((HEAD_DIM, 2 * ROWS), F32)
        for kt in range(y + 1):
            weights = jnp.exp2((score[place_of(y, kt)] - high) * C2)
            score[place_of(y, kt)] = weights
            out_t = out_t + dot(vt_h[kt], weights.astype(BF), NN)
            total = total + jnp.sum(weights, axis=0, keepdims=True)

        inverse = 1.0 / total
        delta = (
            stat(2) * shrink + jnp.sum(out_t * g_t[y].astype(F32), axis=0, keepdims=True)
        ) * inverse
        lse = high * C2 + jnp.log(total) * LOG2E
        row_stat[y, 0:1, :] = inverse
        row_stat[y, 1:2, :] = delta
        out = (out_t * inverse).T.astype(BF)
        for c in range(2):
            half = slice(c * ROWS, (c + 1) * ROWS)
            o_buf[hh, 2 * y + c] = out[half]
            st_back[2 * y + c, hh : hh + 1, :] = lse[:, half]
            st_back[2 * y + c, hh + 2 : hh + 3, :] = delta[:, half]

    def grad_tile(hh, y, kt):
        tile = slice(kt * TILE, (kt + 1) * TILE)
        probs = score[place_of(y, kt)] * row_stat[y, 0:1, :]
        dprob = dot(tile_of(hh, 1, kt), g_t[y], NN)
        dscore = (probs * (dprob - row_stat[y, 1:2, :])).astype(BF)
        grad_kv[hh, 0, tile, :] += dot(dscore, group_rows(q_all, hh, y), NN)
        grad_kv[hh, 1, tile, :] += dot(probs.astype(BF), group_rows(g_all, hh, y), NN)
        return dot(kt_h[kt], dscore, NN)

    def put_grad(hh, y, grad_t):
        grad_q = (grad_t * SCALE).T.astype(BF)
        for c in range(2):
            dq_buf[hh, 2 * y + c] = grad_q[c * ROWS : (c + 1) * ROWS]

    def reduce_start(hh, part):
        lo, count = reduce_parts[hh][part]

        def cast_turn(y, carry):
            tile = pl.ds(pl.multiple_of(y * TILE, TILE), TILE)
            shape = (4, 2, 4, 16, HEAD_DIM)
            part_one[hh, 0, y] = (grad_kv[hh, 0, tile, :] * SCALE).astype(BF).reshape(shape)
            part_one[hh, 1, y] = grad_kv[hh, 1, tile, :].astype(BF).reshape(shape)
            return carry

        lax.fori_loop(lo, lo + count, cast_turn, 0)
        for step in ring_steps:
            for kind in range(2):
                one_copy(hh, part, kind, near_peer(kind, step), near_place[kind]).start()

    def reduce_middle(hh, part):
        lo, count = reduce_parts[hh][part]
        for kind in range(2):
            for step in ring_steps:
                peer = near_peer(kind, step)
                one_copy(hh, part, kind, peer, peer).wait_recv()
        for kind in range(2):

            def add_turn(y, carry, kind=kind):
                if kind == 0:
                    total = part_one[hh, 0, y, x0].astype(F32)
                else:
                    total = part_one[hh, 1, y, :, :, z0].astype(F32)
                for step in ring_steps:
                    total += recv_one[hh, kind, near_peer(kind, step), y].reshape(
                        total.shape
                    ).astype(F32)
                total = total.astype(BF)
                for item in range(4):
                    part_two[hh, kind, item, y] = total[:, item] if kind == 0 else total[item]
                return carry

            lax.fori_loop(lo, lo + count, add_turn, 0)
            for step in ring_steps:
                two_copy(hh, part, kind, far_peer(kind, step), far_place[kind]).start()

    def reduce_end(hh, part):
        lo, count = reduce_parts[hh][part]
        for kind in range(2):
            for step in ring_steps:
                peer = far_peer(kind, step)
                two_copy(hh, part, kind, peer, peer).wait_recv()
        for y in range(lo, lo + count):
            for kind in range(2):
                total = part_two[hh, kind, far_place[kind], y].astype(F32)
                for step in ring_steps:
                    total += recv_two[hh, kind, far_peer(kind, step), y].astype(F32)
                for c in range(2):
                    dkv_sum[hh, 2 * y + c, kind] = total[c]
            for c in range(2):
                pair = 2 * y + c

                @pl.when(pair != j0)
                def _(pair=pair):
                    dkv_copy(hh, pair, j0).start()

    def to_others(y, *starts):
        for c in range(2):
            pair = 2 * y + c

            @pl.when(pair != j0)
            def _(pair=pair):
                for start in starts:
                    start(pair)

    def member_turn(i, carry, hh):
        turn = i if hh == 0 else 3 - i
        dy = turn + lax.div(turn, 2) * (5 - 2 * turn)
        y = lax.rem(y0 + dy, 4)
        to_others(
            y,
            lambda pair: q_copy(hh, pair, pair).wait_recv(),
            lambda pair: g_copy(hh, pair, pair).wait_recv(),
        )
        if hh == 0:
            to_others(y, lambda pair: st_copy(pair, pair).wait_recv())
        for row in range(4):

            @pl.when(y == row)
            def _(row=row):
                forward(hh, row)
                if hh == 0:
                    grad_t = jnp.zeros((HEAD_DIM, 2 * ROWS), F32)
                    for kt in range(row + 1):
                        grad_t = grad_t + grad_tile(hh, row, kt)
                    put_grad(hh, row, grad_t)

        if hh == 1:
            to_others(y, lambda pair: sb_copy(pair, j0).start())
        to_others(y, lambda pair: o_copy(hh, pair, j0).start())
        if hh == 0:
            to_others(y, lambda pair: dq_copy(hh, pair, j0).start())

            @pl.when(i == 0)
            def _():
                gather_forward(1, 0)

        return carry

    own_in[0][0].wait()
    own_in[0][1].wait()
    gather_wait(0, 0)
    lax.fori_loop(0, 4, functools.partial(member_turn, hh=0), 0)
    reduce_start(0, 0)
    own_in[1][0].wait()
    own_in[1][1].wait()
    gather_wait(1, 0)
    lax.fori_loop(0, 4, functools.partial(member_turn, hh=1), 0)
    for kt in range(4):
        for y in range(kt, 4):
            part = grad_tile(1, y, kt)
            if kt == 0 and y > 0:
                grad_q_t[y] = part
            elif y > kt:
                grad_q_t[y] += part
            else:
                put_grad(1, y, part if kt == 0 else grad_q_t[y] + part)
                to_others(y, lambda pair: dq_copy(1, pair, j0).start())
        reduce_start(1, kt)
        if kt == 0:
            reduce_middle(0, 0)
        elif kt == 2:
            reduce_middle(1, 0)
            reduce_end(0, 0)
        elif kt == 3:
            reduce_middle(1, 1)

    def pair_at(t):
        turn = 3 - lax.div(t, 2)
        dy = turn + lax.div(turn, 2) * (5 - 2 * turn)
        return lax.rem(y0 + dy, 4) * 2 + lax.rem(c0 + 1 + lax.rem(t, 2), 2)

    def own_turn(t, carry):
        pair = pair_at(t)

        @pl.when(pair != j0)
        def _():
            sb_copy(pair, pair).wait_recv()

        @pl.when(pair == j0)
        def _():
            st_in[pair] = st_back[pair]

        for hh in range(2):
            cols = head_cols(pair, hh)
            for r in range(2):
                rows = slice(r * BLOCK, (r + 1) * BLOCK)
                lse = st_in[pair, hh : hh + 1, rows]
                delta = st_in[pair, hh + 2 : hh + 3, rows]
                high = st_send[pair, 3 * hh : 3 * hh + 1, rows]
                probs = own_e[pair, 2 * hh + r] * jnp.exp2(high * C2 - lse)
                probs_b = probs.astype(BF)
                dscore = (probs * (own_dp[pair, 2 * hh + r] - delta)).astype(BF)
                own_o[rows, cols] = dot(probs_b, v_v[rows, cols], TN)
                own_dq[rows, cols] = dot(dscore, k_v[rows, cols], TN) * SCALE
                grad_k = dot(dscore, q_v[rows, cols], NN) * SCALE
                gk_v[rows, cols] = grad_k.astype(BF)
                last_rows[0, r, :, cols] = grad_k[BLOCK - 16 :]
                grad_v = dot(probs_b, g_v[rows, cols], NN)
                gv_v[rows, cols] = grad_v.astype(BF)
                last_rows[1, r, :, cols] = grad_v[BLOCK - 16 :]
        return carry

    def sum_turn(t, carry):
        pair = pair_at(t)

        @pl.when(pair != j0)
        def _():
            for hh in range(2):
                o_copy(hh, pair, pair).wait_recv()
                dq_copy(hh, pair, pair).wait_recv()

        @pl.when(pair == j0)
        def _():
            for hh in range(2):
                o_in[hh, pair] = o_buf[hh, pair]
                dq_in[hh, pair] = dq_buf[hh, pair]

        for hh in range(2):
            cols = head_cols(pair, hh)
            out_v[:, cols] = (own_o[:, cols] + o_in[hh, pair].astype(F32)).astype(BF)
            gq_v[:, cols] = (own_dq[:, cols] + dq_in[hh, pair].astype(F32)).astype(BF)
        return carry

    lax.fori_loop(0, 3, own_turn, 0)
    reduce_middle(1, 2)
    reduce_end(1, 0)
    lax.fori_loop(3, 6, own_turn, 0)
    reduce_middle(1, 3)
    reduce_end(1, 1)
    reduce_end(1, 2)
    lax.fori_loop(6, 8, own_turn, 0)
    lax.fori_loop(0, 4, sum_turn, 0)
    reduce_end(1, 3)
    lax.fori_loop(4, 8, sum_turn, 0)

    def last_turn(t, carry):
        pair = pair_at(t)

        @pl.when(pair != j0)
        def _():
            dkv_copy(0, pair, pair).wait_recv()
            dkv_copy(1, pair, pair).wait_recv()

        @pl.when(pair == j0)
        def _():
            for hh in range(2):
                dkv_in[hh, pair] = dkv_sum[hh, pair]

        for hh in range(2):
            cols = head_cols(pair, hh)
            for kind, dst in enumerate((gk_v, gv_v)):
                for r in range(2):
                    part = dkv_in[hh, pair, kind, r * SUMMARY : (r + 1) * SUMMARY, :]
                    part = jnp.concatenate([jnp.zeros_like(part), part], axis=0)
                    rows = slice((r + 1) * BLOCK - 16, (r + 1) * BLOCK)
                    dst[rows, cols] = (last_rows[kind, r, :, cols] + part).astype(BF)
        return carry

    lax.fori_loop(0, 8, last_turn, 0)
    for step in group_steps:
        pair = group_peer(step)
        kv_copy(pair, j0).wait_send()
        st_copy(pair, j0).wait_send()
        sb_copy(pair, j0).wait_send()
        for hh in range(2):
            for copy in (q_copy, g_copy, o_copy, dq_copy, dkv_copy):
                copy(hh, pair, j0).wait_send()
    for hh in range(2):
        for kind in range(2):
            for step in ring_steps:
                near, far = near_peer(kind, step), far_peer(kind, step)
                for part in range(len(gather_parts[hh])):
                    near_copy(hh, part, kind, near, near_place[kind]).wait_send()
                    for hop in (0,) + ring_steps:
                        item = near_peer(kind, hop)
                        far_copy(hh, part, kind, item, far, far_place[kind]).wait_send()
                for part in range(len(reduce_parts[hh])):
                    one_copy(hh, part, kind, near, near_place[kind]).wait_send()
                    two_copy(hh, part, kind, far, far_place[kind]).wait_send()


def exchange(queries, keys_in, values_in, cotangent):
    hbm_spec = pl.BlockSpec(memory_space=pltpu.HBM)
    vmem_spec = pl.BlockSpec(memory_space=pltpu.VMEM)
    dma = pltpu.SemaphoreType.DMA
    return pl.pallas_call(
        exchange_kernel,
        out_shape=(jax.ShapeDtypeStruct((ROWS, WIDTH), BF),) * 4,
        in_specs=[hbm_spec] * 4,
        out_specs=(vmem_spec,) * 4,
        scratch_shapes=[
            pltpu.VMEM((ROWS, WIDTH), BF),
            pltpu.VMEM((ROWS, WIDTH), BF),
            pltpu.VMEM((ROWS, WIDTH), BF),
            pltpu.VMEM((ROWS, WIDTH), BF),
            pltpu.VMEM((2, 2, 16, WIDTH), BF),
            pltpu.VMEM((8, 2, 2, 16, HEAD_DIM), BF),
            pltpu.VMEM((2, 8, ROWS, HEAD_DIM), BF),
            pltpu.VMEM((2, 8, ROWS, HEAD_DIM), BF),
            pltpu.VMEM((2, 2, 4, 4, 2, 4, 16, HEAD_DIM), BF),
            pltpu.VMEM((4, HEAD_DIM, TILE), BF),
            pltpu.VMEM((4, HEAD_DIM, TILE), BF),
            pltpu.VMEM((HEAD_DIM, 2 * ROWS), BF),
            pltpu.VMEM((4, HEAD_DIM, 2 * ROWS), BF),
            pltpu.VMEM((10, TILE, 2 * ROWS), F32),
            pltpu.VMEM((4, 8, 2 * ROWS), F32),
            pltpu.VMEM((4, HEAD_DIM, 2 * ROWS), F32),
            pltpu.VMEM((2, 2, 4 * TILE, HEAD_DIM), F32),
            pltpu.VMEM((2, 2, 4, 4, 2, 4, 16, HEAD_DIM), BF),
            pltpu.VMEM((2, 2, 4, 4, 8, 16, HEAD_DIM), BF),
            pltpu.VMEM((2, 2, 4, 4, 2, 16, HEAD_DIM), BF),
            pltpu.VMEM((2, 2, 4, 4, 2, 16, HEAD_DIM), BF),
            pltpu.VMEM((2, 8, ROWS, HEAD_DIM), BF),
            pltpu.VMEM((2, 8, ROWS, HEAD_DIM), BF),
            pltpu.VMEM((8, 8, ROWS), F32),
            pltpu.VMEM((8, 8, ROWS), F32),
            pltpu.VMEM((8, 8, ROWS), F32),
            pltpu.VMEM((2, 8, 2, 16, HEAD_DIM), F32),
            pltpu.VMEM((2, 8, ROWS, HEAD_DIM), BF),
            pltpu.VMEM((2, 8, ROWS, HEAD_DIM), BF),
            pltpu.VMEM((8, 8, ROWS), F32),
            pltpu.VMEM((2, 8, 2, 16, HEAD_DIM), F32),
            pltpu.VMEM((8, 4, BLOCK, BLOCK), F32),
            pltpu.VMEM((8, 4, BLOCK, BLOCK), F32),
            pltpu.VMEM((ROWS, WIDTH), F32),
            pltpu.VMEM((ROWS, WIDTH), F32),
            pltpu.VMEM((2, 2, 16, WIDTH), F32),
            dma((4,)),
            dma((2, 2)),
            dma((8,)),
        ]
        + [dma((8,))] * 2
        + [dma((2, 8))] * 4
        + [dma((8,))] * 2
        + [dma((2, 1, 2, 4))] * 2
        + [dma((2, 1, 2, 4, 4))] * 2
        + [dma((2, 8))] * 4
        + [dma((8,))] * 2
        + [dma((2, 4, 2, 4))] * 4
        + [dma((2, 8))] * 2,
        compiler_params=pltpu.CompilerParams(
            collective_id=0, has_side_effects=True, vmem_limit_bytes=50 * 1024 * 1024
        ),
        name="exchange",
    )(queries, keys_in, values_in, cotangent)


def hand_over_kernel(a, b, c, d, w, x, y, z, sem):
    copies = [
        pltpu.make_async_copy(src, dst, sem.at[n])
        for n, (src, dst) in enumerate(((a, w), (b, x), (c, y), (d, z)))
    ]
    for copy in copies:
        copy.start()
    for copy in copies:
        copy.wait()


def hand_over(arrays):
    return pl.pallas_call(
        hand_over_kernel,
        out_shape=(jax.ShapeDtypeStruct((ROWS, WIDTH), BF),) * 4,
        in_specs=[pl.BlockSpec(memory_space=pltpu.VMEM)] * 4,
        out_specs=(pl.BlockSpec(memory_space=pltpu.HBM),) * 4,
        scratch_shapes=[pltpu.SemaphoreType.DMA((4,))],
        compiler_params=pltpu.CompilerParams(vmem_limit_bytes=8 * 1024 * 1024),
        name="hand_over",
    )(*arrays)


def on_device(queries, keys_in, values_in, cotangent):
    return tuple(hand_over(exchange(queries, keys_in, values_in, cotangent)))


def solution(mesh):
    spec = P(("seq", "head"), None)
    return jax.shard_map(
        on_device,
        mesh=mesh,
        in_specs=(spec,) * 4,
        out_specs=(spec,) * 4,
        check_vma=False,
    )
```

```python
import functools
import math

import jax
import jax.numpy as jnp
from jax import lax
from jax.experimental import pallas as pl
from jax.experimental.pallas import tpu as pltpu
from jax.sharding import PartitionSpec as P

HEADS = 16
HEAD_DIM = 128
BLOCK = 128
SUMMARY = 8
WIDTH = 2048
ROWS = 256
PAIR = 256
NY, NX, NC, NZ = 4, 4, 2, 4
TILE = 512

MESH = pl.DeviceIdType.MESH
NEG = -1e30
LOG2E = 1.4426950408889634
SCALE = 1.0 / math.sqrt(HEAD_DIM)
C2 = SCALE * LOG2E
BF = jnp.bfloat16
F32 = jnp.float32

NT = (((1,), (1,)), ((), ()))
TN = (((0,), (0,)), ((), ()))
NN = (((1,), (0,)), ((), ()))


def dot(a, b, dims):
    return lax.dot_general(a, b, dims, preferred_element_type=F32)


def cols_of(pair):
    return pl.ds(pl.multiple_of(pair * PAIR, PAIR), PAIR)


def exchange_kernel(
    q_hbm, k_hbm, v_hbm, g_hbm,
    out_v, gq_v, gk_v, gv_v,
    q_v, k_v, v_v, g_v,
    kv_edge, kv_pack, q_all, g_all, kv_all, kt_h, vt_h,
    q_t, g_t, score, row_stat, grad_q_t, grad_kv,
    part_one, recv_one, part_two, recv_two,
    o_buf, dq_buf, st_send, st_all, st_back, dkv_sum,
    o_in, dq_in, st_in, dkv_in,
    own_e, own_dp, own_o, own_dq, last_rows,
    load_sem, edge_sem, own_sem,
    kv_ss, kv_rs, q_ss, q_rs, g_ss, g_rs, st_ss, st_rs,
    near_ss, near_rs, far_ss, far_rs,
    o_ss, o_rs, dq_ss, dq_rs, sb_ss, sb_rs,
    one_ss, one_rs, two_ss, two_rs, dkv_ss, dkv_rs,
):
    s = lax.axis_index("seq")
    z0 = lax.axis_index("head")
    y0 = lax.div(s, 8)
    x0 = lax.rem(lax.div(s, 2), 4)
    c0 = lax.rem(s, 2)
    j0 = y0 * 2 + c0

    def member_id(pair):
        return (lax.div(pair, 2) * 8 + x0 * 2 + lax.rem(pair, 2), z0)

    def x_id(xt):
        return (y0 * 8 + xt * 2 + c0, z0)

    def z_id(zt):
        return (s, zt)

    def group_peer(step):
        yt = lax.rem(y0 + step // 2, 4)
        ct = lax.rem(c0 + step % 2, 2)
        return yt * 2 + ct

    group_steps = (1, 2, 3, 6, 7, 4, 5)
    ring_steps = (1, 3, 2)
    gather_parts = (((0, 4),), ((0, 4),))
    reduce_parts = (((0, 4),), ((0, 1), (1, 1), (2, 1), (3, 1)))

    def head_cols(pair, hh):
        return pl.ds(pl.multiple_of(pair * PAIR + hh * HEAD_DIM, HEAD_DIM), HEAD_DIM)

    loads = [
        pltpu.make_async_copy(src, dst, load_sem.at[i])
        for i, (src, dst) in enumerate(((k_hbm, k_v), (v_hbm, v_v), (q_hbm, q_v), (g_hbm, g_v)))
    ]
    edges = [
        pltpu.make_async_copy(
            src.at[pl.ds(r * BLOCK + BLOCK - 16, 16)], kv_edge.at[i, r], edge_sem.at[i, r]
        )
        for i, src in enumerate((k_hbm, v_hbm))
        for r in range(2)
    ]
    for edge in edges:
        edge.start()
    own_in = []
    for hh in range(2):
        own_in.append((
            pltpu.make_async_copy(
                q_hbm.at[:, head_cols(j0, hh)], q_all.at[hh, j0], own_sem.at[2 * hh]
            ),
            pltpu.make_async_copy(
                g_hbm.at[:, head_cols(j0, hh)], g_all.at[hh, j0], own_sem.at[2 * hh + 1]
            ),
        ))

    barrier = pltpu.get_barrier_semaphore()

    def greet(device):
        pl.semaphore_signal(barrier, inc=1, device_id=device, device_id_type=MESH)

    for step in range(1, 8):
        greet(member_id(group_peer(step)))
    for step in ring_steps:
        greet(x_id(lax.rem(x0 + step, 4)))
        greet(z_id(lax.rem(z0 + step, 4)))

    for edge in edges:
        edge.wait()
    for i in range(2):
        for j in range(8):
            for hh in range(2):
                cols = slice(j * PAIR + hh * HEAD_DIM, j * PAIR + (hh + 1) * HEAD_DIM)
                top = kv_edge[i, 0, :, cols].astype(F32)[8:, :]
                low = kv_edge[i, 1, :, cols].astype(F32)[8:, :]
                kv_pack[j, hh, i] = jnp.concatenate([top, low], axis=0).astype(BF)
    own_kv = pltpu.make_async_copy(
        kv_pack.at[j0], kv_all.at[:, :, y0, x0, c0, z0], own_sem.at[4]
    )
    own_kv.start()
    pl.semaphore_wait(barrier, 13)

    def remote(src, dst, ssem, rsem, device):
        return pltpu.make_async_remote_copy(
            src_ref=src,
            dst_ref=dst,
            send_sem=ssem,
            recv_sem=rsem,
            device_id=device,
            device_id_type=MESH,
        )

    def kv_copy(pair, slot):
        dst = kv_all.at[:, :, lax.div(slot, 2), x0, lax.rem(slot, 2), z0]
        return remote(kv_pack.at[pair], dst, kv_ss.at[pair], kv_rs.at[slot], member_id(pair))

    def q_copy(hh, pair, slot):
        return remote(
            q_hbm.at[:, head_cols(pair, hh)], q_all.at[hh, slot],
            q_ss.at[hh, pair], q_rs.at[hh, slot], member_id(pair),
        )

    def g_copy(hh, pair, slot):
        return remote(
            g_hbm.at[:, head_cols(pair, hh)], g_all.at[hh, slot],
            g_ss.at[hh, pair], g_rs.at[hh, slot], member_id(pair),
        )

    def st_copy(pair, slot):
        return remote(
            st_send.at[pair], st_all.at[slot], st_ss.at[pair], st_rs.at[slot], member_id(pair)
        )

    def o_copy(hh, pair, slot):
        return remote(
            o_buf.at[hh, pair], o_in.at[hh, slot],
            o_ss.at[hh, pair], o_rs.at[hh, slot], member_id(pair),
        )

    def dq_copy(hh, pair, slot):
        return remote(
            dq_buf.at[hh, pair], dq_in.at[hh, slot],
            dq_ss.at[hh, pair], dq_rs.at[hh, slot], member_id(pair),
        )

    def sb_copy(pair, slot):
        return remote(
            st_back.at[pair], st_in.at[slot], sb_ss.at[pair], sb_rs.at[slot], member_id(pair)
        )

    def dkv_copy(hh, pair, slot):
        return remote(
            dkv_sum.at[hh, pair], dkv_in.at[hh, slot],
            dkv_ss.at[hh, pair], dkv_rs.at[hh, slot], member_id(pair),
        )

    def near_copy(hh, part, kind, peer, slot):
        ys = pl.ds(*gather_parts[hh][part])
        if kind == 0:
            view, device = kv_all.at[hh, 0, ys, slot, :, z0], x_id(peer)
        else:
            view, device = kv_all.at[hh, 1, ys, x0, :, slot], z_id(peer)
        return remote(
            view, view,
            near_ss.at[hh, part, kind, peer], near_rs.at[hh, part, kind, slot], device,
        )

    def far_copy(hh, part, kind, item, peer, slot):
        ys = pl.ds(*gather_parts[hh][part])
        if kind == 0:
            view, device = kv_all.at[hh, 0, ys, item, :, slot], z_id(peer)
        else:
            view, device = kv_all.at[hh, 1, ys, slot, :, item], x_id(peer)
        return remote(
            view, view,
            far_ss.at[hh, part, kind, item, peer], far_rs.at[hh, part, kind, item, slot], device,
        )

    def one_copy(hh, part, kind, peer, slot):
        ys = pl.ds(*reduce_parts[hh][part])
        if kind == 0:
            src, device = part_one.at[hh, 0, ys, peer], x_id(peer)
        else:
            src, device = part_one.at[hh, 1, ys, :, :, peer], z_id(peer)
        dst = recv_one.at[hh, kind, slot, ys].reshape(*src.shape)
        return remote(
            src, dst, one_ss.at[hh, part, kind, peer], one_rs.at[hh, part, kind, slot], device
        )

    def two_copy(hh, part, kind, peer, slot):
        ys = pl.ds(*reduce_parts[hh][part])
        device = z_id(peer) if kind == 0 else x_id(peer)
        return remote(
            part_two.at[hh, kind, peer, ys], recv_two.at[hh, kind, slot, ys],
            two_ss.at[hh, part, kind, peer], two_rs.at[hh, part, kind, slot], device,
        )

    near_place = (x0, z0)
    far_place = (z0, x0)

    def near_peer(kind, step):
        return lax.rem(near_place[kind] + step, 4)

    def far_peer(kind, step):
        return lax.rem(far_place[kind] + step, 4)

    for step in group_steps:
        kv_copy(group_peer(step), j0).start()
    for step in group_steps:
        q_copy(0, group_peer(step), j0).start()
        g_copy(0, group_peer(step), j0).start()

    for load in loads:
        load.start()
    for hh in range(2):
        own_in[hh][0].start()
        own_in[hh][1].start()
    own_kv.wait()
    for step in group_steps:
        kv_copy(group_peer(step), group_peer(step)).wait_recv()

    def gather_start(hh, part):
        for kind in range(2):
            for step in ring_steps:
                near_copy(hh, part, kind, near_peer(kind, step), near_place[kind]).start()
        for kind in range(2):
            for step in ring_steps:
                far_copy(
                    hh, part, kind, near_place[kind], far_peer(kind, step), far_place[kind]
                ).start()

    def gather_forward(hh, part):
        for step in ring_steps:
            for kind in range(2):
                item = near_peer(kind, step)
                near_copy(hh, part, kind, item, item).wait_recv()
                for hop in ring_steps:
                    far_copy(hh, part, kind, item, far_peer(kind, hop), far_place[kind]).start()

    def gather_wait(hh, part):
        for kind in range(2):
            for step in (0,) + ring_steps:
                item = near_peer(kind, step)
                for hop in ring_steps:
                    peer = far_peer(kind, hop)
                    far_copy(hh, part, kind, item, peer, peer).wait_recv()
        lo, count = gather_parts[hh][part]
        for y in range(lo, lo + count):
            kt_h[y] = tile_of(hh, 0, y).T
            vt_h[y] = tile_of(hh, 1, y).T

    gather_start(0, 0)

    for load in loads:
        load.wait()
    key_pos = lax.broadcasted_iota(jnp.int32, (BLOCK, BLOCK), 0)
    query_pos = lax.broadcasted_iota(jnp.int32, (BLOCK, BLOCK), 1)
    causal = key_pos <= query_pos

    def local_turn(j, carry):
        for hh in range(2):
            cols = head_cols(j, hh)
            for r in range(2):
                rows = slice(r * BLOCK, (r + 1) * BLOCK)
                raw = dot(k_v[rows, cols], q_v[rows, cols], NT)
                raw = jnp.where(causal, raw, NEG)
                high = jnp.max(raw, axis=0, keepdims=True)
                weights = jnp.exp2((raw - high) * C2)
                dprob = dot(v_v[rows, cols], g_v[rows, cols], NT)
                own_e[j, 2 * hh + r] = weights
                own_dp[j, 2 * hh + r] = dprob
                st_send[j, 3 * hh : 3 * hh + 1, rows] = high
                st_send[j, 3 * hh + 1 : 3 * hh + 2, rows] = jnp.sum(weights, axis=0, keepdims=True)
                st_send[j, 3 * hh + 2 : 3 * hh + 3, rows] = jnp.sum(
                    weights * dprob, axis=0, keepdims=True
                )
        return carry

    st_send[...] = jnp.zeros_like(st_send)
    lax.fori_loop(0, 8, local_turn, 0)
    own_st = pltpu.make_async_copy(st_send.at[j0], st_all.at[j0], own_sem.at[5])
    own_st.start()
    for step in group_steps:
        st_copy(group_peer(step), j0).start()
    for step in group_steps:
        q_copy(1, group_peer(step), j0).start()
        g_copy(1, group_peer(step), j0).start()

    grad_kv[...] = jnp.zeros_like(grad_kv)
    st_back[...] = jnp.zeros_like(st_back)
    gather_forward(0, 0)
    gather_start(1, 0)
    own_st.wait()

    lane = lax.broadcasted_iota(jnp.int32, (1, 2 * ROWS), 1)
    lane_limit = x0 * 128 + z0 * 16 + lax.div(lane, 256) * 64 + lax.rem(lax.div(lane, 128), 2) * 8
    key_row = lax.broadcasted_iota(jnp.int32, (TILE, 2 * ROWS), 0)

    def tile_of(hh, kind, kt):
        return kv_all[hh, kind, kt].reshape(TILE, HEAD_DIM)

    def place_of(y, kt):
        return y * (y + 1) // 2 + kt

    def group_rows(ref, hh, y):
        return ref[hh, 2 * y : 2 * y + 2].reshape(2 * ROWS, HEAD_DIM)

    def forward(hh, y):
        q_t[...] = group_rows(q_all, hh, y).T
        g_t[y] = group_rows(g_all, hh, y).T

        def stat(kind):
            row = slice(hh * 3 + kind, hh * 3 + kind + 1)
            return jnp.concatenate([st_all[2 * y, row, :], st_all[2 * y + 1, row, :]], axis=1)

        local_high = stat(0)
        high = local_high
        for kt in range(y + 1):
            raw = dot(tile_of(hh, 0, kt), q_t[...], NN)
            if kt == y:
                raw = jnp.where(key_row < lane_limit, raw, NEG)
            score[place_of(y, kt)] = raw
            high = jnp.maximum(high, jnp.max(raw, axis=0, keepdims=True))

        shrink = jnp.exp2((local_high - high) * C2)
        total = stat(1) * shrink
        out_t = jnp.zeros((HEAD_DIM, 2 * ROWS), F32)
        for kt in range(y + 1):
            weights = jnp.exp2((score[place_of(y, kt)] - high) * C2)
            score[place_of(y, kt)] = weights
            out_t = out_t + dot(vt_h[kt], weights.astype(BF), NN)
            total = total + jnp.sum(weights, axis=0, keepdims=True)

        inverse = 1.0 / total
        delta = (
            stat(2) * shrink + jnp.sum(out_t * g_t[y].astype(F32), axis=0, keepdims=True)
        ) * inverse
        lse = high * C2 + jnp.log(total) * LOG2E
        row_stat[y, 0:1, :] = inverse
        row_stat[y, 1:2, :] = delta
        out = (out_t * inverse).T.astype(BF)
        for c in range(2):
            half = slice(c * ROWS, (c + 1) * ROWS)
            o_buf[hh, 2 * y + c] = out[half]
            st_back[2 * y + c, hh : hh + 1, :] = lse[:, half]
            st_back[2 * y + c, hh + 2 : hh + 3, :] = delta[:, half]

    def grad_tile(hh, y, kt):
        tile = slice(kt * TILE, (kt + 1) * TILE)
        probs = score[place_of(y, kt)] * row_stat[y, 0:1, :]
        dprob = dot(tile_of(hh, 1, kt), g_t[y], NN)
        dscore = (probs * (dprob - row_stat[y, 1:2, :])).astype(BF)
        grad_kv[hh, 0, tile, :] += dot(dscore, group_rows(q_all, hh, y), NN)
        grad_kv[hh, 1, tile, :] += dot(probs.astype(BF), group_rows(g_all, hh, y), NN)
        return dot(kt_h[kt], dscore, NN)

    def put_grad(hh, y, grad_t):
        grad_q = (grad_t * SCALE).T.astype(BF)
        for c in range(2):
            dq_buf[hh, 2 * y + c] = grad_q[c * ROWS : (c + 1) * ROWS]

    def reduce_start(hh, part):
        lo, count = reduce_parts[hh][part]

        def cast_turn(y, carry):
            tile = pl.ds(pl.multiple_of(y * TILE, TILE), TILE)
            shape = (4, 2, 4, 16, HEAD_DIM)
            part_one[hh, 0, y] = (grad_kv[hh, 0, tile, :] * SCALE).astype(BF).reshape(shape)
            part_one[hh, 1, y] = grad_kv[hh, 1, tile, :].astype(BF).reshape(shape)
            return carry

        lax.fori_loop(lo, lo + count, cast_turn, 0)
        for step in ring_steps:
            for kind in range(2):
                one_copy(hh, part, kind, near_peer(kind, step), near_place[kind]).start()

    def reduce_middle(hh, part):
        lo, count = reduce_parts[hh][part]
        for kind in range(2):
            for step in ring_steps:
                peer = near_peer(kind, step)
                one_copy(hh, part, kind, peer, peer).wait_recv()
        for kind in range(2):

            def add_turn(y, carry, kind=kind):
                if kind == 0:
                    total = part_one[hh, 0, y, x0].astype(F32)
                else:
                    total = part_one[hh, 1, y, :, :, z0].astype(F32)
                for step in ring_steps:
                    total += recv_one[hh, kind, near_peer(kind, step), y].reshape(
                        total.shape
                    ).astype(F32)
                total = total.astype(BF)
                for item in range(4):
                    part_two[hh, kind, item, y] = total[:, item] if kind == 0 else total[item]
                return carry

            lax.fori_loop(lo, lo + count, add_turn, 0)
            for step in ring_steps:
                two_copy(hh, part, kind, far_peer(kind, step), far_place[kind]).start()

    def reduce_end(hh, part):
        lo, count = reduce_parts[hh][part]
        for kind in range(2):
            for step in ring_steps:
                peer = far_peer(kind, step)
                two_copy(hh, part, kind, peer, peer).wait_recv()
        for y in range(lo, lo + count):
            for kind in range(2):
                total = part_two[hh, kind, far_place[kind], y].astype(F32)
                for step in ring_steps:
                    total += recv_two[hh, kind, far_peer(kind, step), y].astype(F32)
                for c in range(2):
                    dkv_sum[hh, 2 * y + c, kind] = total[c]
            for c in range(2):
                pair = 2 * y + c

                @pl.when(pair != j0)
                def _(pair=pair):
                    dkv_copy(hh, pair, j0).start()

    def to_others(y, *starts):
        for c in range(2):
            pair = 2 * y + c

            @pl.when(pair != j0)
            def _(pair=pair):
                for start in starts:
                    start(pair)

    def member_turn(i, carry, hh):
        turn = i if hh == 0 else 3 - i
        dy = turn + lax.div(turn, 2) * (5 - 2 * turn)
        y = lax.rem(y0 + dy, 4)
        to_others(
            y,
            lambda pair: q_copy(hh, pair, pair).wait_recv(),
            lambda pair: g_copy(hh, pair, pair).wait_recv(),
        )
        if hh == 0:
            to_others(y, lambda pair: st_copy(pair, pair).wait_recv())
        for row in range(4):

            @pl.when(y == row)
            def _(row=row):
                forward(hh, row)
                if hh == 0:
                    grad_t = jnp.zeros((HEAD_DIM, 2 * ROWS), F32)
                    for kt in range(row + 1):
                        grad_t = grad_t + grad_tile(hh, row, kt)
                    put_grad(hh, row, grad_t)

        if hh == 1:
            to_others(y, lambda pair: sb_copy(pair, j0).start())
        to_others(y, lambda pair: o_copy(hh, pair, j0).start())
        if hh == 0:
            to_others(y, lambda pair: dq_copy(hh, pair, j0).start())

            @pl.when(i == 0)
            def _():
                gather_forward(1, 0)

        return carry

    own_in[0][0].wait()
    own_in[0][1].wait()
    gather_wait(0, 0)
    lax.fori_loop(0, 4, functools.partial(member_turn, hh=0), 0)
    reduce_start(0, 0)
    own_in[1][0].wait()
    own_in[1][1].wait()
    gather_wait(1, 0)
    lax.fori_loop(0, 4, functools.partial(member_turn, hh=1), 0)
    for kt in range(4):
        for y in range(kt, 4):
            part = grad_tile(1, y, kt)
            if kt == 0 and y > 0:
                grad_q_t[y] = part
            elif y > kt:
                grad_q_t[y] += part
            else:
                put_grad(1, y, part if kt == 0 else grad_q_t[y] + part)
                to_others(y, lambda pair: dq_copy(1, pair, j0).start())
        reduce_start(1, kt)
        if kt == 0:
            reduce_middle(0, 0)
        elif kt == 2:
            reduce_middle(1, 0)
            reduce_end(0, 0)
        elif kt == 3:
            reduce_middle(1, 1)

    def pair_at(t):
        turn = 3 - lax.div(t, 2)
        dy = turn + lax.div(turn, 2) * (5 - 2 * turn)
        return lax.rem(y0 + dy, 4) * 2 + lax.rem(c0 + 1 + lax.rem(t, 2), 2)

    def own_turn(t, carry):
        pair = pair_at(t)

        @pl.when(pair != j0)
        def _():
            sb_copy(pair, pair).wait_recv()

        @pl.when(pair == j0)
        def _():
            st_in[pair] = st_back[pair]

        for hh in range(2):
            cols = head_cols(pair, hh)
            for r in range(2):
                rows = slice(r * BLOCK, (r + 1) * BLOCK)
                lse = st_in[pair, hh : hh + 1, rows]
                delta = st_in[pair, hh + 2 : hh + 3, rows]
                high = st_send[pair, 3 * hh : 3 * hh + 1, rows]
                probs = own_e[pair, 2 * hh + r] * jnp.exp2(high * C2 - lse)
                probs_b = probs.astype(BF)
                dscore = (probs * (own_dp[pair, 2 * hh + r] - delta)).astype(BF)
                own_o[rows, cols] = dot(probs_b, v_v[rows, cols], TN)
                own_dq[rows, cols] = dot(dscore, k_v[rows, cols], TN) * SCALE
                grad_k = dot(dscore, q_v[rows, cols], NN) * SCALE
                gk_v[rows, cols] = grad_k.astype(BF)
                last_rows[0, r, :, cols] = grad_k[BLOCK - 16 :]
                grad_v = dot(probs_b, g_v[rows, cols], NN)
                gv_v[rows, cols] = grad_v.astype(BF)
                last_rows[1, r, :, cols] = grad_v[BLOCK - 16 :]
        return carry

    def sum_turn(t, carry):
        pair = pair_at(t)

        @pl.when(pair != j0)
        def _():
            for hh in range(2):
                o_copy(hh, pair, pair).wait_recv()
                dq_copy(hh, pair, pair).wait_recv()

        @pl.when(pair == j0)
        def _():
            for hh in range(2):
                o_in[hh, pair] = o_buf[hh, pair]
                dq_in[hh, pair] = dq_buf[hh, pair]

        for hh in range(2):
            cols = head_cols(pair, hh)
            out_v[:, cols] = (own_o[:, cols] + o_in[hh, pair].astype(F32)).astype(BF)
            gq_v[:, cols] = (own_dq[:, cols] + dq_in[hh, pair].astype(F32)).astype(BF)
        return carry

    lax.fori_loop(0, 3, own_turn, 0)
    reduce_middle(1, 2)
    reduce_end(1, 0)
    lax.fori_loop(3, 6, own_turn, 0)
    reduce_middle(1, 3)
    reduce_end(1, 1)
    reduce_end(1, 2)
    lax.fori_loop(6, 8, own_turn, 0)
    lax.fori_loop(0, 4, sum_turn, 0)
    reduce_end(1, 3)
    lax.fori_loop(4, 8, sum_turn, 0)

    def last_turn(t, carry):
        pair = pair_at(t)

        @pl.when(pair != j0)
        def _():
            dkv_copy(0, pair, pair).wait_recv()
            dkv_copy(1, pair, pair).wait_recv()

        @pl.when(pair == j0)
        def _():
            for hh in range(2):
                dkv_in[hh, pair] = dkv_sum[hh, pair]

        for hh in range(2):
            cols = head_cols(pair, hh)
            for kind, dst in enumerate((gk_v, gv_v)):
                for r in range(2):
                    part = dkv_in[hh, pair, kind, r * SUMMARY : (r + 1) * SUMMARY, :]
                    part = jnp.concatenate([jnp.zeros_like(part), part], axis=0)
                    rows = slice((r + 1) * BLOCK - 16, (r + 1) * BLOCK)
                    dst[rows, cols] = (last_rows[kind, r, :, cols] + part).astype(BF)
        return carry

    lax.fori_loop(0, 8, last_turn, 0)
    for step in group_steps:
        pair = group_peer(step)
        kv_copy(pair, j0).wait_send()
        st_copy(pair, j0).wait_send()
        sb_copy(pair, j0).wait_send()
        for hh in range(2):
            for copy in (q_copy, g_copy, o_copy, dq_copy, dkv_copy):
                copy(hh, pair, j0).wait_send()
    for hh in range(2):
        for kind in range(2):
            for step in ring_steps:
                near, far = near_peer(kind, step), far_peer(kind, step)
                for part in range(len(gather_parts[hh])):
                    near_copy(hh, part, kind, near, near_place[kind]).wait_send()
                    for hop in (0,) + ring_steps:
                        item = near_peer(kind, hop)
                        far_copy(hh, part, kind, item, far, far_place[kind]).wait_send()
                for part in range(len(reduce_parts[hh])):
                    one_copy(hh, part, kind, near, near_place[kind]).wait_send()
                    two_copy(hh, part, kind, far, far_place[kind]).wait_send()


def exchange(queries, keys_in, values_in, cotangent):
    hbm_spec = pl.BlockSpec(memory_space=pltpu.HBM)
    vmem_spec = pl.BlockSpec(memory_space=pltpu.VMEM)
    dma = pltpu.SemaphoreType.DMA
    return pl.pallas_call(
        exchange_kernel,
        out_shape=(jax.ShapeDtypeStruct((ROWS, WIDTH), BF),) * 4,
        in_specs=[hbm_spec] * 4,
        out_specs=(vmem_spec,) * 4,
        scratch_shapes=[
            pltpu.VMEM((ROWS, WIDTH), BF),
            pltpu.VMEM((ROWS, WIDTH), BF),
            pltpu.VMEM((ROWS, WIDTH), BF),
            pltpu.VMEM((ROWS, WIDTH), BF),
            pltpu.VMEM((2, 2, 16, WIDTH), BF),
            pltpu.VMEM((8, 2, 2, 16, HEAD_DIM), BF),
            pltpu.VMEM((2, 8, ROWS, HEAD_DIM), BF),
            pltpu.VMEM((2, 8, ROWS, HEAD_DIM), BF),
            pltpu.VMEM((2, 2, 4, 4, 2, 4, 16, HEAD_DIM), BF),
            pltpu.VMEM((4, HEAD_DIM, TILE), BF),
            pltpu.VMEM((4, HEAD_DIM, TILE), BF),
            pltpu.VMEM((HEAD_DIM, 2 * ROWS), BF),
            pltpu.VMEM((4, HEAD_DIM, 2 * ROWS), BF),
            pltpu.VMEM((10, TILE, 2 * ROWS), F32),
            pltpu.VMEM((4, 8, 2 * ROWS), F32),
            pltpu.VMEM((4, HEAD_DIM, 2 * ROWS), F32),
            pltpu.VMEM((2, 2, 4 * TILE, HEAD_DIM), F32),
            pltpu.VMEM((2, 2, 4, 4, 2, 4, 16, HEAD_DIM), BF),
            pltpu.VMEM((2, 2, 4, 4, 8, 16, HEAD_DIM), BF),
            pltpu.VMEM((2, 2, 4, 4, 2, 16, HEAD_DIM), BF),
            pltpu.VMEM((2, 2, 4, 4, 2, 16, HEAD_DIM), BF),
            pltpu.VMEM((2, 8, ROWS, HEAD_DIM), BF),
            pltpu.VMEM((2, 8, ROWS, HEAD_DIM), BF),
            pltpu.VMEM((8, 8, ROWS), F32),
            pltpu.VMEM((8, 8, ROWS), F32),
            pltpu.VMEM((8, 8, ROWS), F32),
            pltpu.VMEM((2, 8, 2, 16, HEAD_DIM), F32),
            pltpu.VMEM((2, 8, ROWS, HEAD_DIM), BF),
            pltpu.VMEM((2, 8, ROWS, HEAD_DIM), BF),
            pltpu.VMEM((8, 8, ROWS), F32),
            pltpu.VMEM((2, 8, 2, 16, HEAD_DIM), F32),
            pltpu.VMEM((8, 4, BLOCK, BLOCK), F32),
            pltpu.VMEM((8, 4, BLOCK, BLOCK), F32),
            pltpu.VMEM((ROWS, WIDTH), F32),
            pltpu.VMEM((ROWS, WIDTH), F32),
            pltpu.VMEM((2, 2, 16, WIDTH), F32),
            dma((4,)),
            dma((2, 2)),
            dma((8,)),
        ]
        + [dma((8,))] * 2
        + [dma((2, 8))] * 4
        + [dma((8,))] * 2
        + [dma((2, 1, 2, 4))] * 2
        + [dma((2, 1, 2, 4, 4))] * 2
        + [dma((2, 8))] * 4
        + [dma((8,))] * 2
        + [dma((2, 4, 2, 4))] * 4
        + [dma((2, 8))] * 2,
        compiler_params=pltpu.CompilerParams(
            collective_id=0, has_side_effects=True, vmem_limit_bytes=49 * 1024 * 1024
        ),
        name="exchange",
    )(queries, keys_in, values_in, cotangent)


def hand_over_kernel(a, b, c, d, w, x, y, z, sem):
    copies = [
        pltpu.make_async_copy(src, dst, sem.at[n])
        for n, (src, dst) in enumerate(((a, w), (b, x), (c, y), (d, z)))
    ]
    for copy in copies:
        copy.start()
    for copy in copies:
        copy.wait()


def hand_over(arrays):
    return pl.pallas_call(
        hand_over_kernel,
        out_shape=(jax.ShapeDtypeStruct((ROWS, WIDTH), BF),) * 4,
        in_specs=[pl.BlockSpec(memory_space=pltpu.VMEM)] * 4,
        out_specs=(pl.BlockSpec(memory_space=pltpu.HBM),) * 4,
        scratch_shapes=[pltpu.SemaphoreType.DMA((4,))],
        compiler_params=pltpu.CompilerParams(vmem_limit_bytes=8 * 1024 * 1024),
        name="hand_over",
    )(*arrays)


def on_device(queries, keys_in, values_in, cotangent):
    return tuple(hand_over(exchange(queries, keys_in, values_in, cotangent)))


def solution(mesh):
    spec = P(("seq", "head"), None)
    return jax.shard_map(
        on_device,
        mesh=mesh,
        in_specs=(spec,) * 4,
        out_specs=(spec,) * 4,
        check_vma=False,
    )
```

```python
import functools
import math

import jax
import jax.numpy as jnp
from jax import lax
from jax.experimental import pallas as pl
from jax.experimental.pallas import tpu as pltpu
from jax.sharding import PartitionSpec as P

HEADS = 16
HEAD_DIM = 128
BLOCK = 128
SUMMARY = 8
WIDTH = 2048
ROWS = 256
PAIR = 256
NY, NX, NC, NZ = 4, 4, 2, 4
TILE = 512

MESH = pl.DeviceIdType.MESH
NEG = -1e30
LOG2E = 1.4426950408889634
SCALE = 1.0 / math.sqrt(HEAD_DIM)
C2 = SCALE * LOG2E
BF = jnp.bfloat16
F32 = jnp.float32

NT = (((1,), (1,)), ((), ()))
TN = (((0,), (0,)), ((), ()))
NN = (((1,), (0,)), ((), ()))


def dot(a, b, dims):
    return lax.dot_general(a, b, dims, preferred_element_type=F32)


def cols_of(pair):
    return pl.ds(pl.multiple_of(pair * PAIR, PAIR), PAIR)


def exchange_kernel(
    q_hbm, k_hbm, v_hbm, g_hbm,
    out_v, gq_v, gk_v, gv_v,
    q_v, k_v, v_v, g_v,
    kv_edge, kv_pack, q_all, g_all, kv_all, kt_h, vt_h,
    q_t, g_t, score, row_stat, grad_q_t, grad_kv,
    part_one, recv_one, part_two, recv_two,
    o_buf, dq_buf, st_send, st_all, st_back, dkv_sum,
    o_in, dq_in, st_in, dkv_in,
    own_e, own_dp, own_o, own_dq, last_rows,
    load_sem, edge_sem, own_sem,
    kv_ss, kv_rs, q_ss, q_rs, g_ss, g_rs, st_ss, st_rs,
    near_ss, near_rs, far_ss, far_rs,
    o_ss, o_rs, dq_ss, dq_rs, sb_ss, sb_rs,
    one_ss, one_rs, two_ss, two_rs, dkv_ss, dkv_rs,
):
    s = lax.axis_index("seq")
    z0 = lax.axis_index("head")
    y0 = lax.div(s, 8)
    x0 = lax.rem(lax.div(s, 2), 4)
    c0 = lax.rem(s, 2)
    j0 = y0 * 2 + c0

    def member_id(pair):
        return (lax.div(pair, 2) * 8 + x0 * 2 + lax.rem(pair, 2), z0)

    def x_id(xt):
        return (y0 * 8 + xt * 2 + c0, z0)

    def z_id(zt):
        return (s, zt)

    def group_peer(step):
        yt = lax.rem(y0 + step // 2, 4)
        ct = lax.rem(c0 + step % 2, 2)
        return yt * 2 + ct

    group_steps = (1, 2, 3, 6, 7, 4, 5)
    ring_steps = (1, 3, 2)
    gather_parts = (((0, 4),), ((0, 4),))
    reduce_parts = (((0, 4),), ((0, 1), (1, 1), (2, 1), (3, 1)))

    def head_cols(pair, hh):
        return pl.ds(pl.multiple_of(pair * PAIR + hh * HEAD_DIM, HEAD_DIM), HEAD_DIM)

    loads = [
        pltpu.make_async_copy(src, dst, load_sem.at[i])
        for i, (src, dst) in enumerate(((k_hbm, k_v), (v_hbm, v_v), (q_hbm, q_v), (g_hbm, g_v)))
    ]
    edges = [
        pltpu.make_async_copy(
            src.at[pl.ds(r * BLOCK + BLOCK - 16, 16)], kv_edge.at[i, r], edge_sem.at[i, r]
        )
        for i, src in enumerate((k_hbm, v_hbm))
        for r in range(2)
    ]
    for edge in edges:
        edge.start()
    own_in = []
    for hh in range(2):
        own_in.append((
            pltpu.make_async_copy(
                q_hbm.at[:, head_cols(j0, hh)], q_all.at[hh, j0], own_sem.at[2 * hh]
            ),
            pltpu.make_async_copy(
                g_hbm.at[:, head_cols(j0, hh)], g_all.at[hh, j0], own_sem.at[2 * hh + 1]
            ),
        ))

    barrier = pltpu.get_barrier_semaphore()

    def greet(device):
        pl.semaphore_signal(barrier, inc=1, device_id=device, device_id_type=MESH)

    for step in range(1, 8):
        greet(member_id(group_peer(step)))
    for step in ring_steps:
        greet(x_id(lax.rem(x0 + step, 4)))
        greet(z_id(lax.rem(z0 + step, 4)))

    for edge in edges:
        edge.wait()
    for i in range(2):
        for j in range(8):
            for hh in range(2):
                cols = slice(j * PAIR + hh * HEAD_DIM, j * PAIR + (hh + 1) * HEAD_DIM)
                top = kv_edge[i, 0, :, cols].astype(F32)[8:, :]
                low = kv_edge[i, 1, :, cols].astype(F32)[8:, :]
                kv_pack[j, hh, i] = jnp.concatenate([top, low], axis=0).astype(BF)
    own_kv = pltpu.make_async_copy(
        kv_pack.at[j0], kv_all.at[:, :, y0, x0, c0, z0], own_sem.at[4]
    )
    own_kv.start()
    pl.semaphore_wait(barrier, 13)

    def remote(src, dst, ssem, rsem, device):
        return pltpu.make_async_remote_copy(
            src_ref=src,
            dst_ref=dst,
            send_sem=ssem,
            recv_sem=rsem,
            device_id=device,
            device_id_type=MESH,
        )

    def kv_copy(pair, slot):
        dst = kv_all.at[:, :, lax.div(slot, 2), x0, lax.rem(slot, 2), z0]
        return remote(kv_pack.at[pair], dst, kv_ss.at[pair], kv_rs.at[slot], member_id(pair))

    def q_copy(hh, pair, slot):
        return remote(
            q_hbm.at[:, head_cols(pair, hh)], q_all.at[hh, slot],
            q_ss.at[hh, pair], q_rs.at[hh, slot], member_id(pair),
        )

    def g_copy(hh, pair, slot):
        return remote(
            g_hbm.at[:, head_cols(pair, hh)], g_all.at[hh, slot],
            g_ss.at[hh, pair], g_rs.at[hh, slot], member_id(pair),
        )

    def st_copy(pair, slot):
        return remote(
            st_send.at[pair], st_all.at[slot], st_ss.at[pair], st_rs.at[slot], member_id(pair)
        )

    def o_copy(hh, pair, slot):
        return remote(
            o_buf.at[hh, pair], o_in.at[hh, slot],
            o_ss.at[hh, pair], o_rs.at[hh, slot], member_id(pair),
        )

    def dq_copy(hh, pair, slot):
        return remote(
            dq_buf.at[hh, pair], dq_in.at[hh, slot],
            dq_ss.at[hh, pair], dq_rs.at[hh, slot], member_id(pair),
        )

    def sb_copy(pair, slot):
        return remote(
            st_back.at[pair], st_in.at[slot], sb_ss.at[pair], sb_rs.at[slot], member_id(pair)
        )

    def dkv_copy(hh, pair, slot):
        return remote(
            dkv_sum.at[hh, pair], dkv_in.at[hh, slot],
            dkv_ss.at[hh, pair], dkv_rs.at[hh, slot], member_id(pair),
        )

    def near_copy(hh, part, kind, peer, slot):
        ys = pl.ds(*gather_parts[hh][part])
        if kind == 0:
            view, device = kv_all.at[hh, 0, ys, slot, :, z0], x_id(peer)
        else:
            view, device = kv_all.at[hh, 1, ys, x0, :, slot], z_id(peer)
        return remote(
            view, view,
            near_ss.at[hh, part, kind, peer], near_rs.at[hh, part, kind, slot], device,
        )

    def far_copy(hh, part, kind, item, peer, slot):
        ys = pl.ds(*gather_parts[hh][part])
        if kind == 0:
            view, device = kv_all.at[hh, 0, ys, item, :, slot], z_id(peer)
        else:
            view, device = kv_all.at[hh, 1, ys, slot, :, item], x_id(peer)
        return remote(
            view, view,
            far_ss.at[hh, part, kind, item, peer], far_rs.at[hh, part, kind, item, slot], device,
        )

    def one_copy(hh, part, kind, peer, slot):
        ys = pl.ds(*reduce_parts[hh][part])
        if kind == 0:
            src, device = part_one.at[hh, 0, ys, peer], x_id(peer)
        else:
            src, device = part_one.at[hh, 1, ys, :, :, peer], z_id(peer)
        dst = recv_one.at[hh, kind, slot, ys].reshape(*src.shape)
        return remote(
            src, dst, one_ss.at[hh, part, kind, peer], one_rs.at[hh, part, kind, slot], device
        )

    def two_copy(hh, part, kind, peer, slot):
        ys = pl.ds(*reduce_parts[hh][part])
        device = z_id(peer) if kind == 0 else x_id(peer)
        return remote(
            part_two.at[hh, kind, peer, ys], recv_two.at[hh, kind, slot, ys],
            two_ss.at[hh, part, kind, peer], two_rs.at[hh, part, kind, slot], device,
        )

    near_place = (x0, z0)
    far_place = (z0, x0)

    def near_peer(kind, step):
        return lax.rem(near_place[kind] + step, 4)

    def far_peer(kind, step):
        return lax.rem(far_place[kind] + step, 4)

    for step in group_steps:
        kv_copy(group_peer(step), j0).start()
    for step in group_steps:
        q_copy(0, group_peer(step), j0).start()
        g_copy(0, group_peer(step), j0).start()

    for load in loads:
        load.start()
    for hh in range(2):
        own_in[hh][0].start()
        own_in[hh][1].start()
    own_kv.wait()
    for step in group_steps:
        kv_copy(group_peer(step), group_peer(step)).wait_recv()

    def gather_start(hh, part):
        for kind in range(2):
            for step in ring_steps:
                near_copy(hh, part, kind, near_peer(kind, step), near_place[kind]).start()
        for kind in range(2):
            for step in ring_steps:
                far_copy(
                    hh, part, kind, near_place[kind], far_peer(kind, step), far_place[kind]
                ).start()

    def gather_forward(hh, part):
        for step in ring_steps:
            for kind in range(2):
                item = near_peer(kind, step)
                near_copy(hh, part, kind, item, item).wait_recv()
                for hop in ring_steps:
                    far_copy(hh, part, kind, item, far_peer(kind, hop), far_place[kind]).start()

    def gather_wait(hh, part):
        for kind in range(2):
            for step in (0,) + ring_steps:
                item = near_peer(kind, step)
                for hop in ring_steps:
                    peer = far_peer(kind, hop)
                    far_copy(hh, part, kind, item, peer, peer).wait_recv()
        lo, count = gather_parts[hh][part]
        for y in range(lo, lo + count):
            kt_h[y] = tile_of(hh, 0, y).T
            vt_h[y] = tile_of(hh, 1, y).T

    gather_start(0, 0)

    for load in loads:
        load.wait()
    key_pos = lax.broadcasted_iota(jnp.int32, (BLOCK, BLOCK), 0)
    query_pos = lax.broadcasted_iota(jnp.int32, (BLOCK, BLOCK), 1)
    causal = key_pos <= query_pos

    def local_turn(j, carry):
        for hh in range(2):
            cols = head_cols(j, hh)
            for r in range(2):
                rows = slice(r * BLOCK, (r + 1) * BLOCK)
                raw = dot(k_v[rows, cols], q_v[rows, cols], NT)
                raw = jnp.where(causal, raw, NEG)
                high = jnp.max(raw, axis=0, keepdims=True)
                weights = jnp.exp2((raw - high) * C2)
                dprob = dot(v_v[rows, cols], g_v[rows, cols], NT)
                own_e[j, 2 * hh + r] = weights
                own_dp[j, 2 * hh + r] = dprob
                st_send[j, 3 * hh : 3 * hh + 1, rows] = high
                st_send[j, 3 * hh + 1 : 3 * hh + 2, rows] = jnp.sum(weights, axis=0, keepdims=True)
                st_send[j, 3 * hh + 2 : 3 * hh + 3, rows] = jnp.sum(
                    weights * dprob, axis=0, keepdims=True
                )
        return carry

    st_send[...] = jnp.zeros_like(st_send)
    lax.fori_loop(0, 8, local_turn, 0)
    own_st = pltpu.make_async_copy(st_send.at[j0], st_all.at[j0], own_sem.at[5])
    own_st.start()
    for step in group_steps:
        st_copy(group_peer(step), j0).start()
    for step in group_steps:
        q_copy(1, group_peer(step), j0).start()
        g_copy(1, group_peer(step), j0).start()

    grad_kv[...] = jnp.zeros_like(grad_kv)
    st_back[...] = jnp.zeros_like(st_back)
    gather_forward(0, 0)
    gather_start(1, 0)
    own_st.wait()

    lane = lax.broadcasted_iota(jnp.int32, (1, 2 * ROWS), 1)
    lane_limit = x0 * 128 + z0 * 16 + lax.div(lane, 256) * 64 + lax.rem(lax.div(lane, 128), 2) * 8
    key_row = lax.broadcasted_iota(jnp.int32, (TILE, 2 * ROWS), 0)

    def tile_of(hh, kind, kt):
        return kv_all[hh, kind, kt].reshape(TILE, HEAD_DIM)

    def place_of(y, kt):
        return y * (y + 1) // 2 + kt

    def group_rows(ref, hh, y):
        return ref[hh, 2 * y : 2 * y + 2].reshape(2 * ROWS, HEAD_DIM)

    def forward(hh, y):
        q_t[...] = group_rows(q_all, hh, y).T
        g_t[y] = group_rows(g_all, hh, y).T

        def stat(kind):
            row = slice(hh * 3 + kind, hh * 3 + kind + 1)
            return jnp.concatenate([st_all[2 * y, row, :], st_all[2 * y + 1, row, :]], axis=1)

        local_high = stat(0)
        high = local_high
        for kt in range(y + 1):
            raw = dot(tile_of(hh, 0, kt), q_t[...], NN)
            if kt == y:
                raw = jnp.where(key_row < lane_limit, raw, NEG)
            score[place_of(y, kt)] = raw
            high = jnp.maximum(high, jnp.max(raw, axis=0, keepdims=True))

        shrink = jnp.exp2((local_high - high) * C2)
        total = stat(1) * shrink
        out_t = jnp.zeros((HEAD_DIM, 2 * ROWS), F32)
        for kt in range(y + 1):
            weights = jnp.exp2((score[place_of(y, kt)] - high) * C2)
            score[place_of(y, kt)] = weights
            out_t = out_t + dot(vt_h[kt], weights.astype(BF), NN)
            total = total + jnp.sum(weights, axis=0, keepdims=True)

        inverse = 1.0 / total
        delta = (
            stat(2) * shrink + jnp.sum(out_t * g_t[y].astype(F32), axis=0, keepdims=True)
        ) * inverse
        lse = high * C2 + jnp.log(total) * LOG2E
        row_stat[y, 0:1, :] = inverse
        row_stat[y, 1:2, :] = delta
        out = (out_t * inverse).T.astype(BF)
        for c in range(2):
            half = slice(c * ROWS, (c + 1) * ROWS)
            o_buf[hh, 2 * y + c] = out[half]
            st_back[2 * y + c, hh : hh + 1, :] = lse[:, half]
            st_back[2 * y + c, hh + 2 : hh + 3, :] = delta[:, half]

    def grad_tile(hh, y, kt):
        tile = slice(kt * TILE, (kt + 1) * TILE)
        probs = score[place_of(y, kt)] * row_stat[y, 0:1, :]
        dprob = dot(tile_of(hh, 1, kt), g_t[y], NN)
        dscore = (probs * (dprob - row_stat[y, 1:2, :])).astype(BF)
        grad_kv[hh, 0, tile, :] += dot(dscore, group_rows(q_all, hh, y), NN)
        grad_kv[hh, 1, tile, :] += dot(probs.astype(BF), group_rows(g_all, hh, y), NN)
        return dot(kt_h[kt], dscore, NN)

    def put_grad(hh, y, grad_t):
        grad_q = (grad_t * SCALE).T.astype(BF)
        for c in range(2):
            dq_buf[hh, 2 * y + c] = grad_q[c * ROWS : (c + 1) * ROWS]

    def reduce_start(hh, part):
        lo, count = reduce_parts[hh][part]

        def cast_turn(y, carry):
            tile = pl.ds(pl.multiple_of(y * TILE, TILE), TILE)
            shape = (4, 2, 4, 16, HEAD_DIM)
            part_one[hh, 0, y] = (grad_kv[hh, 0, tile, :] * SCALE).astype(BF).reshape(shape)
            part_one[hh, 1, y] = grad_kv[hh, 1, tile, :].astype(BF).reshape(shape)
            return carry

        lax.fori_loop(lo, lo + count, cast_turn, 0)
        for step in ring_steps:
            for kind in range(2):
                one_copy(hh, part, kind, near_peer(kind, step), near_place[kind]).start()

    def reduce_middle(hh, part):
        lo, count = reduce_parts[hh][part]
        for kind in range(2):
            for step in ring_steps:
                peer = near_peer(kind, step)
                one_copy(hh, part, kind, peer, peer).wait_recv()
        for kind in range(2):

            def add_turn(y, carry, kind=kind):
                if kind == 0:
                    total = part_one[hh, 0, y, x0].astype(F32)
                else:
                    total = part_one[hh, 1, y, :, :, z0].astype(F32)
                for step in ring_steps:
                    total += recv_one[hh, kind, near_peer(kind, step), y].reshape(
                        total.shape
                    ).astype(F32)
                total = total.astype(BF)
                for item in range(4):
                    part_two[hh, kind, item, y] = total[:, item] if kind == 0 else total[item]
                return carry

            lax.fori_loop(lo, lo + count, add_turn, 0)
            for step in ring_steps:
                two_copy(hh, part, kind, far_peer(kind, step), far_place[kind]).start()

    def reduce_end(hh, part):
        lo, count = reduce_parts[hh][part]
        for kind in range(2):
            for step in ring_steps:
                peer = far_peer(kind, step)
                two_copy(hh, part, kind, peer, peer).wait_recv()
        for y in range(lo, lo + count):
            for kind in range(2):
                total = part_two[hh, kind, far_place[kind], y].astype(F32)
                for step in ring_steps:
                    total += recv_two[hh, kind, far_peer(kind, step), y].astype(F32)
                for c in range(2):
                    dkv_sum[hh, 2 * y + c, kind] = total[c]
            for c in range(2):
                pair = 2 * y + c

                @pl.when(pair != j0)
                def _(pair=pair):
                    dkv_copy(hh, pair, j0).start()

    def to_others(y, *starts):
        for c in range(2):
            pair = 2 * y + c

            @pl.when(pair != j0)
            def _(pair=pair):
                for start in starts:
                    start(pair)

    def member_turn(i, carry, hh):
        turn = i if hh == 0 else 3 - i
        dy = turn + lax.div(turn, 2) * (5 - 2 * turn)
        y = lax.rem(y0 + dy, 4)
        to_others(
            y,
            lambda pair: q_copy(hh, pair, pair).wait_recv(),
            lambda pair: g_copy(hh, pair, pair).wait_recv(),
        )
        if hh == 0:
            to_others(y, lambda pair: st_copy(pair, pair).wait_recv())
        for row in range(4):

            @pl.when(y == row)
            def _(row=row):
                forward(hh, row)
                if hh == 0:
                    grad_t = jnp.zeros((HEAD_DIM, 2 * ROWS), F32)
                    for kt in range(row + 1):
                        grad_t = grad_t + grad_tile(hh, row, kt)
                    put_grad(hh, row, grad_t)

        if hh == 1:
            to_others(y, lambda pair: sb_copy(pair, j0).start())
        to_others(y, lambda pair: o_copy(hh, pair, j0).start())
        if hh == 0:
            to_others(y, lambda pair: dq_copy(hh, pair, j0).start())

            @pl.when(i == 0)
            def _():
                gather_forward(1, 0)

        return carry

    own_in[0][0].wait()
    own_in[0][1].wait()
    gather_wait(0, 0)
    lax.fori_loop(0, 4, functools.partial(member_turn, hh=0), 0)
    reduce_start(0, 0)
    own_in[1][0].wait()
    own_in[1][1].wait()
    gather_wait(1, 0)
    lax.fori_loop(0, 4, functools.partial(member_turn, hh=1), 0)
    for kt in range(4):
        for y in range(kt, 4):
            part = grad_tile(1, y, kt)
            if kt == 0 and y > 0:
                grad_q_t[y] = part
            elif y > kt:
                grad_q_t[y] += part
            else:
                put_grad(1, y, part if kt == 0 else grad_q_t[y] + part)
                to_others(y, lambda pair: dq_copy(1, pair, j0).start())
        reduce_start(1, kt)
        if kt == 0:
            reduce_middle(0, 0)
        elif kt == 2:
            reduce_middle(1, 0)
        elif kt == 3:
            reduce_middle(1, 1)

    def pair_at(t):
        turn = 3 - lax.div(t, 2)
        dy = turn + lax.div(turn, 2) * (5 - 2 * turn)
        return lax.rem(y0 + dy, 4) * 2 + lax.rem(c0 + 1 + lax.rem(t, 2), 2)

    def own_turn(t, carry):
        pair = pair_at(t)

        @pl.when(pair != j0)
        def _():
            sb_copy(pair, pair).wait_recv()

        @pl.when(pair == j0)
        def _():
            st_in[pair] = st_back[pair]

        for hh in range(2):
            cols = head_cols(pair, hh)
            for r in range(2):
                rows = slice(r * BLOCK, (r + 1) * BLOCK)
                lse = st_in[pair, hh : hh + 1, rows]
                delta = st_in[pair, hh + 2 : hh + 3, rows]
                high = st_send[pair, 3 * hh : 3 * hh + 1, rows]
                probs = own_e[pair, 2 * hh + r] * jnp.exp2(high * C2 - lse)
                probs_b = probs.astype(BF)
                dscore = (probs * (own_dp[pair, 2 * hh + r] - delta)).astype(BF)
                own_o[rows, cols] = dot(probs_b, v_v[rows, cols], TN)
                own_dq[rows, cols] = dot(dscore, k_v[rows, cols], TN) * SCALE
                grad_k = dot(dscore, q_v[rows, cols], NN) * SCALE
                gk_v[rows, cols] = grad_k.astype(BF)
                last_rows[0, r, :, cols] = grad_k[BLOCK - 16 :]
                grad_v = dot(probs_b, g_v[rows, cols], NN)
                gv_v[rows, cols] = grad_v.astype(BF)
                last_rows[1, r, :, cols] = grad_v[BLOCK - 16 :]
        return carry

    def sum_turn(t, carry):
        pair = pair_at(t)

        @pl.when(pair != j0)
        def _():
            for hh in range(2):
                o_copy(hh, pair, pair).wait_recv()
                dq_copy(hh, pair, pair).wait_recv()

        @pl.when(pair == j0)
        def _():
            for hh in range(2):
                o_in[hh, pair] = o_buf[hh, pair]
                dq_in[hh, pair] = dq_buf[hh, pair]

        for hh in range(2):
            cols = head_cols(pair, hh)
            out_v[:, cols] = (own_o[:, cols] + o_in[hh, pair].astype(F32)).astype(BF)
            gq_v[:, cols] = (own_dq[:, cols] + dq_in[hh, pair].astype(F32)).astype(BF)
        return carry

    reduce_end(0, 0)
    lax.fori_loop(0, 3, own_turn, 0)
    reduce_middle(1, 2)
    reduce_end(1, 0)
    lax.fori_loop(3, 6, own_turn, 0)
    reduce_middle(1, 3)
    reduce_end(1, 1)
    reduce_end(1, 2)
    lax.fori_loop(6, 8, own_turn, 0)
    lax.fori_loop(0, 4, sum_turn, 0)
    reduce_end(1, 3)
    lax.fori_loop(4, 8, sum_turn, 0)

    def last_turn(t, carry):
        pair = pair_at(t)

        @pl.when(pair != j0)
        def _():
            dkv_copy(0, pair, pair).wait_recv()
            dkv_copy(1, pair, pair).wait_recv()

        @pl.when(pair == j0)
        def _():
            for hh in range(2):
                dkv_in[hh, pair] = dkv_sum[hh, pair]

        for hh in range(2):
            cols = head_cols(pair, hh)
            for kind, dst in enumerate((gk_v, gv_v)):
                for r in range(2):
                    part = dkv_in[hh, pair, kind, r * SUMMARY : (r + 1) * SUMMARY, :]
                    part = jnp.concatenate([jnp.zeros_like(part), part], axis=0)
                    rows = slice((r + 1) * BLOCK - 16, (r + 1) * BLOCK)
                    dst[rows, cols] = (last_rows[kind, r, :, cols] + part).astype(BF)
        return carry

    lax.fori_loop(0, 8, last_turn, 0)
    for step in group_steps:
        pair = group_peer(step)
        kv_copy(pair, j0).wait_send()
        st_copy(pair, j0).wait_send()
        sb_copy(pair, j0).wait_send()
        for hh in range(2):
            for copy in (q_copy, g_copy, o_copy, dq_copy, dkv_copy):
                copy(hh, pair, j0).wait_send()
    for hh in range(2):
        for kind in range(2):
            for step in ring_steps:
                near, far = near_peer(kind, step), far_peer(kind, step)
                for part in range(len(gather_parts[hh])):
                    near_copy(hh, part, kind, near, near_place[kind]).wait_send()
                    for hop in (0,) + ring_steps:
                        item = near_peer(kind, hop)
                        far_copy(hh, part, kind, item, far, far_place[kind]).wait_send()
                for part in range(len(reduce_parts[hh])):
                    one_copy(hh, part, kind, near, near_place[kind]).wait_send()
                    two_copy(hh, part, kind, far, far_place[kind]).wait_send()


def exchange(queries, keys_in, values_in, cotangent):
    hbm_spec = pl.BlockSpec(memory_space=pltpu.HBM)
    vmem_spec = pl.BlockSpec(memory_space=pltpu.VMEM)
    dma = pltpu.SemaphoreType.DMA
    return pl.pallas_call(
        exchange_kernel,
        out_shape=(jax.ShapeDtypeStruct((ROWS, WIDTH), BF),) * 4,
        in_specs=[hbm_spec] * 4,
        out_specs=(vmem_spec,) * 4,
        scratch_shapes=[
            pltpu.VMEM((ROWS, WIDTH), BF),
            pltpu.VMEM((ROWS, WIDTH), BF),
            pltpu.VMEM((ROWS, WIDTH), BF),
            pltpu.VMEM((ROWS, WIDTH), BF),
            pltpu.VMEM((2, 2, 16, WIDTH), BF),
            pltpu.VMEM((8, 2, 2, 16, HEAD_DIM), BF),
            pltpu.VMEM((2, 8, ROWS, HEAD_DIM), BF),
            pltpu.VMEM((2, 8, ROWS, HEAD_DIM), BF),
            pltpu.VMEM((2, 2, 4, 4, 2, 4, 16, HEAD_DIM), BF),
            pltpu.VMEM((4, HEAD_DIM, TILE), BF),
            pltpu.VMEM((4, HEAD_DIM, TILE), BF),
            pltpu.VMEM((HEAD_DIM, 2 * ROWS), BF),
            pltpu.VMEM((4, HEAD_DIM, 2 * ROWS), BF),
            pltpu.VMEM((10, TILE, 2 * ROWS), F32),
            pltpu.VMEM((4, 8, 2 * ROWS), F32),
            pltpu.VMEM((4, HEAD_DIM, 2 * ROWS), F32),
            pltpu.VMEM((2, 2, 4 * TILE, HEAD_DIM), F32),
            pltpu.VMEM((2, 2, 4, 4, 2, 4, 16, HEAD_DIM), BF),
            pltpu.VMEM((2, 2, 4, 4, 8, 16, HEAD_DIM), BF),
            pltpu.VMEM((2, 2, 4, 4, 2, 16, HEAD_DIM), BF),
            pltpu.VMEM((2, 2, 4, 4, 2, 16, HEAD_DIM), BF),
            pltpu.VMEM((2, 8, ROWS, HEAD_DIM), BF),
            pltpu.VMEM((2, 8, ROWS, HEAD_DIM), BF),
            pltpu.VMEM((8, 8, ROWS), F32),
            pltpu.VMEM((8, 8, ROWS), F32),
            pltpu.VMEM((8, 8, ROWS), F32),
            pltpu.VMEM((2, 8, 2, 16, HEAD_DIM), F32),
            pltpu.VMEM((2, 8, ROWS, HEAD_DIM), BF),
            pltpu.VMEM((2, 8, ROWS, HEAD_DIM), BF),
            pltpu.VMEM((8, 8, ROWS), F32),
            pltpu.VMEM((2, 8, 2, 16, HEAD_DIM), F32),
            pltpu.VMEM((8, 4, BLOCK, BLOCK), F32),
            pltpu.VMEM((8, 4, BLOCK, BLOCK), F32),
            pltpu.VMEM((ROWS, WIDTH), F32),
            pltpu.VMEM((ROWS, WIDTH), F32),
            pltpu.VMEM((2, 2, 16, WIDTH), F32),
            dma((4,)),
            dma((2, 2)),
            dma((8,)),
        ]
        + [dma((8,))] * 2
        + [dma((2, 8))] * 4
        + [dma((8,))] * 2
        + [dma((2, 1, 2, 4))] * 2
        + [dma((2, 1, 2, 4, 4))] * 2
        + [dma((2, 8))] * 4
        + [dma((8,))] * 2
        + [dma((2, 4, 2, 4))] * 4
        + [dma((2, 8))] * 2,
        compiler_params=pltpu.CompilerParams(
            collective_id=0, has_side_effects=True, vmem_limit_bytes=49 * 1024 * 1024
        ),
        name="exchange",
    )(queries, keys_in, values_in, cotangent)


def hand_over_kernel(a, b, c, d, w, x, y, z, sem):
    copies = [
        pltpu.make_async_copy(src, dst, sem.at[n])
        for n, (src, dst) in enumerate(((a, w), (b, x), (c, y), (d, z)))
    ]
    for copy in copies:
        copy.start()
    for copy in copies:
        copy.wait()


def hand_over(arrays):
    return pl.pallas_call(
        hand_over_kernel,
        out_shape=(jax.ShapeDtypeStruct((ROWS, WIDTH), BF),) * 4,
        in_specs=[pl.BlockSpec(memory_space=pltpu.VMEM)] * 4,
        out_specs=(pl.BlockSpec(memory_space=pltpu.HBM),) * 4,
        scratch_shapes=[pltpu.SemaphoreType.DMA((4,))],
        compiler_params=pltpu.CompilerParams(vmem_limit_bytes=8 * 1024 * 1024),
        name="hand_over",
    )(*arrays)


def on_device(queries, keys_in, values_in, cotangent):
    return tuple(hand_over(exchange(queries, keys_in, values_in, cotangent)))


def solution(mesh):
    spec = P(("seq", "head"), None)
    return jax.shard_map(
        on_device,
        mesh=mesh,
        in_specs=(spec,) * 4,
        out_specs=(spec,) * 4,
        check_vma=False,
    )
```
